32 devices in a mesh: seq: 4 (over z), fsdp: 8 (over y, x, core).
Axes of the slice: x: 2, y: 2, z: 4, core: 2. Of those that a mesh axis runs over, the one named last changes fastest.
Arguments:
- tokens: bfloat16 [16, 2048, 768], P('fsdp', 'seq'), may hold values from -6 to 6
- segment_ids: int32 [16, 2048], P('fsdp', 'seq'), may hold values from 0 to 3, never falling along the last dimension, each value on 1 to 1024 neighbouring positions
- mix_weight: bfloat16 [768, 2304], P('fsdp'), may hold values from -0.21875 to 0.21875
- query_bias: bfloat16 [768], P('fsdp'), may hold values from -3 to 3
- value_bias: bfloat16 [768], P('fsdp'), may hold values from -3 to 3
- merge_weight: bfloat16 [768, 768], P('fsdp'), may hold values from -0.875 to 0.875
- merge_bias: bfloat16 [768], P('fsdp'), may hold values from -2 to 2
- first_gain: bfloat16 [768], P('fsdp'), may hold values from 0.5 to 1.5
- first_shift: bfloat16 [768], P('fsdp'), may hold values from -2 to 2
- up_weight: bfloat16 [768, 3072], P('fsdp'), may hold values from -0.21875 to 0.21875
- up_bias: bfloat16 [3072], P('fsdp'), may hold values from -3 to 3
- down_weight: bfloat16 [3072, 768], P('fsdp'), may hold values from -0.109375 to 0.109375
- down_bias: bfloat16 [768], P('fsdp'), may hold values from -2 to 2
- second_gain: bfloat16 [768], P('fsdp'), may hold values from 0.5 to 1.5
- second_shift: bfloat16 [768], P('fsdp'), may hold values from -2 to 2
- output_grad: bfloat16 [16, 2048, 768], P('fsdp', 'seq'), may hold values from -6 to 6
Outputs:
- output: bfloat16 [16, 2048, 768], P('fsdp', 'seq')
- input_grad: float32 [16, 2048, 768], P('fsdp', 'seq')
- mix_weight_grad: float32 [768, 2304], P('fsdp')
- query_bias_grad: float32 [768], P('fsdp')
- value_bias_grad: float32 [768], P('fsdp')
- merge_weight_grad: float32 [768, 768], P('fsdp')
- merge_bias_grad: float32 [768], P('fsdp')
- first_gain_grad: float32 [768], P('fsdp')
- first_shift_grad: float32 [768], P('fsdp')
- up_weight_grad: float32 [768, 3072], P('fsdp')
- up_bias_grad: float32 [3072], P('fsdp')
- down_weight_grad: float32 [3072, 768], P('fsdp')
- down_bias_grad: float32 [768], P('fsdp')
- second_gain_grad: float32 [768], P('fsdp')
- second_shift_grad: float32 [768], P('fsdp')
The draws below stay inside these ranges and needn't reach their ends.
Inputs may be any that keep to these rules, and one draw needn't show every extreme that they name: `segment_ids`: within a sequence the ids never fall; a document spans 1 to 1024 positions, and one in each draw spans exactly 1024.
All inputs are finite; a program needn't handle non-finite values.
Results may differ from the reference program's by a relative error of at most 0.014.
Values may be sent and summed in bfloat16 or wider, within the bound.
No kernel may reach another device: no remote copies, remote signals or barrier semaphores. Data moves between devices by JAX's collectives and lax.ppermute only.
A program may use at most 192 MiB of HBM per device.

```python
import math
import jax
import jax.numpy as jnp
import numpy as np
from jax import lax

D = 768
H = 12
HD = 64
FF = 3072
SEQ_LEN = 2048
SEQ_ALL = 16


def levels(own_key, extent, split, smallest, top_value):
    level, own = 1.0, jax.random.fold_in(own_key, 6)
    for position, shards_of in split:
        heights = jnp.exp(jax.random.uniform(jax.random.fold_in(own, position), (shards_of,), jnp.float32, smallest / len(split), top_value / len(split)))
        level = level * jnp.repeat(heights, extent[position] // shards_of).reshape([-1 if axis == position else 1 for axis in range(len(extent))])
    return level


def length_profile(count, total, bound, slope):
    loads = [(1 << 20) // math.isqrt(standing ** slope) + 1 for standing in range(2, count + 1)]
    surplus, given = total - bound - (count - 1), [1] * (count - 1)
    while surplus > 0:
        free = [i for i in range(count - 1) if given[i] < bound]
        mass, budget = sum([loads[i] for i in free]), surplus
        for i in free:
            extra = min(bound - given[i], max(1, budget * loads[i] // mass), surplus)
            given[i] = given[i] + extra
            surplus = surplus - extra
    return np.array([bound] + given)


def ragged(rng, count, total, most, skew):
    if count == 2:
        one = jax.random.randint(rng, (), max(1, total - most), min(most, total - 1) + 1)
        return jnp.stack([one, total - one])
    lengths = jnp.asarray(length_profile(count, total, most, skew), jnp.int32)
    couples = (count - 1) // 2
    giver, receiver = lengths[1:1 + 2 * couples:2], lengths[2:2 + 2 * couples:2]
    margin = jnp.minimum(giver - 1, most - receiver)
    passed = jax.random.randint(jax.random.fold_in(rng, 1), (couples,), 0, 1 << 20) % (margin + 1)
    lengths = lengths.at[1:1 + 2 * couples:2].set(giver - passed).at[2:2 + 2 * couples:2].set(receiver + passed)
    return lengths[jax.random.permutation(jax.random.fold_in(rng, 2), count)]


def normal_values(rng, extent, width, most, split=(), kind=jnp.bfloat16):
    values = width * jax.random.normal(rng, extent, jnp.float32)
    if split:
        values = values * levels(rng, extent, split, -0.22, 0.18)
    return jnp.clip(values, -most, most).astype(kind)


def setup_inputs(seed: int = 0) -> dict:
    seeds = jax.random.split(jax.random.key(seed), 17)
    tokens = normal_values(seeds[0], (SEQ_ALL, SEQ_LEN, D), 1.0, 6.0, ((0, 8), (1, 4)))
    segment_ids = jax.vmap(lambda own: jnp.searchsorted(jnp.cumsum(ragged(own, 4, SEQ_LEN, SEQ_LEN // 2, 1)), jnp.arange(SEQ_LEN), side="right"))(jax.random.split(seeds[1], SEQ_ALL)).reshape((SEQ_ALL, SEQ_LEN)).astype(jnp.int32)
    mix_weight = normal_values(seeds[2], (D, 3 * D), D ** -0.5, 0.21875, ((0, 8),))
    query_bias = normal_values(seeds[3], (D,), 0.5, 3.0, ((0, 8),))
    value_bias = normal_values(seeds[4], (D,), 0.5, 3.0, ((0, 8),))
    merge_weight = normal_values(seeds[5], (D, D), (D // 16) ** -0.5, 0.875, ((0, 8),))
    merge_bias = normal_values(seeds[6], (D,), 0.3, 2.0, ((0, 8),))
    first_gain = jnp.clip(1.0 + 0.1 * jax.random.normal(seeds[7], (D,), jnp.float32), 0.5, 1.5).astype(jnp.bfloat16)
    first_shift = normal_values(seeds[8], (D,), 0.3, 2.0, ((0, 8),))
    up_weight = normal_values(seeds[9], (D, FF), D ** -0.5, 0.21875, ((0, 8),))
    up_bias = normal_values(seeds[10], (FF,), 0.5, 3.0, ((0, 8),))
    down_weight = normal_values(seeds[11], (FF, D), FF ** -0.5, 0.109375, ((0, 8),))
    down_bias = normal_values(seeds[12], (D,), 0.3, 2.0, ((0, 8),))
    second_gain = jnp.clip(1.0 + 0.1 * jax.random.normal(seeds[13], (D,), jnp.float32), 0.5, 1.5).astype(jnp.bfloat16)
    second_shift = normal_values(seeds[14], (D,), 0.3, 2.0, ((0, 8),))
    output_grad = normal_values(seeds[15], (SEQ_ALL, SEQ_LEN, D), 1.0, 6.0, ((0, 8), (1, 4)))
    return dict(tokens=tokens, segment_ids=segment_ids, mix_weight=mix_weight, query_bias=query_bias, value_bias=value_bias, merge_weight=merge_weight, merge_bias=merge_bias, first_gain=first_gain, first_shift=first_shift, up_weight=up_weight, up_bias=up_bias, down_weight=down_weight, down_bias=down_bias, second_gain=second_gain, second_shift=second_shift, output_grad=output_grad)


eps_norm = 1e-06
highest = lax.Precision.HIGHEST

@jax.custom_vjp
def low(v):
    return lax.optimization_barrier(v.astype(jnp.bfloat16)).astype(jnp.float32)

@jax.custom_vjp
def low_back(v):
    return v

def low_keep(v):
    return (low(v), None)

def low_pass(kept, grad):
    return (grad,)

def back_keep(v):
    return (v, None)

def back_low(kept, grad):
    return (low(grad),)
low.defvjp(low_keep, low_pass)
low_back.defvjp(back_keep, back_low)

def layer_norm(total, gain, shift):
    middle = lax.optimization_barrier(jnp.mean(total, axis=-1, keepdims=True))
    centred = total - middle
    spread = lax.optimization_barrier(jnp.mean(centred * centred, axis=-1, keepdims=True))
    return centred * lax.rsqrt(spread + eps_norm) * gain + shift

def attend(packed):
    head_rows, doc_ids = packed
    queries = head_rows[:, :, 0]
    keys_all = head_rows[:, :, 1]
    values_all = head_rows[:, :, 2]
    scores = jnp.einsum('qhe,khe->hqk', queries, keys_all, precision=highest) * (1.0 / math.sqrt(HD))
    scores = low_back(scores)
    same = doc_ids[:, None] == doc_ids[None, :]
    scores = jnp.where(same[None, :, :], scores, -1000000000.0)
    probs = jax.nn.softmax(scores, axis=-1)
    context = jnp.einsum('hqk,khe->qhe', low(probs), values_all, precision=highest)
    return low(low_back(context.reshape(head_rows.shape[0], D)))

def make_forward(segment_ids):

    def forward(tokens, mix_weight, query_bias, value_bias, merge_weight, merge_bias, first_gain, first_shift, up_weight, up_bias, down_weight, down_bias, second_gain, second_shift):
        flat = tokens.reshape(-1, D)
        empty = jnp.zeros((H, HD), tokens.dtype)
        mix_bias = jnp.stack([query_bias.reshape(H, HD), empty, value_bias.reshape(H, HD)], axis=1).reshape(3 * D)
        mixed = low(low_back(jnp.dot(flat, mix_weight, precision=highest) + mix_bias))
        head_rows = mixed.reshape(SEQ_ALL, SEQ_LEN, H, 3, HD)
        context = lax.map(jax.checkpoint(attend), (head_rows, segment_ids)).reshape(-1, D)
        attended = low_back(jnp.dot(context, merge_weight, precision=highest) + merge_bias)
        first_out = layer_norm(flat + attended, first_gain, first_shift)
        hidden = low_back(jnp.dot(low(first_out), up_weight, precision=highest) + up_bias)
        active = low(jax.nn.gelu(hidden, approximate=False))
        branch = low_back(jnp.dot(active, down_weight, precision=highest) + down_bias)
        return layer_norm(first_out + branch, second_gain, second_shift).reshape(tokens.shape)
    return forward

def reference(tokens, segment_ids, mix_weight, query_bias, value_bias, merge_weight, merge_bias, first_gain, first_shift, up_weight, up_bias, down_weight, down_bias, second_gain, second_shift, output_grad):
    forward = make_forward(segment_ids)
    result, pull = jax.vjp(forward, tokens.astype(jnp.float32), mix_weight.astype(jnp.float32), query_bias.astype(jnp.float32), value_bias.astype(jnp.float32), merge_weight.astype(jnp.float32), merge_bias.astype(jnp.float32), first_gain.astype(jnp.float32), first_shift.astype(jnp.float32), up_weight.astype(jnp.float32), up_bias.astype(jnp.float32), down_weight.astype(jnp.float32), down_bias.astype(jnp.float32), second_gain.astype(jnp.float32), second_shift.astype(jnp.float32))
    input_grad, mix_grad, query_grad, value_grad, merge_grad, merge_bias_grad, first_gain_grad, first_shift_grad, up_grad, up_bias_grad, down_grad, down_bias_grad, second_gain_grad, second_shift_grad = pull(output_grad.astype(jnp.float32))
    return (result.astype(jnp.bfloat16), input_grad, mix_grad, query_grad, value_grad, merge_grad, merge_bias_grad, first_gain_grad, first_shift_grad, up_grad, up_bias_grad, down_grad, down_bias_grad, second_gain_grad, second_shift_grad)
```

```python
import functools, math
import jax, jax.numpy as jnp
from jax import lax
from jax.experimental import pallas as pl
from jax.experimental.pallas import tpu as pltpu
from jax.sharding import PartitionSpec as P

LANES = 128
FAR = -1000000000.0
IDS = 4
LN2 = math.log(2.0)


def nt(a, b):
    return lax.dot_general(a, b, (((1,), (1,)), ((), ())), preferred_element_type=jnp.float32)


def nn(a, b):
    return lax.dot_general(a, b, (((1,), (0,)), ((), ())), preferred_element_type=jnp.float32)


def lane_of(rows):
    return lax.broadcasted_iota(jnp.int32, (rows, LANES), 1)


def split3(x):
    high = x.astype(jnp.bfloat16).astype(jnp.float32)
    middle = (x - high).astype(jnp.bfloat16).astype(jnp.float32)
    return high, middle, x - high - middle


def gather_blocks(info, block, count, own_ref, mate_ref, put):
    for b in range(count):
        start = pl.multiple_of(((b // 2) ^ info[1]) * block, block)

        @pl.when(info[0] == b % 2)
        def _():
            put(b, own_ref[pl.ds(start, block), :])

        @pl.when(info[0] != b % 2)
        def _():
            put(b, mate_ref[pl.ds(start, block), :])


def forward_kernel(info, q_ref, k_own, k_mate, v_own, v_mate, qx_ref, kx_ref, out_ref, ext_ref, k_all, vt_all, *, size):
    slot = pl.program_id(1)
    block = q_ref.shape[0]
    count = kx_ref.shape[0] // block
    heads = LANES // size
    lane_head = lane_of(block) // size

    @pl.when(slot == 0)
    def _():
        def put_k(b, rows):
            ext = kx_ref[b * block : (b + 1) * block, :]
            for h in range(heads):
                k_all[h, b * block : (b + 1) * block, :] = jnp.where(lane_head == h, rows, ext)

        def put_v(b, rows):
            turned = rows.T
            for h in range(heads):
                vt_all[h, :size, b * block : (b + 1) * block] = turned[h * size : (h + 1) * size]

        gather_blocks(info, block, count, k_own, k_mate, put_k)
        gather_blocks(info, block, count, v_own, v_mate, put_v)
        for h in range(heads):
            vt_all[h, size:, :] = jnp.ones((vt_all.shape[1] - size, vt_all.shape[2]), vt_all.dtype)

    rows = q_ref[...]
    qx = qx_ref[...]
    queries = [jnp.where(lane_head == h, rows, qx) for h in range(heads)]

    def step(kb, carry):
        start = pl.multiple_of(kb * block, block)
        fresh = []
        for h in range(heads):
            m, acc = carry[h]
            st = nt(k_all[h, pl.ds(start, block), :], queries[h])
            m_new = jnp.maximum(m, jnp.max(st, axis=0, keepdims=True))
            p = jnp.exp2(st - m_new).astype(jnp.bfloat16)
            acc = acc * jnp.exp2(m - m_new) + nn(vt_all[h, :, pl.ds(start, block)], p)
            fresh.append((m_new, acc))
        return tuple(fresh)

    start = tuple(
        (jnp.full((1, block), -jnp.inf, jnp.float32), jnp.zeros((vt_all.shape[1], block), jnp.float32))
        for _ in range(heads)
    )
    done = lax.fori_loop(info[2 + 2 * slot], info[3 + 2 * slot], step, start)
    sums = [acc[size : size + 1] for _, acc in done]
    out_t = jnp.concatenate([acc[:size] * (1.0 / l) for (_, acc), l in zip(done, sums)], axis=0)
    out_ref[...] = out_t.T.astype(out_ref.dtype)
    row = lax.broadcasted_iota(jnp.int32, (size, block), 0)
    parts = []
    for (m, _), l in zip(done, sums):
        pieces = split3(-(m + jnp.log2(l)))
        part = jnp.zeros((size, block), jnp.float32)
        for j, piece in enumerate(pieces):
            part = jnp.where(row == IDS + j, piece, part)
        parts.append(part)
    ext_ref[...] = (jnp.concatenate(parts[::-1], axis=0).T + qx.astype(jnp.float32)).astype(ext_ref.dtype)


def attention_forward(info, q, kv_own, kv_mate, qx, kx, size):
    rows, width = q.shape
    length = kx.shape[0]
    slots = (info.shape[0] - 2) // 2
    block = rows // slots
    pairs = width // LANES
    heads = LANES // size
    return pl.pallas_call(
        functools.partial(forward_kernel, size=size),
        grid_spec=pltpu.PrefetchScalarGridSpec(
            num_scalar_prefetch=1,
            grid=(pairs, slots),
            in_specs=[
                pl.BlockSpec((block, LANES), lambda p, s, i: (s, p)),
                pl.BlockSpec((rows, LANES), lambda p, s, i: (0, p)),
                pl.BlockSpec((rows, LANES), lambda p, s, i: (0, p)),
                pl.BlockSpec((rows, LANES), lambda p, s, i: (0, pairs + p)),
                pl.BlockSpec((rows, LANES), lambda p, s, i: (0, pairs + p)),
                pl.BlockSpec((block, LANES), lambda p, s, i: (s, 0)),
                pl.BlockSpec((length, LANES), lambda p, s, i: (0, 0)),
            ],
            out_specs=[pl.BlockSpec((block, LANES), lambda p, s, i: (s, p))] * 2,
            scratch_shapes=[
                pltpu.VMEM((heads, length, LANES), jnp.bfloat16),
                pltpu.VMEM((heads, size + 16, length), jnp.bfloat16),
            ],
        ),
        out_shape=[jax.ShapeDtypeStruct((rows, width), jnp.bfloat16)] * 2,
        compiler_params=pltpu.CompilerParams(dimension_semantics=("arbitrary", "arbitrary")),
        cost_estimate=pl.CostEstimate(
            flops=2 * rows * length * width, bytes_accessed=8 * rows * width * 2, transcendentals=rows * length * pairs
        ),
        name="attention_forward",
    )(info, q, kv_own, kv_mate, kv_own, kv_mate, qx, kx)


def backward_kernel(
    info, q_ref, ext_ref, do_ref, ctx_ref, k_own, k_mate, v_own, v_mate, kx_ref,
    dq_ref, own_ref, mate_ref, k_all, kt_all, v_all, dk_all, dv_all, *, size
):
    slot = pl.program_id(1)
    block = q_ref.shape[0]
    count = kx_ref.shape[0] // block
    heads = LANES // size
    lane = lane_of(block)
    lane_head = lane // size
    place = lane % size
    three = (place >= IDS) & (place < IDS + 3)

    @pl.when(slot == 0)
    def _():
        def put_k(b, rows):
            ext = kx_ref[b * block : (b + 1) * block, :]
            for h in range(heads):
                k_all[h, b * block : (b + 1) * block, :] = jnp.where(lane_head == h, rows, ext)
            kt_all[:, b * block : (b + 1) * block] = rows.T

        def put_v(b, rows):
            one = three.astype(rows.dtype)
            for h in range(heads):
                v_all[h, b * block : (b + 1) * block, :] = jnp.where(lane_head == h, rows, one)

        gather_blocks(info, block, count, k_own, k_mate, put_k)
        gather_blocks(info, block, count, v_own, v_mate, put_v)
        dk_all[...] = jnp.zeros_like(dk_all)
        dv_all[...] = jnp.zeros_like(dv_all)

    rows = q_ref[...]
    ext = ext_ref[...]
    grads = do_ref[...]
    zero = jnp.zeros_like(rows)
    queries = [jnp.where(lane_head == h, rows, ext) for h in range(heads)]
    plain_q = jnp.concatenate([jnp.where(lane_head == h, rows, zero) for h in range(heads)], axis=0)
    plain_do = jnp.concatenate([jnp.where(lane_head == h, grads, zero) for h in range(heads)], axis=0)
    product = grads.astype(jnp.float32) * ctx_ref[...].astype(jnp.float32)
    outs = []
    for h in range(heads):
        delta = jnp.sum(jnp.where(lane_head == h, product, 0.0), axis=1, keepdims=True)
        wide = jnp.zeros((block, LANES), jnp.float32)
        for j, piece in enumerate(split3(-delta)):
            wide = jnp.where(place == IDS + j, piece, wide)
        outs.append(jnp.where(lane_head == h, grads, wide.astype(grads.dtype)))

    def step(kb, carry):
        start = pl.multiple_of(kb * block, block)
        probs, scores, fresh = [], [], []
        for h in range(heads):
            p = jnp.exp2(nt(k_all[h, pl.ds(start, block), :], queries[h]))
            ds = (p * nt(v_all[h, pl.ds(start, block), :], outs[h])).astype(jnp.bfloat16)
            probs.append(p.astype(jnp.bfloat16))
            scores.append(ds)
            fresh.append(carry[h] + nn(kt_all[h * size : (h + 1) * size, pl.ds(start, block)], ds))
        dv_all[pl.ds(start, block), :] += nn(jnp.concatenate(probs, axis=1), plain_do)
        dk_all[pl.ds(start, block), :] += nn(jnp.concatenate(scores, axis=1), plain_q)
        return tuple(fresh)

    dq = lax.fori_loop(
        info[2 + 2 * slot], info[3 + 2 * slot], step,
        tuple(jnp.zeros((size, block), jnp.float32) for _ in range(heads)),
    )
    dq_ref[...] = (jnp.concatenate(dq, axis=0) * (1.0 / math.sqrt(size))).T.astype(dq_ref.dtype)

    @pl.when(slot == pl.num_programs(1) - 1)
    def _():
        for b in range(count):
            spot = pl.multiple_of(((b // 2) ^ info[1]) * block, block)
            for j, (total, factor) in enumerate(((dk_all, LN2), (dv_all, 1.0))):

                @pl.when(info[0] == b % 2)
                def _():
                    own_ref[j, pl.ds(spot, block), :] = (total[pl.ds(b * block, block), :] * factor).astype(own_ref.dtype)

                @pl.when(info[0] != b % 2)
                def _():
                    mate_ref[j, pl.ds(spot, block), :] = (total[pl.ds(b * block, block), :] * factor).astype(mate_ref.dtype)


def attention_backward(info, q, ext, grads, ctx, kv_own, kv_mate, kx, size):
    rows, width = q.shape
    length = kx.shape[0]
    slots = (info.shape[0] - 2) // 2
    block = rows // slots
    pairs = width // LANES
    heads = LANES // size
    tile = pl.BlockSpec((block, LANES), lambda p, s, i: (s, p))
    return pl.pallas_call(
        functools.partial(backward_kernel, size=size),
        grid_spec=pltpu.PrefetchScalarGridSpec(
            num_scalar_prefetch=1,
            grid=(pairs, slots),
            in_specs=[
                tile, tile, tile, tile,
                pl.BlockSpec((rows, LANES), lambda p, s, i: (0, p)),
                pl.BlockSpec((rows, LANES), lambda p, s, i: (0, p)),
                pl.BlockSpec((rows, LANES), lambda p, s, i: (0, pairs + p)),
                pl.BlockSpec((rows, LANES), lambda p, s, i: (0, pairs + p)),
                pl.BlockSpec((length, LANES), lambda p, s, i: (0, 0)),
            ],
            out_specs=[
                tile,
                pl.BlockSpec((2, rows, LANES), lambda p, s, i: (0, 0, p)),
                pl.BlockSpec((2, rows, LANES), lambda p, s, i: (0, 0, p)),
            ],
            scratch_shapes=[
                pltpu.VMEM((heads, length, LANES), jnp.bfloat16),
                pltpu.VMEM((LANES, length), jnp.bfloat16),
                pltpu.VMEM((heads, length, LANES), jnp.bfloat16),
                pltpu.VMEM((length, LANES), jnp.float32),
                pltpu.VMEM((length, LANES), jnp.float32),
            ],
        ),
        out_shape=[
            jax.ShapeDtypeStruct((rows, width), jnp.bfloat16),
            jax.ShapeDtypeStruct((2, rows, width), jnp.float32),
            jax.ShapeDtypeStruct((2, rows, width), jnp.bfloat16),
        ],
        compiler_params=pltpu.CompilerParams(dimension_semantics=("arbitrary", "arbitrary")),
        cost_estimate=pl.CostEstimate(
            flops=5 * rows * length * width, bytes_accessed=12 * rows * width * 2, transcendentals=rows * length * pairs
        ),
        name="attention_backward",
    )(info, q, ext, grads, ctx, kv_own, kv_mate, kv_own, kv_mate, kx)


def key_extension(ids):
    place = jnp.arange(LANES) % (LANES // 2)
    hot = ids[:, None] == place[None, :]
    return (hot | ((place >= IDS) & (place < IDS + 3))[None, :]).astype(jnp.bfloat16)


def query_extension(ids):
    place = jnp.arange(LANES) % (LANES // 2)
    other = (place < IDS)[None, :] & (ids[:, None] != place[None, :])
    return jnp.where(other, FAR, 0.0).astype(jnp.bfloat16)


H = 12
HD = 64
LOG2E = 1.0 / LN2
eps_norm = 1e-06
bf16 = jnp.bfloat16
f32 = jnp.float32


def norm_forward(total, gain, shift):
    middle = jnp.mean(total, axis=-1, keepdims=True)
    centred = total - middle
    factor = lax.rsqrt(jnp.mean(centred * centred, axis=-1, keepdims=True) + eps_norm)
    normed = centred * factor
    return (normed * gain + shift, normed, factor)


def norm_backward(grad_out, normed, factor, gain):
    scaled = grad_out * gain
    inner = (
        scaled
        - jnp.mean(scaled, axis=-1, keepdims=True)
        - normed * jnp.mean(scaled * normed, axis=-1, keepdims=True)
    )
    return (factor * inner, jnp.sum(grad_out * normed, axis=0), jnp.sum(grad_out, axis=0))


def gelu_parts(hidden):
    normal_cdf = 0.5 * (1.0 + jax.scipy.special.erf(hidden * (1.0 / math.sqrt(2.0))))
    density = jnp.exp(-0.5 * hidden * hidden) * (1.0 / math.sqrt(2.0 * math.pi))
    return (hidden * normal_cdf, normal_cdf + hidden * density)


def dot(a, b):
    return jnp.dot(a, b, preferred_element_type=f32)


def column_sums(values):
    return jnp.sum(values.astype(f32), axis=0)


def xor_pairs(size, bits):
    return [(i, i ^ bits) for i in range(size)]


def pick(values, index, axis=0):
    return lax.dynamic_index_in_dim(values, index, axis, keepdims=False)


class Places:
    def __init__(self):
        self.columns = lax.axis_size("seq")
        self.shards = lax.axis_size("fsdp")
        self.column = lax.axis_index("seq")
        shard = lax.axis_index("fsdp")
        self.core = shard & 1
        self.plane = shard >> 1

    def mate(self, values):
        return lax.ppermute(values, "fsdp", xor_pairs(self.shards, 1))

    def across(self, values, bits):
        return lax.ppermute(values, "seq", xor_pairs(self.columns, bits))

    def aside(self, values, bits):
        return lax.ppermute(values, "fsdp", xor_pairs(self.shards, 2 * bits))


def to_sequence(here, values):
    groups, piece, width = values.shape
    halves = values.reshape(groups, 2, piece // 2, width)
    kept = pick(halves, here.core, 1)
    other = here.mate(pick(halves, 1 - here.core, 1))
    both = jnp.concatenate([kept, other], axis=0)
    slots = []
    for k in range(here.columns):
        want = here.column ^ k
        part = pick(both, ((want // groups) ^ here.core) * groups + want % groups)
        slots.append(here.across(part, k) if k else part)
    return jnp.stack(slots)


def from_sequence(here, slots, groups):
    rows = jnp.stack([here.across(slots[k], k) if k else slots[k] for k in range(here.columns)])

    def of(core):
        return jnp.stack([pick(rows, here.column ^ (core * groups + j)) for j in range(groups)])

    kept = of(here.core)
    other = here.mate(of(1 - here.core))
    first = here.core == 0
    return jnp.concatenate([jnp.where(first, kept, other), jnp.where(first, other, kept)], axis=1)


def reduce_share(here, partial):
    shards, rows, width = partial.shape
    pairs = partial.reshape(shards // 2, 2, rows, width)
    total = pick(pairs, here.core, 1).astype(f32) + here.mate(pick(pairs, 1 - here.core, 1).astype(bf16)).astype(f32)
    low = total.astype(bf16)
    share = pick(total, here.plane)
    for k in range(1, shards // 2):
        share = share + here.aside(pick(low, here.plane ^ k), k).astype(f32)
    low = share.astype(bf16).reshape(2, rows // 2, width)
    side = here.column & 1
    half = pick(low, side).astype(f32) + here.across(pick(low, 1 - side), 1).astype(f32)
    step = 2
    while step < here.columns:
        low = half.astype(bf16)
        half = low.astype(f32) + here.across(low, step).astype(f32)
        step *= 2
    half = half.astype(bf16)
    other = here.across(half, 1)
    first = side == 0
    return jnp.concatenate([jnp.where(first, half, other), jnp.where(first, other, half)], axis=0).astype(f32)


def per_device(
    tokens,
    segment_ids,
    mix_weight,
    query_bias,
    value_bias,
    merge_weight,
    merge_bias,
    first_gain,
    first_shift,
    up_weight,
    up_bias,
    down_weight,
    down_bias,
    second_gain,
    second_shift,
    output_grad,
):
    here = Places()
    groups, piece, width = tokens.shape
    shards = here.shards
    own = width // shards
    hidden_size = up_weight.shape[1]
    half = piece // 2
    rows = here.columns * half
    length = here.columns * piece

    mix_local = mix_weight.reshape(own, H, 3, HD).transpose(0, 2, 1, 3).reshape(own, 3 * width)
    mix_full = lax.all_gather(mix_local, "fsdp", axis=0, tiled=True)
    small = (query_bias, value_bias, merge_bias, first_gain, first_shift, down_bias, second_gain, second_shift, up_bias)
    packed = lax.all_gather(jnp.concatenate(small).reshape(1, -1), "fsdp", axis=0, tiled=True).astype(f32)

    def vector(j):
        return packed[:, j * own : (j + 1) * own].reshape(-1)

    query_full, value_full, merge_bias_full, gain_one, shift_one, down_bias_full, gain_two, shift_two = map(vector, range(8))
    up_bias_full = packed[:, 8 * own :].reshape(-1)
    merge_full = lax.all_gather(merge_weight, "fsdp", axis=0, tiled=True)
    up_full = lax.all_gather(up_weight, "fsdp", axis=0, tiled=True)
    down_full = lax.all_gather(down_weight, "fsdp", axis=0, tiled=True)

    ids_own = to_sequence(here, segment_ids.reshape(groups, piece, 1)).reshape(here.columns, half)
    ids_mate = here.mate(ids_own)
    by_core = jnp.stack([jnp.where(here.core == 0, ids_own, ids_mate), jnp.where(here.core == 0, ids_mate, ids_own)], axis=1)
    ids = jnp.stack([pick(by_core, k ^ here.column) for k in range(here.columns)]).reshape(2 * here.columns, half)
    blocks = 2 * (jnp.arange(here.columns) ^ here.column) + here.core
    first_id, last_id = ids[:, 0], ids[:, -1]
    low = jnp.sum(last_id[None, :] < ids_own[:, :1], axis=1)
    high = jnp.sum(first_id[None, :] <= ids_own[:, -1:], axis=1)
    info = jnp.concatenate([jnp.stack([here.core, here.column]), jnp.stack([low, high], axis=1).reshape(-1)]).astype(jnp.int32)
    key_ext = key_extension(ids.reshape(length))
    query_ext = query_extension(ids_own.reshape(rows))

    flat = to_sequence(here, tokens).reshape(rows, width)
    cotangent = to_sequence(here, output_grad).reshape(rows, width).astype(f32)

    kv_bias = jnp.concatenate([jnp.zeros_like(value_full), value_full])
    key_value = (dot(flat, mix_full[:, width:]) + kv_bias).astype(bf16)
    query = ((dot(flat, mix_full[:, :width]) + query_full) * (LOG2E / math.sqrt(HD))).astype(bf16)
    key_value_mate = here.mate(key_value)
    context, ext = attention_forward(info, query, key_value, key_value_mate, query_ext, key_ext, HD)

    attended = dot(context, merge_full) + merge_bias_full
    first_out, normed_one, factor_one = norm_forward(flat.astype(f32) + attended, gain_one, shift_one)
    first_low = first_out.astype(bf16)
    hidden = dot(first_low, up_full) + up_bias_full
    active, slope = gelu_parts(hidden)
    active_low = active.astype(bf16)
    branch = dot(active_low, down_full) + down_bias_full
    result, normed_two, factor_two = norm_forward(first_out + branch, gain_two, shift_two)
    output = from_sequence(here, result.astype(bf16).reshape(here.columns, half, width), groups)

    grad_second, second_gain_grad, second_shift_grad = norm_backward(cotangent, normed_two, factor_two, gain_two)
    grad_branch = grad_second.astype(bf16)
    down_grad = dot(active_low.T, grad_branch)
    down_bias_grad = column_sums(grad_branch)
    grad_active = dot(grad_branch, down_full.T)
    grad_hidden = (grad_active * slope).astype(bf16)
    up_grad = dot(first_low.T, grad_hidden)
    up_bias_grad = column_sums(grad_hidden)
    grad_first = grad_second + dot(grad_hidden, up_full.T)
    grad_sum, first_gain_grad, first_shift_grad = norm_backward(grad_first, normed_one, factor_one, gain_one)
    grad_attended = grad_sum.astype(bf16)
    merge_grad = dot(context.T, grad_attended)
    merge_bias_grad = column_sums(grad_attended)
    grad_context = dot(grad_attended, merge_full.T).astype(bf16)

    final_down = reduce_share(here, down_grad.reshape(shards, -1, width))
    final_up = reduce_share(here, up_grad.reshape(shards, own, hidden_size))
    final_merge = reduce_share(here, merge_grad.reshape(shards, own, width))

    grad_query, grad_own, grad_mate = attention_backward(
        info, query, ext, grad_context, context, key_value, key_value_mate, key_ext, HD
    )
    grad_kv = (grad_own + here.mate(grad_mate).astype(f32)).astype(bf16)
    grad_mixed = jnp.concatenate([grad_query, grad_kv[0], grad_kv[1]], axis=1)
    mix_grad = dot(flat.T, grad_mixed)
    bias_sums = column_sums(grad_mixed)
    query_grad, value_grad = bias_sums[:width], bias_sums[2 * width :]
    input_grad = (grad_sum + dot(grad_mixed, mix_full.T)).astype(bf16)
    final_input = from_sequence(here, input_grad.reshape(here.columns, half, width), groups).astype(f32)

    final_mix = reduce_share(here, mix_grad.reshape(shards, own, 3 * width))
    final_mix = final_mix.reshape(own, 3, H, HD).transpose(0, 2, 1, 3).reshape(own, 3 * width)
    vectors = (
        query_grad,
        value_grad,
        merge_bias_grad,
        first_gain_grad,
        first_shift_grad,
        down_bias_grad,
        second_gain_grad,
        second_shift_grad,
        up_bias_grad,
    )
    packed_grad = jnp.concatenate([v.reshape(shards, -1) for v in vectors], axis=1)
    final_packed = reduce_share(here, packed_grad.reshape(shards, 2, -1)).reshape(-1)
    finals = [final_packed[j * own : (j + 1) * own] for j in range(8)] + [final_packed[8 * own :]]
    (
        final_query,
        final_value,
        final_merge_bias,
        final_gain_one,
        final_shift_one,
        final_down_bias,
        final_gain_two,
        final_shift_two,
        final_up_bias,
    ) = finals
    return (
        output,
        final_input,
        final_mix,
        final_query,
        final_value,
        final_merge,
        final_merge_bias,
        final_gain_one,
        final_shift_one,
        final_up,
        final_up_bias,
        final_down,
        final_down_bias,
        final_gain_two,
        final_shift_two,
    )


def solution(mesh):
    wide, row, thin = P("fsdp", "seq", None), P("fsdp", None), P("fsdp")
    return jax.shard_map(
        per_device,
        mesh=mesh,
        in_specs=(wide, P("fsdp", "seq"), row, thin, thin, row, thin, thin, thin, row, thin, row, thin, thin, thin, wide),
        out_specs=(wide, wide, row, thin, thin, row, thin, thin, thin, row, thin, row, thin, thin, thin),
        check_vma=False,
    )
```

```python
import functools, math
import jax, jax.numpy as jnp
from jax import lax
from jax.experimental import pallas as pl
from jax.experimental.pallas import tpu as pltpu
from jax.sharding import PartitionSpec as P

LANES = 128
FAR = -1000000000.0
IDS = 4
LN2 = math.log(2.0)


def nt(a, b):
    return lax.dot_general(a, b, (((1,), (1,)), ((), ())), preferred_element_type=jnp.float32)


def nn(a, b):
    return lax.dot_general(a, b, (((1,), (0,)), ((), ())), preferred_element_type=jnp.float32)


def lane_of(rows):
    return lax.broadcasted_iota(jnp.int32, (rows, LANES), 1)


def split3(x):
    high = x.astype(jnp.bfloat16).astype(jnp.float32)
    middle = (x - high).astype(jnp.bfloat16).astype(jnp.float32)
    return high, middle, x - high - middle


def gather_blocks(info, block, count, own_ref, mate_ref, put):
    for b in range(count):
        start = pl.multiple_of(((b // 2) ^ info[1]) * block, block)

        @pl.when(info[0] == b % 2)
        def _():
            put(b, own_ref[pl.ds(start, block), :])

        @pl.when(info[0] != b % 2)
        def _():
            put(b, mate_ref[pl.ds(start, block), :])


def forward_kernel(info, q_ref, k_own, k_mate, v_own, v_mate, qx_ref, kx_ref, out_ref, ext_ref, k_all, vt_all, s_all, *, size):
    slot = pl.program_id(1)
    block = q_ref.shape[0]
    count = kx_ref.shape[0] // block
    heads = LANES // size
    lane_head = lane_of(block) // size

    @pl.when(slot == 0)
    def _():
        def put_k(b, rows):
            ext = kx_ref[b * block : (b + 1) * block, :]
            for h in range(heads):
                k_all[h, b * block : (b + 1) * block, :] = jnp.where(lane_head == h, rows, ext)

        def put_v(b, rows):
            turned = rows.T
            for h in range(heads):
                vt_all[h, :size, b * block : (b + 1) * block] = turned[h * size : (h + 1) * size]

        gather_blocks(info, block, count, k_own, k_mate, put_k)
        gather_blocks(info, block, count, v_own, v_mate, put_v)
        for h in range(heads):
            vt_all[h, size:, :] = jnp.ones((vt_all.shape[1] - size, vt_all.shape[2]), vt_all.dtype)

    rows = q_ref[...]
    qx = qx_ref[...]
    queries = [jnp.where(lane_head == h, rows, qx) for h in range(heads)]

    part = block
    lo, hi = info[2 + 2 * slot], info[3 + 2 * slot]

    def score(h, kb, i, top):
        at = pl.multiple_of(kb * block + i * part, part)
        st = nt(k_all[h, pl.ds(at, part), :], queries[h])
        s_all[h, i * part : (i + 1) * part, :] = st
        return jnp.maximum(top, jnp.max(st.reshape(part // 8, 8, block), axis=0))

    def weigh(h, kb, i, m, acc):
        at = pl.multiple_of(kb * block + i * part, part)
        p = jnp.exp2(s_all[h, i * part : (i + 1) * part, :] - m).astype(jnp.bfloat16)
        return acc + nn(vt_all[h, :, pl.ds(at, part)], p)

    least = jnp.full((8, block), -jnp.inf, jnp.float32)

    def step(kb, carry):
        tops, state = carry
        tops, state = list(tops), list(state)
        after = jnp.minimum(kb + 1, count - 1)
        for h in range(heads):
            ahead = (h + 1) % heads
            ahead_kb = kb if ahead else after
            m, acc = state[h]
            m_new = jnp.maximum(m, jnp.max(tops[h], axis=0, keepdims=True))
            acc = acc * jnp.exp2(m - m_new)
            top = least
            for i in range(1):
                top = score(ahead, ahead_kb, i, top)
                acc = weigh(h, kb, i, m_new, acc)
            tops[ahead] = top
            state[h] = (m_new, acc)
        return tuple(tops), tuple(state)

    start = tuple(
        (jnp.full((1, block), -jnp.inf, jnp.float32), jnp.zeros((vt_all.shape[1], block), jnp.float32))
        for _ in range(heads)
    )
    first = score(0, lo, 0, least)
    _, done = lax.fori_loop(lo, hi, step, ((first,) + (least,) * (heads - 1), start))
    sums = [acc[size : size + 1] for _, acc in done]
    out_t = jnp.concatenate([acc[:size] * (1.0 / l) for (_, acc), l in zip(done, sums)], axis=0)
    out_ref[...] = out_t.T.astype(out_ref.dtype)
    row = lax.broadcasted_iota(jnp.int32, (size, block), 0)
    parts = []
    for (m, _), l in zip(done, sums):
        pieces = split3(-(m + jnp.log2(l)))
        part = jnp.zeros((size, block), jnp.float32)
        for j, piece in enumerate(pieces):
            part = jnp.where(row == IDS + j, piece, part)
        parts.append(part)
    ext_ref[...] = (jnp.concatenate(parts[::-1], axis=0).T + qx.astype(jnp.float32)).astype(ext_ref.dtype)


def attention_forward(info, q, kv_own, kv_mate, qx, kx, size):
    rows, width = q.shape
    length = kx.shape[0]
    slots = (info.shape[0] - 2) // 2
    block = rows // slots
    pairs = width // LANES
    heads = LANES // size
    return pl.pallas_call(
        functools.partial(forward_kernel, size=size),
        grid_spec=pltpu.PrefetchScalarGridSpec(
            num_scalar_prefetch=1,
            grid=(pairs, slots),
            in_specs=[
                pl.BlockSpec((block, LANES), lambda p, s, i: (s, p)),
                pl.BlockSpec((rows, LANES), lambda p, s, i: (0, p)),
                pl.BlockSpec((rows, LANES), lambda p, s, i: (0, p)),
                pl.BlockSpec((rows, LANES), lambda p, s, i: (0, pairs + p)),
                pl.BlockSpec((rows, LANES), lambda p, s, i: (0, pairs + p)),
                pl.BlockSpec((block, LANES), lambda p, s, i: (s, 0)),
                pl.BlockSpec((length, LANES), lambda p, s, i: (0, 0)),
            ],
            out_specs=[pl.BlockSpec((block, LANES), lambda p, s, i: (s, p))] * 2,
            scratch_shapes=[
                pltpu.VMEM((heads, length, LANES), jnp.bfloat16),
                pltpu.VMEM((heads, size + 16, length), jnp.bfloat16),
                pltpu.VMEM((heads, block, block), jnp.float32),
            ],
        ),
        out_shape=[jax.ShapeDtypeStruct((rows, width), jnp.bfloat16)] * 2,
        compiler_params=pltpu.CompilerParams(dimension_semantics=("arbitrary", "arbitrary")),
        cost_estimate=pl.CostEstimate(
            flops=2 * rows * length * width, bytes_accessed=8 * rows * width * 2, transcendentals=rows * length * pairs
        ),
        name="attention_forward",
    )(info, q, kv_own, kv_mate, kv_own, kv_mate, qx, kx)


def backward_kernel(
    info, q_ref, ext_ref, do_ref, ctx_ref, k_own, k_mate, v_own, v_mate, kx_ref,
    dq_ref, own_ref, mate_ref, k_all, kt_all, v_all, dk_all, dv_all, *, size
):
    slot = pl.program_id(1)
    block = q_ref.shape[0]
    count = kx_ref.shape[0] // block
    heads = LANES // size
    lane = lane_of(block)
    lane_head = lane // size
    place = lane % size
    three = (place >= IDS) & (place < IDS + 3)

    @pl.when(slot == 0)
    def _():
        def put_k(b, rows):
            ext = kx_ref[b * block : (b + 1) * block, :]
            for h in range(heads):
                k_all[h, b * block : (b + 1) * block, :] = jnp.where(lane_head == h, rows, ext)
            kt_all[:, b * block : (b + 1) * block] = rows.T

        def put_v(b, rows):
            one = three.astype(rows.dtype)
            for h in range(heads):
                v_all[h, b * block : (b + 1) * block, :] = jnp.where(lane_head == h, rows, one)

        gather_blocks(info, block, count, k_own, k_mate, put_k)
        gather_blocks(info, block, count, v_own, v_mate, put_v)
        dk_all[...] = jnp.zeros_like(dk_all)
        dv_all[...] = jnp.zeros_like(dv_all)

    rows = q_ref[...]
    ext = ext_ref[...]
    grads = do_ref[...]
    zero = jnp.zeros_like(rows)
    queries = [jnp.where(lane_head == h, rows, ext) for h in range(heads)]
    plain_q = jnp.concatenate([jnp.where(lane_head == h, rows, zero) for h in range(heads)], axis=0)
    plain_do = jnp.concatenate([jnp.where(lane_head == h, grads, zero) for h in range(heads)], axis=0)
    product = grads.astype(jnp.float32) * ctx_ref[...].astype(jnp.float32)
    outs = []
    for h in range(heads):
        delta = jnp.sum(jnp.where(lane_head == h, product, 0.0), axis=1, keepdims=True)
        wide = jnp.zeros((block, LANES), jnp.float32)
        for j, piece in enumerate(split3(-delta)):
            wide = jnp.where(place == IDS + j, piece, wide)
        outs.append(jnp.where(lane_head == h, grads, wide.astype(grads.dtype)))

    def step(kb, carry):
        start = pl.multiple_of(kb * block, block)
        probs, scores, fresh = [], [], []
        for h in range(heads):
            p = jnp.exp2(nt(k_all[h, pl.ds(start, block), :], queries[h]))
            ds = (p * nt(v_all[h, pl.ds(start, block), :], outs[h])).astype(jnp.bfloat16)
            probs.append(p.astype(jnp.bfloat16))
            scores.append(ds)
            fresh.append(carry[h] + nn(kt_all[h * size : (h + 1) * size, pl.ds(start, block)], ds))
        dv_all[pl.ds(start, block), :] += nn(jnp.concatenate(probs, axis=1), plain_do)
        dk_all[pl.ds(start, block), :] += nn(jnp.concatenate(scores, axis=1), plain_q)
        return tuple(fresh)

    dq = lax.fori_loop(
        info[2 + 2 * slot], info[3 + 2 * slot], step,
        tuple(jnp.zeros((size, block), jnp.float32) for _ in range(heads)),
    )
    dq_ref[...] = (jnp.concatenate(dq, axis=0) * (1.0 / math.sqrt(size))).T.astype(dq_ref.dtype)

    @pl.when(slot == pl.num_programs(1) - 1)
    def _():
        for b in range(count):
            spot = pl.multiple_of(((b // 2) ^ info[1]) * block, block)
            for j, (total, factor) in enumerate(((dk_all, LN2), (dv_all, 1.0))):

                @pl.when(info[0] == b % 2)
                def _():
                    own_ref[j, pl.ds(spot, block), :] = (total[pl.ds(b * block, block), :] * factor).astype(own_ref.dtype)

                @pl.when(info[0] != b % 2)
                def _():
                    mate_ref[j, pl.ds(spot, block), :] = (total[pl.ds(b * block, block), :] * factor).astype(mate_ref.dtype)


def attention_backward(info, q, ext, grads, ctx, kv_own, kv_mate, kx, size, first, some):
    rows, width = q.shape
    length = kx.shape[0]
    slots = (info.shape[0] - 2) // 2
    block = rows // slots
    pairs = width // LANES
    heads = LANES // size
    tile = pl.BlockSpec((block, LANES), lambda p, s, i: (s, first + p))
    out_tile = pl.BlockSpec((block, LANES), lambda p, s, i: (s, p))
    return pl.pallas_call(
        functools.partial(backward_kernel, size=size),
        grid_spec=pltpu.PrefetchScalarGridSpec(
            num_scalar_prefetch=1,
            grid=(some, slots),
            in_specs=[
                tile, tile, tile, tile,
                pl.BlockSpec((rows, LANES), lambda p, s, i: (0, first + p)),
                pl.BlockSpec((rows, LANES), lambda p, s, i: (0, first + p)),
                pl.BlockSpec((rows, LANES), lambda p, s, i: (0, pairs + first + p)),
                pl.BlockSpec((rows, LANES), lambda p, s, i: (0, pairs + first + p)),
                pl.BlockSpec((length, LANES), lambda p, s, i: (0, 0)),
            ],
            out_specs=[
                out_tile,
                pl.BlockSpec((2, rows, LANES), lambda p, s, i: (0, 0, p)),
                pl.BlockSpec((2, rows, LANES), lambda p, s, i: (0, 0, p)),
            ],
            scratch_shapes=[
                pltpu.VMEM((heads, length, LANES), jnp.bfloat16),
                pltpu.VMEM((LANES, length), jnp.bfloat16),
                pltpu.VMEM((heads, length, LANES), jnp.bfloat16),
                pltpu.VMEM((length, LANES), jnp.float32),
                pltpu.VMEM((length, LANES), jnp.float32),
            ],
        ),
        out_shape=[
            jax.ShapeDtypeStruct((rows, some * LANES), jnp.bfloat16),
            jax.ShapeDtypeStruct((2, rows, some * LANES), jnp.float32),
            jax.ShapeDtypeStruct((2, rows, some * LANES), jnp.bfloat16),
        ],
        compiler_params=pltpu.CompilerParams(dimension_semantics=("arbitrary", "arbitrary")),
        cost_estimate=pl.CostEstimate(
            flops=5 * rows * length * some * LANES,
            bytes_accessed=24 * rows * some * LANES,
            transcendentals=rows * length * some,
        ),
        name="attention_backward",
    )(info, q, ext, grads, ctx, kv_own, kv_mate, kv_own, kv_mate, kx)


def key_extension(ids):
    place = jnp.arange(LANES) % (LANES // 2)
    hot = ids[:, None] == place[None, :]
    return (hot | ((place >= IDS) & (place < IDS + 3))[None, :]).astype(jnp.bfloat16)


def query_extension(ids):
    place = jnp.arange(LANES) % (LANES // 2)
    other = (place < IDS)[None, :] & (ids[:, None] != place[None, :])
    return jnp.where(other, FAR, 0.0).astype(jnp.bfloat16)


H = 12
HD = 64
LOG2E = 1.0 / LN2
PARTS = 3
eps_norm = 1e-06
bf16 = jnp.bfloat16
f32 = jnp.float32


def norm_forward(total, gain, shift):
    middle = jnp.mean(total, axis=-1, keepdims=True)
    centred = total - middle
    factor = lax.rsqrt(jnp.mean(centred * centred, axis=-1, keepdims=True) + eps_norm)
    normed = centred * factor
    return (normed * gain + shift, normed, factor)


def norm_backward(grad_out, normed, factor, gain):
    scaled = grad_out * gain
    inner = (
        scaled
        - jnp.mean(scaled, axis=-1, keepdims=True)
        - normed * jnp.mean(scaled * normed, axis=-1, keepdims=True)
    )
    return (factor * inner, jnp.sum(grad_out * normed, axis=0), jnp.sum(grad_out, axis=0))


def gelu_parts(hidden):
    normal_cdf = 0.5 * (1.0 + jax.scipy.special.erf(hidden * (1.0 / math.sqrt(2.0))))
    density = jnp.exp(-0.5 * hidden * hidden) * (1.0 / math.sqrt(2.0 * math.pi))
    return (hidden * normal_cdf, normal_cdf + hidden * density)


def dot(a, b):
    return jnp.dot(a, b, preferred_element_type=f32)


def column_sums(values):
    return jnp.sum(values.astype(f32), axis=0)


def xor_pairs(size, bits):
    return [(i, i ^ bits) for i in range(size)]


def pick(values, index, axis=0):
    return lax.dynamic_index_in_dim(values, index, axis, keepdims=False)


def after(values, *marks):
    return lax.optimization_barrier((values, marks))[0]


class Places:
    def __init__(self):
        self.columns = lax.axis_size("seq")
        self.shards = lax.axis_size("fsdp")
        self.column = lax.axis_index("seq")
        self.shard = lax.axis_index("fsdp")
        self.core = self.shard & 1
        self.plane = self.shard >> 1

    def mate(self, values):
        return lax.ppermute(values, "fsdp", xor_pairs(self.shards, 1))

    def across(self, values, bits):
        return lax.ppermute(values, "seq", xor_pairs(self.columns, bits))

    def aside(self, values, bits):
        return lax.ppermute(values, "fsdp", xor_pairs(self.shards, 2 * bits))


def to_sequence(here, values):
    groups, piece, width = values.shape
    halves = values.reshape(groups, 2, piece // 2, width)
    kept = pick(halves, here.core, 1)
    other = here.mate(pick(halves, 1 - here.core, 1))
    both = jnp.concatenate([kept, other], axis=0)
    slots = []
    for k in range(here.columns):
        want = here.column ^ k
        part = pick(both, ((want // groups) ^ here.core) * groups + want % groups)
        slots.append(here.across(part, k) if k else part)
    return slots


def from_sequence_send(here, slots):
    return [here.across(slots[k], k) if k else slots[k] for k in range(here.columns)]


def from_sequence_end(here, slots, groups):
    rows = jnp.stack(slots)

    def of(core):
        return jnp.stack([pick(rows, here.column ^ (core * groups + j)) for j in range(groups)])

    kept = of(here.core)
    other = here.mate(of(1 - here.core))
    first = here.core == 0
    return jnp.concatenate([jnp.where(first, kept, other), jnp.where(first, other, kept)], axis=1)


def place_kernel(info, *refs):
    count = (len(refs) - 3) // 2
    parts, out, buffers = refs[:count], refs[count], refs[count + 1 : 2 * count + 1]
    in_sem, out_sem = refs[2 * count + 1 :]
    reads = [pltpu.make_async_copy(parts[k], buffers[k], in_sem.at[k]) for k in range(count)]
    writes = [pltpu.make_async_copy(buffers[k], out.at[info[k]], out_sem.at[k]) for k in range(count)]
    for read in reads:
        read.start()
    for read, write in zip(reads, writes):
        read.wait()
        write.start()
    for write in writes:
        write.wait()


def place(parts, spots):
    count, (rows, width), kind = len(parts), parts[0].shape, parts[0].dtype
    full = pl.pallas_call(
        place_kernel,
        grid_spec=pltpu.PrefetchScalarGridSpec(
            num_scalar_prefetch=1,
            grid=(),
            in_specs=[pl.BlockSpec(memory_space=pl.ANY)] * count,
            out_specs=pl.BlockSpec(memory_space=pl.ANY),
            scratch_shapes=[pltpu.VMEM((rows, width), kind)] * count
            + [pltpu.SemaphoreType.DMA((count,)), pltpu.SemaphoreType.DMA((count,))],
        ),
        out_shape=jax.ShapeDtypeStruct((count, rows, width), kind),
        cost_estimate=pl.CostEstimate(flops=0, bytes_accessed=2 * count * rows * width * 2, transcendentals=0),
        name="place_parts",
    )(jnp.stack(spots).astype(jnp.int32), *parts)
    return full.reshape(count * rows, width)


def gather_shards(here, local):
    if here.shards != 8:
        return lax.all_gather(local, "fsdp", axis=0, tiled=True)
    middle = local.shape[0] // 2
    across_x, across_y = here.aside(local, 1), here.aside(local, 2)
    corner = jnp.concatenate([here.aside(across_x[:middle], 2), here.aside(across_y[middle:], 1)], axis=0)
    parts = [local, across_x, across_y, corner]
    spots = [here.shard ^ (2 * k) for k in range(4)]
    return place(parts + [here.mate(part) for part in parts], spots + [spot ^ 1 for spot in spots])


def share_pair(here, partial):
    shards, rows, width = partial.shape
    pairs = partial.reshape(shards // 2, 2, rows, width)
    return pick(pairs, here.core, 1), here.mate(pick(pairs, 1 - here.core, 1).astype(bf16))


def share_plane(here, kept, other):
    total = kept.astype(f32) + other.astype(f32)
    low = total.astype(bf16)
    return pick(total, here.plane), [here.aside(pick(low, here.plane ^ k), k) for k in range(1, here.shards // 2)]


def share_sum(share, others):
    for other in others:
        share = share + other.astype(f32)
    return share.astype(bf16)


def column_first(here, share):
    low = share.reshape(2, share.shape[0] // 2, share.shape[1])
    side = here.column & 1
    return pick(low, side), here.across(pick(low, 1 - side), 1)


def column_second(here, half, other):
    low = (half.astype(f32) + other.astype(f32)).astype(bf16)
    step, others = 2, []
    while 2 * step < here.columns:
        low = (low.astype(f32) + here.across(low, step).astype(f32)).astype(bf16)
        step *= 2
    return low, here.across(low, step)


def column_third(here, half, other):
    half = (half.astype(f32) + other.astype(f32)).astype(bf16)
    return half, here.across(half, 1)


def column_last(here, half, other):
    first = (here.column & 1) == 0
    return jnp.concatenate([jnp.where(first, half, other), jnp.where(first, other, half)], axis=0)


def per_device(
    tokens,
    segment_ids,
    mix_weight,
    query_bias,
    value_bias,
    merge_weight,
    merge_bias,
    first_gain,
    first_shift,
    up_weight,
    up_bias,
    down_weight,
    down_bias,
    second_gain,
    second_shift,
    output_grad,
):
    here = Places()
    groups, piece, width = tokens.shape
    shards = here.shards
    own = width // shards
    hidden_size = up_weight.shape[1]
    half = piece // 2
    rows = here.columns * half
    length = here.columns * piece

    flat = jnp.concatenate(to_sequence(here, tokens), axis=0)

    vectors = (query_bias, value_bias, merge_bias, first_gain, first_shift, down_bias, second_gain, second_shift)
    columns = jnp.concatenate([jnp.stack(vectors, axis=1), up_bias.reshape(own, -1)], axis=1)
    columns = jnp.pad(columns, ((0, 0), (0, LANES - columns.shape[1])))
    mix_local = mix_weight.reshape(own, H, 3, HD).transpose(0, 2, 1, 3).reshape(own, 3 * width)
    mix_all = gather_shards(here, jnp.concatenate([mix_local, columns], axis=1))
    mix_full, columns_full = mix_all[:, : 3 * width], mix_all[:, 3 * width :].astype(f32)
    merge_up = gather_shards(here, jnp.concatenate([merge_weight, up_weight], axis=1))
    merge_full, up_full = merge_up[:, :width], merge_up[:, width:]
    down_full = gather_shards(here, down_weight)
    turned = columns_full[:, :8].T
    query_full, value_full, merge_bias_full, gain_one, shift_one, down_bias_full, gain_two, shift_two = [
        turned[j] for j in range(8)
    ]
    up_bias_full = columns_full[:, 8 : 8 + hidden_size // width].reshape(-1)

    ids_own = jnp.concatenate(to_sequence(here, segment_ids.reshape(groups, piece, 1)), axis=0).reshape(here.columns, half)
    ids_mate = here.mate(ids_own)
    by_core = jnp.stack([jnp.where(here.core == 0, ids_own, ids_mate), jnp.where(here.core == 0, ids_mate, ids_own)], axis=1)
    ids = jnp.stack([pick(by_core, k ^ here.column) for k in range(here.columns)]).reshape(2 * here.columns, half)
    first_id, last_id = ids[:, 0], ids[:, -1]
    low = jnp.sum(last_id[None, :] < ids_own[:, :1], axis=1)
    high = jnp.sum(first_id[None, :] <= ids_own[:, -1:], axis=1)
    info = jnp.concatenate([jnp.stack([here.core, here.column]), jnp.stack([low, high], axis=1).reshape(-1)]).astype(jnp.int32)
    key_ext = key_extension(ids.reshape(length))
    query_ext = query_extension(ids_own.reshape(rows))

    cotangent_slots = to_sequence(here, after(output_grad, flat))

    kv_bias = jnp.concatenate([jnp.zeros_like(value_full), value_full])
    key_value = (dot(flat, mix_full[:, width:]) + kv_bias).astype(bf16)
    query = ((dot(flat, mix_full[:, :width]) + query_full) * (LOG2E / math.sqrt(HD))).astype(bf16)
    key_value_mate = here.mate(key_value)
    context, ext = attention_forward(info, query, key_value, key_value_mate, query_ext, key_ext, HD)

    cotangent = jnp.concatenate(after(cotangent_slots, context), axis=0).astype(f32)
    merge_full, up_full, down_full = after((merge_full, up_full, down_full), context)

    attended = dot(context, merge_full) + merge_bias_full
    first_out, normed_one, factor_one = norm_forward(flat.astype(f32) + attended, gain_one, shift_one)
    first_low = first_out.astype(bf16)
    hidden = dot(first_low, up_full) + up_bias_full
    active, slope = gelu_parts(hidden)
    active_low = active.astype(bf16)
    branch = dot(active_low, down_full) + down_bias_full
    result, normed_two, factor_two = norm_forward(first_out + branch, gain_two, shift_two)
    output_slots = from_sequence_send(here, list(result.astype(bf16).reshape(here.columns, half, width)))

    grad_second, second_gain_grad, second_shift_grad = norm_backward(cotangent, normed_two, factor_two, gain_two)
    grad_branch = grad_second.astype(bf16)
    down_grad = dot(active_low.T, grad_branch)
    down_kept, down_other = share_pair(here, down_grad.reshape(shards, -1, width))
    down_bias_grad = column_sums(grad_branch)
    grad_active = dot(grad_branch, down_full.T)
    grad_hidden = (grad_active * slope).astype(bf16)
    down_share, down_others = share_plane(here, down_kept, after(down_other, grad_hidden))
    up_grad = dot(first_low.T, grad_hidden)
    up_bias_grad = column_sums(grad_hidden)
    grad_first = grad_second + dot(grad_hidden, up_full.T)
    grad_sum, first_gain_grad, first_shift_grad = norm_backward(grad_first, normed_one, factor_one, gain_one)
    grad_attended = grad_sum.astype(bf16)
    merge_grad = dot(context.T, grad_attended)
    merge_bias_grad = column_sums(grad_attended)
    up_merge = jnp.concatenate([up_grad.reshape(shards, own, hidden_size), merge_grad.reshape(shards, own, width)], axis=2)
    up_kept, up_other = share_pair(here, up_merge)
    grad_context = dot(grad_attended, merge_full.T).astype(bf16)
    up_share, up_others = share_plane(here, up_kept, after(up_other, grad_context))

    def backward(part, grads):
        pairs = width // LANES // PARTS
        dq, kept, other = attention_backward(
            info, query, ext, grads, context, key_value, key_value_mate, key_ext, HD, part * pairs, pairs
        )
        return dq, kept, here.mate(other)

    def mixed_part(pieces):
        dq, kept, other = pieces
        kv = (kept + other.astype(f32)).astype(bf16)
        return jnp.concatenate([dq, kv[0], kv[1]], axis=1)

    part_width = width // PARTS

    def weight_part(part):
        return jnp.concatenate(
            [mix_full[:, j * width + part * part_width : j * width + (part + 1) * part_width] for j in range(3)], axis=1
        )

    one = backward(0, after(grad_context, down_share, up_share))
    down_others, down_share = after((down_others, down_share), one[0])
    down_half, down_other = column_first(here, share_sum(down_share, down_others))
    up_others, up_share = after((up_others, up_share), one[0])
    up_half, up_other = column_first(here, share_sum(up_share, up_others))
    two = backward(1, after(grad_context, down_half, up_half))
    down_half, down_other = column_second(here, *after((down_half, down_other), two[0]))
    up_half, up_other = column_second(here, *after((up_half, up_other), two[0]))
    mixed_one = mixed_part(after(one, two[0]))
    mix_grad_one = dot(flat.T, mixed_one)
    mix_kept_one, mix_other_one = share_pair(here, mix_grad_one.reshape(shards, own, -1))
    input_part = dot(mixed_one, weight_part(0).T)
    three = backward(2, after(grad_context, down_half, up_half, input_part, mix_kept_one))
    down_half, down_other = column_third(here, *after((down_half, down_other), three[0]))
    up_half, up_other = column_third(here, *after((up_half, up_other), three[0]))
    mixed_two = mixed_part(after(two, three[0]))
    mixed_three = mixed_part(three)
    mixed_rest = jnp.concatenate([mixed_two, mixed_three], axis=1)
    input_grad = grad_sum + input_part + dot(mixed_rest, jnp.concatenate([weight_part(1), weight_part(2)], axis=1).T)
    input_slots = from_sequence_send(here, list(input_grad.astype(bf16).reshape(here.columns, half, width)))
    mix_grad_rest = dot(flat.T, mixed_rest)

    sums = [column_sums(m) for m in (mixed_one, mixed_two, mixed_three)]
    query_grad = jnp.concatenate([s[:part_width] for s in sums])
    value_grad = jnp.concatenate([s[2 * part_width :] for s in sums])
    vectors = (
        query_grad,
        value_grad,
        merge_bias_grad,
        first_gain_grad,
        first_shift_grad,
        down_bias_grad,
        second_gain_grad,
        second_shift_grad,
    )
    columns_grad = jnp.concatenate([jnp.stack(vectors, axis=1), up_bias_grad.reshape(width, -1)], axis=1)
    columns_grad = jnp.pad(columns_grad, ((0, 0), (0, LANES - columns_grad.shape[1])))
    rest = jnp.concatenate([mix_grad_rest, columns_grad], axis=1).reshape(shards, own, -1)
    rest_kept, rest_other = share_pair(here, rest)
    mix_share_one, mix_others_one = share_plane(here, mix_kept_one, mix_other_one)
    rest_share, rest_others = share_plane(here, rest_kept, rest_other)
    mix_share = jnp.concatenate([share_sum(mix_share_one, mix_others_one), share_sum(rest_share, rest_others)], axis=1)
    mix_last = column_last(here, *column_third(here, *column_second(here, *column_first(here, mix_share))))

    output = from_sequence_end(here, after(output_slots, three[0]), groups)
    final_input = from_sequence_end(here, input_slots, groups).astype(f32)
    final_down = column_last(here, down_half, down_other).astype(f32)
    final_up_merge = column_last(here, up_half, up_other).astype(f32)
    final_mix = mix_last[:, : 3 * width].astype(f32).reshape(own, PARTS, 3, H // PARTS, HD)
    final_mix = final_mix.transpose(0, 1, 3, 2, 4).reshape(own, 3 * width)
    final_columns = mix_last[:, 3 * width :].astype(f32)
    finals = final_columns[:, :8].T
    (
        final_query,
        final_value,
        final_merge_bias,
        final_gain_one,
        final_shift_one,
        final_down_bias,
        final_gain_two,
        final_shift_two,
    ) = [finals[j] for j in range(8)]
    final_up_bias = final_columns[:, 8 : 8 + hidden_size // width].reshape(-1)
    return (
        output,
        final_input,
        final_mix,
        final_query,
        final_value,
        final_up_merge[:, hidden_size:],
        final_merge_bias,
        final_gain_one,
        final_shift_one,
        final_up_merge[:, :hidden_size],
        final_up_bias,
        final_down,
        final_down_bias,
        final_gain_two,
        final_shift_two,
    )


def solution(mesh):
    wide, row, thin = P("fsdp", "seq", None), P("fsdp", None), P("fsdp")
    return jax.shard_map(
        per_device,
        mesh=mesh,
        in_specs=(wide, P("fsdp", "seq"), row, thin, thin, row, thin, thin, thin, row, thin, row, thin, thin, thin, wide),
        out_specs=(wide, wide, row, thin, thin, row, thin, thin, thin, row, thin, row, thin, thin, thin),
        check_vma=False,
    )
```

```python
import functools, math
import jax, jax.numpy as jnp
from jax import lax
from jax.experimental import pallas as pl
from jax.experimental.pallas import tpu as pltpu
from jax.sharding import PartitionSpec as P

LANES = 128
FAR = -1000000000.0
IDS = 4
LN2 = math.log(2.0)


def nt(a, b):
    return lax.dot_general(a, b, (((1,), (1,)), ((), ())), preferred_element_type=jnp.float32)


def nn(a, b):
    return lax.dot_general(a, b, (((1,), (0,)), ((), ())), preferred_element_type=jnp.float32)


def lane_of(rows):
    return lax.broadcasted_iota(jnp.int32, (rows, LANES), 1)


def split3(x):
    high = x.astype(jnp.bfloat16).astype(jnp.float32)
    middle = (x - high).astype(jnp.bfloat16).astype(jnp.float32)
    return high, middle, x - high - middle


def gather_blocks(info, block, count, own_ref, mate_ref, put):
    for b in range(count):
        start = pl.multiple_of(((b // 2) ^ info[1]) * block, block)

        @pl.when(info[0] == b % 2)
        def _():
            put(b, own_ref[pl.ds(start, block), :])

        @pl.when(info[0] != b % 2)
        def _():
            put(b, mate_ref[pl.ds(start, block), :])


def forward_kernel(info, q_ref, k_own, k_mate, v_own, v_mate, qx_ref, kx_ref, out_ref, ext_ref, k_all, vt_all, s_all, *, size):
    slot = pl.program_id(1)
    block = q_ref.shape[0]
    count = kx_ref.shape[0] // block
    heads = LANES // size
    lane_head = lane_of(block) // size

    @pl.when(slot == 0)
    def _():
        def put_k(b, rows):
            ext = kx_ref[b * block : (b + 1) * block, :]
            for h in range(heads):
                k_all[h, b * block : (b + 1) * block, :] = jnp.where(lane_head == h, rows, ext)

        def put_v(b, rows):
            turned = rows.T
            for h in range(heads):
                vt_all[h, :size, b * block : (b + 1) * block] = turned[h * size : (h + 1) * size]

        gather_blocks(info, block, count, k_own, k_mate, put_k)
        gather_blocks(info, block, count, v_own, v_mate, put_v)
        for h in range(heads):
            vt_all[h, size:, :] = jnp.ones((vt_all.shape[1] - size, vt_all.shape[2]), vt_all.dtype)

    rows = q_ref[...]
    qx = qx_ref[...]
    queries = [jnp.where(lane_head == h, rows, qx) for h in range(heads)]

    part = block
    lo, hi = info[2 + 2 * slot], info[3 + 2 * slot]

    def score(h, kb, i, top):
        at = pl.multiple_of(kb * block + i * part, part)
        st = nt(k_all[h, pl.ds(at, part), :], queries[h])
        s_all[h, i * part : (i + 1) * part, :] = st
        return jnp.maximum(top, jnp.max(st.reshape(part // 8, 8, block), axis=0))

    def weigh(h, kb, i, m, acc):
        at = pl.multiple_of(kb * block + i * part, part)
        p = jnp.exp2(s_all[h, i * part : (i + 1) * part, :] - m).astype(jnp.bfloat16)
        return acc + nn(vt_all[h, :, pl.ds(at, part)], p)

    least = jnp.full((8, block), -jnp.inf, jnp.float32)

    def step(kb, carry):
        tops, state = carry
        tops, state = list(tops), list(state)
        after = jnp.minimum(kb + 1, count - 1)
        for h in range(heads):
            ahead = (h + 1) % heads
            ahead_kb = kb if ahead else after
            m, acc = state[h]
            m_new = jnp.maximum(m, jnp.max(tops[h], axis=0, keepdims=True))
            acc = acc * jnp.exp2(m - m_new)
            top = least
            for i in range(1):
                top = score(ahead, ahead_kb, i, top)
                acc = weigh(h, kb, i, m_new, acc)
            tops[ahead] = top
            state[h] = (m_new, acc)
        return tuple(tops), tuple(state)

    start = tuple(
        (jnp.full((1, block), -jnp.inf, jnp.float32), jnp.zeros((vt_all.shape[1], block), jnp.float32))
        for _ in range(heads)
    )
    first = score(0, lo, 0, least)
    _, done = lax.fori_loop(lo, hi, step, ((first,) + (least,) * (heads - 1), start))
    sums = [acc[size : size + 1] for _, acc in done]
    out_t = jnp.concatenate([acc[:size] * (1.0 / l) for (_, acc), l in zip(done, sums)], axis=0)
    out_ref[...] = out_t.T.astype(out_ref.dtype)
    row = lax.broadcasted_iota(jnp.int32, (size, block), 0)
    parts = []
    for (m, _), l in zip(done, sums):
        pieces = split3(-(m + jnp.log2(l)))
        part = jnp.zeros((size, block), jnp.float32)
        for j, piece in enumerate(pieces):
            part = jnp.where(row == IDS + j, piece, part)
        parts.append(part)
    ext_ref[...] = (jnp.concatenate(parts[::-1], axis=0).T + qx.astype(jnp.float32)).astype(ext_ref.dtype)


def attention_forward(info, own, mate, qx, kx, size):
    rows, width = own.shape[0], own.shape[1] // 3
    length = kx.shape[0]
    slots = (info.shape[0] - 2) // 2
    block = rows // slots
    pairs = width // LANES
    heads = LANES // size
    return pl.pallas_call(
        functools.partial(forward_kernel, size=size),
        grid_spec=pltpu.PrefetchScalarGridSpec(
            num_scalar_prefetch=1,
            grid=(pairs, slots),
            in_specs=[
                pl.BlockSpec((block, LANES), lambda p, s, i: (s, p)),
                pl.BlockSpec((rows, LANES), lambda p, s, i: (0, pairs + p)),
                pl.BlockSpec((rows, LANES), lambda p, s, i: (0, pairs + p)),
                pl.BlockSpec((rows, LANES), lambda p, s, i: (0, 2 * pairs + p)),
                pl.BlockSpec((rows, LANES), lambda p, s, i: (0, 2 * pairs + p)),
                pl.BlockSpec((block, LANES), lambda p, s, i: (s, 0)),
                pl.BlockSpec((length, LANES), lambda p, s, i: (0, 0)),
            ],
            out_specs=[pl.BlockSpec((block, LANES), lambda p, s, i: (s, p))] * 2,
            scratch_shapes=[
                pltpu.VMEM((heads, length, LANES), jnp.bfloat16),
                pltpu.VMEM((heads, size + 16, length), jnp.bfloat16),
                pltpu.VMEM((heads, block, block), jnp.float32),
            ],
        ),
        out_shape=[jax.ShapeDtypeStruct((rows, width), jnp.bfloat16)] * 2,
        compiler_params=pltpu.CompilerParams(dimension_semantics=("arbitrary", "arbitrary")),
        cost_estimate=pl.CostEstimate(
            flops=2 * rows * length * width, bytes_accessed=8 * rows * width * 2, transcendentals=rows * length * pairs
        ),
        name="attention_forward",
    )(info, own, own, mate, own, mate, qx, kx)


def backward_kernel(
    info, q_ref, ext_ref, do_ref, ctx_ref, k_own, k_mate, v_own, v_mate, kx_ref,
    dq_ref, own_ref, mate_ref, k_all, kt_all, v_all, dk_all, dv_all, *, size
):
    slot = pl.program_id(1)
    block = q_ref.shape[0]
    count = kx_ref.shape[0] // block
    heads = LANES // size
    lane = lane_of(block)
    lane_head = lane // size
    place = lane % size
    three = (place >= IDS) & (place < IDS + 3)

    @pl.when(slot == 0)
    def _():
        def put_k(b, rows):
            ext = kx_ref[b * block : (b + 1) * block, :]
            for h in range(heads):
                k_all[h, b * block : (b + 1) * block, :] = jnp.where(lane_head == h, rows, ext)
            kt_all[:, b * block : (b + 1) * block] = rows.T

        def put_v(b, rows):
            one = three.astype(rows.dtype)
            for h in range(heads):
                v_all[h, b * block : (b + 1) * block, :] = jnp.where(lane_head == h, rows, one)

        gather_blocks(info, block, count, k_own, k_mate, put_k)
        gather_blocks(info, block, count, v_own, v_mate, put_v)
        dk_all[...] = jnp.zeros_like(dk_all)
        dv_all[...] = jnp.zeros_like(dv_all)

    rows = q_ref[...]
    ext = ext_ref[...]
    grads = do_ref[...]
    zero = jnp.zeros_like(rows)
    queries = [jnp.where(lane_head == h, rows, ext) for h in range(heads)]
    plain_q = jnp.concatenate([jnp.where(lane_head == h, rows, zero) for h in range(heads)], axis=0)
    plain_do = jnp.concatenate([jnp.where(lane_head == h, grads, zero) for h in range(heads)], axis=0)
    product = grads.astype(jnp.float32) * ctx_ref[...].astype(jnp.float32)
    outs = []
    for h in range(heads):
        delta = jnp.sum(jnp.where(lane_head == h, product, 0.0), axis=1, keepdims=True)
        wide = jnp.zeros((block, LANES), jnp.float32)
        for j, piece in enumerate(split3(-delta)):
            wide = jnp.where(place == IDS + j, piece, wide)
        outs.append(jnp.where(lane_head == h, grads, wide.astype(grads.dtype)))

    def step(kb, carry):
        start = pl.multiple_of(kb * block, block)
        probs, scores, fresh = [], [], []
        for h in range(heads):
            p = jnp.exp2(nt(k_all[h, pl.ds(start, block), :], queries[h]))
            ds = (p * nt(v_all[h, pl.ds(start, block), :], outs[h])).astype(jnp.bfloat16)
            probs.append(p.astype(jnp.bfloat16))
            scores.append(ds)
            fresh.append(carry[h] + nn(kt_all[h * size : (h + 1) * size, pl.ds(start, block)], ds))
        dv_all[pl.ds(start, block), :] += nn(jnp.concatenate(probs, axis=1), plain_do)
        dk_all[pl.ds(start, block), :] += nn(jnp.concatenate(scores, axis=1), plain_q)
        return tuple(fresh)

    dq = lax.fori_loop(
        info[2 + 2 * slot], info[3 + 2 * slot], step,
        tuple(jnp.zeros((size, block), jnp.float32) for _ in range(heads)),
    )
    dq_ref[...] = (jnp.concatenate(dq, axis=0) * (1.0 / math.sqrt(size))).T.astype(dq_ref.dtype)

    @pl.when(slot == pl.num_programs(1) - 1)
    def _():
        for b in range(count):
            spot = pl.multiple_of(((b // 2) ^ info[1]) * block, block)
            for j, (total, factor) in enumerate(((dk_all, LN2), (dv_all, 1.0))):

                @pl.when(info[0] == b % 2)
                def _():
                    own_ref[j, pl.ds(spot, block), :] = (total[pl.ds(b * block, block), :] * factor).astype(own_ref.dtype)

                @pl.when(info[0] != b % 2)
                def _():
                    mate_ref[j, pl.ds(spot, block), :] = (total[pl.ds(b * block, block), :] * factor).astype(mate_ref.dtype)


def attention_backward(info, own, mate, ext, grads, ctx, kx, size, first):
    rows, width = ctx.shape
    length = kx.shape[0]
    slots = (info.shape[0] - 2) // 2
    block = rows // slots
    pairs = width // LANES
    heads = LANES // size
    tile = pl.BlockSpec((block, LANES), lambda p, s, i: (s, p))
    return pl.pallas_call(
        functools.partial(backward_kernel, size=size),
        grid_spec=pltpu.PrefetchScalarGridSpec(
            num_scalar_prefetch=1,
            grid=(pairs, slots),
            in_specs=[
                tile,
                tile,
                pl.BlockSpec((block, LANES), lambda p, s, i: (s, first + p)),
                tile,
                pl.BlockSpec((rows, LANES), lambda p, s, i: (0, pairs + p)),
                pl.BlockSpec((rows, LANES), lambda p, s, i: (0, pairs + p)),
                pl.BlockSpec((rows, LANES), lambda p, s, i: (0, 2 * pairs + p)),
                pl.BlockSpec((rows, LANES), lambda p, s, i: (0, 2 * pairs + p)),
                pl.BlockSpec((length, LANES), lambda p, s, i: (0, 0)),
            ],
            out_specs=[
                tile,
                pl.BlockSpec((2, rows, LANES), lambda p, s, i: (0, 0, p)),
                pl.BlockSpec((2, rows, LANES), lambda p, s, i: (0, 0, p)),
            ],
            scratch_shapes=[
                pltpu.VMEM((heads, length, LANES), jnp.bfloat16),
                pltpu.VMEM((LANES, length), jnp.bfloat16),
                pltpu.VMEM((heads, length, LANES), jnp.bfloat16),
                pltpu.VMEM((length, LANES), jnp.float32),
                pltpu.VMEM((length, LANES), jnp.float32),
            ],
        ),
        out_shape=[
            jax.ShapeDtypeStruct((rows, width), jnp.bfloat16),
            jax.ShapeDtypeStruct((2, rows, width), jnp.float32),
            jax.ShapeDtypeStruct((2, rows, width), jnp.bfloat16),
        ],
        compiler_params=pltpu.CompilerParams(dimension_semantics=("arbitrary", "arbitrary")),
        cost_estimate=pl.CostEstimate(
            flops=5 * rows * length * width, bytes_accessed=24 * rows * width, transcendentals=rows * length * pairs
        ),
        name="attention_backward",
    )(info, own, ext, grads, ctx, own, mate, own, mate, kx)


def key_extension(ids):
    place = jnp.arange(LANES) % (LANES // 2)
    hot = ids[:, None] == place[None, :]
    return (hot | ((place >= IDS) & (place < IDS + 3))[None, :]).astype(jnp.bfloat16)


def query_extension(ids):
    place = jnp.arange(LANES) % (LANES // 2)
    other = (place < IDS)[None, :] & (ids[:, None] != place[None, :])
    return jnp.where(other, FAR, 0.0).astype(jnp.bfloat16)


H = 12
HD = 64
LOG2E = 1.0 / LN2
PARTS = 3
eps_norm = 1e-06
bf16 = jnp.bfloat16
f32 = jnp.float32


def norm_forward(total, gain, shift):
    middle = jnp.mean(total, axis=-1, keepdims=True)
    centred = total - middle
    factor = lax.rsqrt(jnp.mean(centred * centred, axis=-1, keepdims=True) + eps_norm)
    normed = centred * factor
    return (normed * gain + shift, normed, factor)


def norm_backward(grad_out, normed, factor, gain):
    scaled = grad_out * gain
    inner = (
        scaled
        - jnp.mean(scaled, axis=-1, keepdims=True)
        - normed * jnp.mean(scaled * normed, axis=-1, keepdims=True)
    )
    return (factor * inner, jnp.sum(grad_out * normed, axis=0), jnp.sum(grad_out, axis=0))


def gelu_parts(hidden):
    normal_cdf = 0.5 * (1.0 + jax.scipy.special.erf(hidden * (1.0 / math.sqrt(2.0))))
    density = jnp.exp(-0.5 * hidden * hidden) * (1.0 / math.sqrt(2.0 * math.pi))
    return (hidden * normal_cdf, normal_cdf + hidden * density)


def dot(a, b):
    return jnp.dot(a, b, preferred_element_type=f32)


def column_sums(values):
    return jnp.sum(values.astype(f32), axis=0)


def xor_pairs(size, bits):
    return [(i, i ^ bits) for i in range(size)]


def pick(values, index, axis=0):
    return lax.dynamic_index_in_dim(values, index, axis, keepdims=False)


def after(values, *marks):
    return lax.optimization_barrier((values, marks))[0]


class Places:
    def __init__(self):
        self.columns = lax.axis_size("seq")
        self.shards = lax.axis_size("fsdp")
        self.column = lax.axis_index("seq")
        self.shard = lax.axis_index("fsdp")
        self.core = self.shard & 1
        self.plane = self.shard >> 1

    def mate(self, values):
        return lax.ppermute(values, "fsdp", xor_pairs(self.shards, 1))

    def across(self, values, bits):
        return lax.ppermute(values, "seq", xor_pairs(self.columns, bits))

    def aside(self, values, bits):
        return lax.ppermute(values, "fsdp", xor_pairs(self.shards, 2 * bits))


def to_sequence_parts(here, values):
    groups, piece, width = values.shape
    halves = values.reshape(groups, 2, piece // 2, width)
    kept = pick(halves, here.core, 1)
    other = here.mate(pick(halves, 1 - here.core, 1))
    parts = []
    for k in range(here.columns):
        want = here.column ^ k
        same = lax.div(want, groups) == here.core
        spot = lax.rem(want, groups)
        parts.append(jnp.where(same, pick(kept, spot), pick(other, spot)))
    return parts


def from_sequence_send(here, slots):
    return [here.across(slots[k], k) if k else slots[k] for k in range(here.columns)]


def from_sequence_end(here, slots, groups):
    rows = jnp.stack(slots)

    def of(core):
        return jnp.stack([pick(rows, here.column ^ (core * groups + j)) for j in range(groups)])

    kept = of(here.core)
    other = here.mate(of(1 - here.core))
    first = here.core == 0
    return jnp.concatenate([jnp.where(first, kept, other), jnp.where(first, other, kept)], axis=1)


def place_kernel(info, *refs, count, cuts, outs):
    parts, full, buffers = refs[:count], refs[count : count + outs], refs[count + outs : 2 * count + outs]
    in_sem, out_sem = refs[2 * count + outs :]
    reads = [pltpu.make_async_copy(parts[k], buffers[k], in_sem.at[k]) for k in range(count)]
    for read in reads:
        read.start()
    writes = []
    for k in range(count):
        reads[k].wait()
        for j, (row, rows, col, cols, out, out_col) in enumerate(cuts):
            write = pltpu.make_async_copy(
                buffers[k].at[pl.ds(row, rows), pl.ds(col, cols)],
                full[out].at[info[k], :, pl.ds(out_col, cols)],
                out_sem.at[k, j],
            )
            write.start()
            writes.append(write)
    for write in writes:
        write.wait()


def out_shapes(cuts):
    shapes = {}
    for row, rows, col, cols, out, out_col in cuts:
        shapes[out] = (rows, max(shapes.get(out, (0, 0))[1], out_col + cols))
    return [shapes[out] for out in sorted(shapes)]


def place(parts, spots, cuts):
    count, (rows, width), kind = len(parts), parts[0].shape, parts[0].dtype
    shapes = out_shapes(cuts)
    return pl.pallas_call(
        functools.partial(place_kernel, count=count, cuts=cuts, outs=len(shapes)),
        grid_spec=pltpu.PrefetchScalarGridSpec(
            num_scalar_prefetch=1,
            grid=(),
            in_specs=[pl.BlockSpec(memory_space=pl.ANY)] * count,
            out_specs=[pl.BlockSpec(memory_space=pl.ANY)] * len(shapes),
            scratch_shapes=[pltpu.VMEM((rows, width), kind)] * count
            + [pltpu.SemaphoreType.DMA((count,)), pltpu.SemaphoreType.DMA((count, len(cuts)))],
        ),
        out_shape=[jax.ShapeDtypeStruct((count,) + shape, kind) for shape in shapes],
        cost_estimate=pl.CostEstimate(flops=0, bytes_accessed=2 * count * rows * width * 2, transcendentals=0),
        name="place_parts",
    )(jnp.stack(spots).astype(jnp.int32), *parts)


class Gather:
    def __init__(self, here, local, cuts):
        self.here, self.local, self.cuts = here, local, cuts
        self.direct = here.shards == 8
        if self.direct:
            self.parts = [local, here.aside(local, 1), here.aside(local, 2)]
        else:
            self.full = lax.all_gather(local, "fsdp", axis=0, tiled=False)

    def corner(self, *marks):
        if self.direct:
            here = self.here
            middle = self.local.shape[0] // 32 * 16
            _, across_x, across_y = self.parts = after(self.parts, *marks)
            self.mates = [here.mate(part) for part in self.parts]
            self.last = [here.aside(across_x[:middle], 2), here.aside(across_y[middle:], 1)]

    def finish(self, *marks):
        here = self.here
        if not self.direct:
            shapes = out_shapes(self.cuts)
            full = [[] for _ in shapes]
            for row, rows, col, cols, out, out_col in self.cuts:
                full[out].append(self.full[:, row : row + rows, col : col + cols])
            whole = [jnp.concatenate(pieces, axis=2) for pieces in full]
        else:
            corner = jnp.concatenate(after(self.last, *marks), axis=0)
            spots = [here.shard ^ (2 * k) for k in range(4)]
            mates = self.mates + [here.mate(corner)]
            whole = place(self.parts + [corner] + mates, spots + [spot ^ 1 for spot in spots], self.cuts)
        return [w.reshape(-1, w.shape[2]) for w in whole]


def share_pair(here, partial):
    shards, rows, width = partial.shape
    pairs = partial.reshape(shards // 2, 2, rows, width)
    return pick(pairs, here.core, 1), here.mate(pick(pairs, 1 - here.core, 1).astype(bf16))


def share_plane(here, kept, other):
    def total(k):
        spot = here.plane ^ k
        return pick(kept, spot).astype(f32) + pick(other, spot).astype(f32)

    return total(0), [here.aside(total(k).astype(bf16), k) for k in range(1, here.shards // 2)]


def share_sum(share, others):
    for other in others:
        share = share + other.astype(f32)
    return share.astype(bf16)


def column_first(here, share):
    low = share.reshape(2, share.shape[0] // 2, share.shape[1])
    side = here.column & 1
    return pick(low, side), here.across(pick(low, 1 - side), 1)


def column_second(here, half, other):
    low = (half.astype(f32) + other.astype(f32)).astype(bf16)
    step, others = 2, []
    while 2 * step < here.columns:
        low = (low.astype(f32) + here.across(low, step).astype(f32)).astype(bf16)
        step *= 2
    return low, here.across(low, step)


def column_third(here, half, other):
    half = (half.astype(f32) + other.astype(f32)).astype(bf16)
    return half, here.across(half, 1)


def column_last(here, half, other):
    first = (here.column & 1) == 0
    return jnp.concatenate([jnp.where(first, half, other), jnp.where(first, other, half)], axis=0)


def per_device(
    tokens,
    segment_ids,
    mix_weight,
    query_bias,
    value_bias,
    merge_weight,
    merge_bias,
    first_gain,
    first_shift,
    up_weight,
    up_bias,
    down_weight,
    down_bias,
    second_gain,
    second_shift,
    output_grad,
):
    here = Places()
    groups, piece, width = tokens.shape
    shards = here.shards
    own = width // shards
    hidden_size = up_weight.shape[1]
    half = piece // 2
    rows = here.columns * half
    length = here.columns * piece

    def sequence(values):
        return from_sequence_send(here, to_sequence_parts(here, values))

    ups = hidden_size // width
    part_width = width // PARTS
    token_parts = to_sequence_parts(here, tokens)
    flat = jnp.concatenate(from_sequence_send(here, token_parts), axis=0)

    vectors = (query_bias, value_bias, merge_bias, first_gain, first_shift, down_bias, second_gain, second_shift)
    lines = jnp.concatenate([jnp.stack(vectors), up_bias.reshape(ups, own)], axis=0)
    columns = jnp.pad(lines, ((0, LANES - lines.shape[0]), (0, 0))).T
    mix_local = mix_weight.reshape(own, PARTS, H // PARTS, 3, HD).transpose(0, 1, 3, 2, 4).reshape(own, 3 * width)
    mix_local = jnp.concatenate([mix_local, columns], axis=1)
    mix_cuts = [(0, own, p * width, width, p, 0) for p in range(PARTS)] + [(0, own, 3 * width, LANES, PARTS, 0)]
    mix_gather = Gather(here, after(mix_local, token_parts), mix_cuts)
    mix_gather.corner()
    *mix_parts, columns_full = mix_gather.finish()
    lines_full = columns_full.T.astype(f32)
    query_full, value_full, merge_bias_full, gain_one, shift_one, down_bias_full, gain_two, shift_two = [
        lines_full[j] for j in range(8)
    ]
    up_bias_full = lines_full[8 : 8 + ups].reshape(ups, shards, own).transpose(1, 0, 2).reshape(-1)

    ids_local = after(segment_ids, token_parts).reshape(groups, piece, 1)
    ids_own = jnp.concatenate(sequence(ids_local), axis=0).reshape(here.columns, half)
    ids_mate = here.mate(ids_own)
    by_core = jnp.stack([jnp.where(here.core == 0, ids_own, ids_mate), jnp.where(here.core == 0, ids_mate, ids_own)], axis=1)
    ids = jnp.stack([pick(by_core, k ^ here.column) for k in range(here.columns)]).reshape(2 * here.columns, half)
    first_id, last_id = ids[:, 0], ids[:, -1]
    low = jnp.sum(last_id[None, :] < ids_own[:, :1], axis=1)
    high = jnp.sum(first_id[None, :] <= ids_own[:, -1:], axis=1)
    info = jnp.concatenate([jnp.stack([here.core, here.column]), jnp.stack([low, high], axis=1).reshape(-1)]).astype(jnp.int32)
    key_ext = key_extension(ids.reshape(length))
    query_ext = query_extension(ids_own.reshape(rows))

    packed = jnp.concatenate(
        [merge_weight] + [up_weight[:, j * width : (j + 1) * width] for j in range(ups)] + [down_weight], axis=0
    )
    cuts = [(0, own, 0, width, 0, 0)] + [((1 + j) * own, own, 0, width, 1, j * width) for j in range(ups)]
    cuts.append(((1 + ups) * own, ups * own, 0, width, 2, 0))
    weight_gather = Gather(here, after(packed, flat), cuts)
    cotangent_slots = sequence(after(output_grad, flat))

    column_scale = jnp.where(jnp.arange(width) < part_width, LOG2E / math.sqrt(HD), 1.0)
    mixed, mixed_mate = [], []
    for p in range(PARTS):
        of_part = slice(p * part_width, (p + 1) * part_width)
        bias = jnp.concatenate([query_full[of_part], jnp.zeros((part_width,), f32), value_full[of_part]])
        mixed.append(((dot(flat, mix_parts[p]) + bias) * column_scale).astype(bf16))
        mixed_mate.append(here.mate(mixed[p]))

    contexts, exts = [], []
    for p in range(PARTS):
        if p:
            mixed[p], mixed_mate[p] = after((mixed[p], mixed_mate[p]), contexts[-1])
        if p == 1:
            weight_gather.corner(contexts[-1])
        context, ext = attention_forward(info, mixed[p], mixed_mate[p], query_ext, key_ext, HD)
        contexts.append(context)
        exts.append(ext)
    context = jnp.concatenate(contexts, axis=1)

    cotangent = jnp.concatenate(after(cotangent_slots, contexts[-1]), axis=0).astype(f32)
    merge_full, up_full, down_full = weight_gather.finish(contexts[-2])
    merge_full, up_full, down_full = after((merge_full, up_full, down_full), contexts[-1])

    attended = dot(context, merge_full) + merge_bias_full
    first_out, normed_one, factor_one = norm_forward(flat.astype(f32) + attended, gain_one, shift_one)
    first_low = first_out.astype(bf16)
    hidden = dot(first_low, up_full) + up_bias_full
    active, slope = gelu_parts(hidden)
    active_low = active.astype(bf16)
    branch = dot(active_low, down_full) + down_bias_full
    result, normed_two, factor_two = norm_forward(first_out + branch, gain_two, shift_two)
    output_slots = from_sequence_send(here, list(result.astype(bf16).reshape(here.columns, half, width)))

    grad_second, second_gain_grad, second_shift_grad = norm_backward(cotangent, normed_two, factor_two, gain_two)
    grad_branch = grad_second.astype(bf16)
    down_grad = dot(active_low.T, grad_branch)
    down_kept, down_other = share_pair(here, down_grad.reshape(shards, -1, width))
    down_bias_grad = column_sums(grad_branch)
    grad_active = dot(grad_branch, down_full.T)
    grad_hidden = (grad_active * slope).astype(bf16)
    down_share, down_others = share_plane(here, down_kept, after(down_other, grad_hidden))
    up_grad = dot(first_low.T, grad_hidden)
    up_bias_grad = column_sums(grad_hidden)
    grad_first = grad_second + dot(grad_hidden, up_full.T)
    grad_sum, first_gain_grad, first_shift_grad = norm_backward(grad_first, normed_one, factor_one, gain_one)
    grad_attended = grad_sum.astype(bf16)
    merge_grad = dot(context.T, grad_attended)
    merge_bias_grad = column_sums(grad_attended)
    up_merge = jnp.concatenate([up_grad.reshape(shards, own, hidden_size), merge_grad.reshape(shards, own, width)], axis=2)
    up_kept, up_other = share_pair(here, up_merge)
    grad_context = dot(grad_attended, merge_full.T).astype(bf16)
    up_share, up_others = share_plane(here, up_kept, after(up_other, grad_context))

    def backward(part, grads):
        dq, kept, other = attention_backward(
            info, mixed[part], mixed_mate[part], exts[part], grads, contexts[part], key_ext, HD, part * part_width // LANES
        )
        return dq, kept, here.mate(other)

    def mixed_part(pieces):
        dq, kept, other = pieces
        kv = (kept + other.astype(f32)).astype(bf16)
        return jnp.concatenate([dq, kv[0], kv[1]], axis=1)

    one = backward(0, after(grad_context, down_share, up_share))
    down_others, down_share = after((down_others, down_share), one[0])
    down_half, down_other = column_first(here, share_sum(down_share, down_others))
    up_others, up_share = after((up_others, up_share), one[0])
    up_half, up_other = column_first(here, share_sum(up_share, up_others))
    two = backward(1, after(grad_context, down_half, up_half))
    down_half, down_other = column_second(here, *after((down_half, down_other), two[0]))
    up_half, up_other = column_second(here, *after((up_half, up_other), two[0]))
    mixed_one = mixed_part(after(one, two[0]))
    mix_grad_one = dot(flat.T, mixed_one)
    mix_kept_one, mix_other_one = share_pair(here, mix_grad_one.reshape(shards, own, -1))
    input_part = grad_sum + dot(mixed_one, mix_parts[0].T)
    mix_share_one, mix_others_one = share_plane(here, mix_kept_one, after(mix_other_one, input_part))
    three = backward(2, after(grad_context, down_half, up_half, mix_share_one))
    down_half, down_other = column_third(here, *after((down_half, down_other), three[0]))
    up_half, up_other = column_third(here, *after((up_half, up_other), three[0]))
    mixed_two = mixed_part(after(two, three[0]))
    input_part = input_part + dot(mixed_two, mix_parts[1].T)
    mixed_three = mixed_part(after(three, input_part))
    input_low = (input_part + dot(mixed_three, mix_parts[2].T)).astype(bf16)
    input_slots = from_sequence_send(here, list(input_low.reshape(here.columns, half, width)))
    mixed_rest = after(jnp.concatenate([mixed_two, mixed_three], axis=1), input_low)
    mix_grad_rest = dot(flat.T, mixed_rest)

    sums = [column_sums(m) for m in (mixed_one, mixed_two, mixed_three)]
    query_grad = jnp.concatenate([s[:part_width] for s in sums])
    value_grad = jnp.concatenate([s[2 * part_width :] for s in sums])
    vectors = (
        query_grad,
        value_grad,
        merge_bias_grad,
        first_gain_grad,
        first_shift_grad,
        down_bias_grad,
        second_gain_grad,
        second_shift_grad,
    )
    up_lines = up_bias_grad.reshape(shards, ups, own).transpose(1, 0, 2).reshape(ups, width)
    lines_grad = jnp.concatenate([jnp.stack(vectors), up_lines], axis=0)
    columns_grad = jnp.pad(lines_grad, ((0, LANES - lines_grad.shape[0]), (0, 0))).T
    rest = jnp.concatenate([mix_grad_rest, columns_grad], axis=1).reshape(shards, own, -1)
    rest_kept, rest_other = share_pair(here, rest)
    rest_share, rest_others = share_plane(here, rest_kept, rest_other)
    mix_share = jnp.concatenate([share_sum(mix_share_one, mix_others_one), share_sum(rest_share, rest_others)], axis=1)
    mix_last = column_last(here, *column_third(here, *column_second(here, *column_first(here, mix_share))))

    output = from_sequence_end(here, after(output_slots, three[0]), groups)
    final_input = from_sequence_end(here, input_slots, groups).astype(f32)
    final_down = column_last(here, down_half, down_other).astype(f32)
    final_up_merge = column_last(here, up_half, up_other).astype(f32)
    final_mix = mix_last[:, : 3 * width].astype(f32).reshape(own, PARTS, 3, H // PARTS, HD)
    final_mix = final_mix.transpose(0, 1, 3, 2, 4).reshape(own, 3 * width)
    final_columns = mix_last[:, 3 * width :].astype(f32)
    finals = final_columns.T
    (
        final_query,
        final_value,
        final_merge_bias,
        final_gain_one,
        final_shift_one,
        final_down_bias,
        final_gain_two,
        final_shift_two,
    ) = [finals[j] for j in range(8)]
    final_up_bias = finals[8 : 8 + ups].reshape(-1)
    return (
        output,
        final_input,
        final_mix,
        final_query,
        final_value,
        final_up_merge[:, hidden_size:],
        final_merge_bias,
        final_gain_one,
        final_shift_one,
        final_up_merge[:, :hidden_size],
        final_up_bias,
        final_down,
        final_down_bias,
        final_gain_two,
        final_shift_two,
    )


def solution(mesh):
    wide, row, thin = P("fsdp", "seq", None), P("fsdp", None), P("fsdp")
    return jax.shard_map(
        per_device,
        mesh=mesh,
        in_specs=(wide, P("fsdp", "seq"), row, thin, thin, row, thin, thin, thin, row, thin, row, thin, thin, thin, wide),
        out_specs=(wide, wide, row, thin, thin, row, thin, thin, thin, row, thin, row, thin, thin, thin),
        check_vma=False,
    )
```

```python
import functools, math
import jax, jax.numpy as jnp
from jax import lax
from jax.experimental import pallas as pl
from jax.experimental.layout import Layout, with_layout_constraint
from jax.experimental.pallas import tpu as pltpu
from jax.sharding import PartitionSpec as P

LANES = 128
FAR = -1000000000.0
IDS = 4
LN2 = math.log(2.0)


def nt(a, b):
    return lax.dot_general(a, b, (((1,), (1,)), ((), ())), preferred_element_type=jnp.float32)


def nn(a, b):
    return lax.dot_general(a, b, (((1,), (0,)), ((), ())), preferred_element_type=jnp.float32)


def lane_of(rows):
    return lax.broadcasted_iota(jnp.int32, (rows, LANES), 1)


def split3(x):
    high = x.astype(jnp.bfloat16).astype(jnp.float32)
    middle = (x - high).astype(jnp.bfloat16).astype(jnp.float32)
    return high, middle, x - high - middle


def gather_blocks(info, block, count, own_ref, mate_ref, put):
    for b in range(count):
        start = pl.multiple_of(((b // 2) ^ info[1]) * block, block)

        @pl.when(info[0] == b % 2)
        def _():
            put(b, own_ref[pl.ds(start, block), :])

        @pl.when(info[0] != b % 2)
        def _():
            put(b, mate_ref[pl.ds(start, block), :])


def forward_kernel(info, q_ref, k_own, k_mate, v_own, v_mate, qx_ref, kx_ref, *refs, size, plan):
    pieces, moves, outs = plan
    count = len(pieces)
    beside, (out_ref, ext_ref), full = refs[:count], refs[count : count + 2], refs[count + 2 : count + 2 + len(outs)]
    k_all, vt_all, s_all, *sems = refs[count + 2 + len(outs) :]
    slot = pl.program_id(1)
    if count:
        copies = [
            pltpu.make_async_copy(beside[j], full[out].at[info[info.shape[0] - count + j]], sems[0].at[j])
            for j, out in enumerate(moves)
        ]

        @pl.when((pl.program_id(0) == 0) & (slot == 0))
        def _():
            for copy in copies:
                copy.start()

        @pl.when((pl.program_id(0) == pl.num_programs(0) - 1) & (slot == pl.num_programs(1) - 1))
        def _():
            for copy in copies:
                copy.wait()

    block = q_ref.shape[0]
    count = kx_ref.shape[0] // block
    heads = LANES // size
    lane_head = lane_of(block) // size

    @pl.when(slot == 0)
    def _():
        def put_k(b, rows):
            ext = kx_ref[b * block : (b + 1) * block, :]
            for h in range(heads):
                k_all[h, b * block : (b + 1) * block, :] = jnp.where(lane_head == h, rows, ext)

        def put_v(b, rows):
            turned = rows.T
            for h in range(heads):
                vt_all[h, :size, b * block : (b + 1) * block] = turned[h * size : (h + 1) * size]

        gather_blocks(info, block, count, k_own, k_mate, put_k)
        gather_blocks(info, block, count, v_own, v_mate, put_v)
        for h in range(heads):
            vt_all[h, size:, :] = jnp.ones((vt_all.shape[1] - size, vt_all.shape[2]), vt_all.dtype)

    rows = q_ref[...]
    qx = qx_ref[...]
    queries = [jnp.where(lane_head == h, rows, qx) for h in range(heads)]

    part = block
    lo, hi = info[2 + 2 * slot], info[3 + 2 * slot]

    def score(h, kb, i, top):
        at = pl.multiple_of(kb * block + i * part, part)
        st = nt(k_all[h, pl.ds(at, part), :], queries[h])
        s_all[h, i * part : (i + 1) * part, :] = st
        return jnp.maximum(top, jnp.max(st.reshape(part // 8, 8, block), axis=0))

    def weigh(h, kb, i, m, acc):
        at = pl.multiple_of(kb * block + i * part, part)
        p = jnp.exp2(s_all[h, i * part : (i + 1) * part, :] - m).astype(jnp.bfloat16)
        return acc + nn(vt_all[h, :, pl.ds(at, part)], p)

    least = jnp.full((8, block), -jnp.inf, jnp.float32)

    def step(kb, carry):
        tops, state = carry
        tops, state = list(tops), list(state)
        after = jnp.minimum(kb + 1, count - 1)
        for h in range(heads):
            ahead = (h + 1) % heads
            ahead_kb = kb if ahead else after
            m, acc = state[h]
            m_new = jnp.maximum(m, jnp.max(tops[h], axis=0, keepdims=True))
            acc = acc * jnp.exp2(m - m_new)
            top = least
            for i in range(1):
                top = score(ahead, ahead_kb, i, top)
                acc = weigh(h, kb, i, m_new, acc)
            tops[ahead] = top
            state[h] = (m_new, acc)
        return tuple(tops), tuple(state)

    start = tuple(
        (jnp.full((1, block), -jnp.inf, jnp.float32), jnp.zeros((vt_all.shape[1], block), jnp.float32))
        for _ in range(heads)
    )
    first = score(0, lo, 0, least)
    _, done = lax.fori_loop(lo, hi, step, ((first,) + (least,) * (heads - 1), start))
    sums = [acc[size : size + 1] for _, acc in done]
    out_t = jnp.concatenate([acc[:size] * (1.0 / l) for (_, acc), l in zip(done, sums)], axis=0)
    out_ref[...] = out_t.T.astype(out_ref.dtype)
    row = lax.broadcasted_iota(jnp.int32, (size, block), 0)
    parts = []
    for (m, _), l in zip(done, sums):
        pieces = split3(-(m + jnp.log2(l)))
        part = jnp.zeros((size, block), jnp.float32)
        for j, piece in enumerate(pieces):
            part = jnp.where(row == IDS + j, piece, part)
        parts.append(part)
    ext_ref[...] = (jnp.concatenate(parts[::-1], axis=0).T + qx.astype(jnp.float32)).astype(ext_ref.dtype)


NOTHING = ((), (), ())


def attention_forward(info, own, mate, qx, kx, size, plan=NOTHING, spots=()):
    rows, width = own.shape[0], own.shape[1] // 3
    length = kx.shape[0]
    slots = (info.shape[0] - 2) // 2
    block = rows // slots
    pairs = width // LANES
    heads = LANES // size
    pieces, moves, outs = plan
    if pieces:
        info = jnp.concatenate([info, jnp.stack(spots).astype(jnp.int32)])
    anywhere = pl.BlockSpec(memory_space=pl.ANY)
    return pl.pallas_call(
        functools.partial(forward_kernel, size=size, plan=(moves, moves, outs)),
        grid_spec=pltpu.PrefetchScalarGridSpec(
            num_scalar_prefetch=1,
            grid=(pairs, slots),
            in_specs=[
                pl.BlockSpec((block, LANES), lambda p, s, i: (s, p)),
                pl.BlockSpec((rows, LANES), lambda p, s, i: (0, pairs + p)),
                pl.BlockSpec((rows, LANES), lambda p, s, i: (0, pairs + p)),
                pl.BlockSpec((rows, LANES), lambda p, s, i: (0, 2 * pairs + p)),
                pl.BlockSpec((rows, LANES), lambda p, s, i: (0, 2 * pairs + p)),
                pl.BlockSpec((block, LANES), lambda p, s, i: (s, 0)),
                pl.BlockSpec((length, LANES), lambda p, s, i: (0, 0)),
            ]
            + [anywhere] * len(pieces),
            out_specs=[pl.BlockSpec((block, LANES), lambda p, s, i: (s, p))] * 2 + [anywhere] * len(outs),
            scratch_shapes=[
                pltpu.VMEM((heads, length, LANES), jnp.bfloat16),
                pltpu.VMEM((heads, size + 16, length), jnp.bfloat16),
                pltpu.VMEM((heads, block, block), jnp.float32),
            ]
            + [pltpu.SemaphoreType.DMA((len(pieces),))] * bool(pieces),
        ),
        out_shape=[jax.ShapeDtypeStruct((rows, width), jnp.bfloat16)] * 2
        + [jax.ShapeDtypeStruct(shape, jnp.bfloat16) for shape in outs],
        compiler_params=pltpu.CompilerParams(dimension_semantics=("arbitrary", "arbitrary")),
        cost_estimate=pl.CostEstimate(
            flops=2 * rows * length * width, bytes_accessed=8 * rows * width * 2, transcendentals=rows * length * pairs
        ),
        name="attention_forward",
    )(info, own, own, mate, own, mate, qx, kx, *pieces)


def backward_kernel(
    info, q_ref, ext_ref, do_ref, ctx_ref, k_own, k_mate, v_own, v_mate, kx_ref,
    dq_ref, own_ref, mate_ref, k_all, kt_all, v_all, dk_all, dv_all, *, size
):
    slot = pl.program_id(1)
    block = q_ref.shape[0]
    count = kx_ref.shape[0] // block
    heads = LANES // size
    lane = lane_of(block)
    lane_head = lane // size
    place = lane % size
    three = (place >= IDS) & (place < IDS + 3)

    @pl.when(slot == 0)
    def _():
        def put_k(b, rows):
            ext = kx_ref[b * block : (b + 1) * block, :]
            for h in range(heads):
                k_all[h, b * block : (b + 1) * block, :] = jnp.where(lane_head == h, rows, ext)
            kt_all[:, b * block : (b + 1) * block] = rows.T

        def put_v(b, rows):
            one = three.astype(rows.dtype)
            for h in range(heads):
                v_all[h, b * block : (b + 1) * block, :] = jnp.where(lane_head == h, rows, one)

        gather_blocks(info, block, count, k_own, k_mate, put_k)
        gather_blocks(info, block, count, v_own, v_mate, put_v)
        dk_all[...] = jnp.zeros_like(dk_all)
        dv_all[...] = jnp.zeros_like(dv_all)

    rows = q_ref[...]
    ext = ext_ref[...]
    grads = do_ref[...]
    zero = jnp.zeros_like(rows)
    queries = [jnp.where(lane_head == h, rows, ext) for h in range(heads)]
    plain_q = jnp.concatenate([jnp.where(lane_head == h, rows, zero) for h in range(heads)], axis=0)
    plain_do = jnp.concatenate([jnp.where(lane_head == h, grads, zero) for h in range(heads)], axis=0)
    product = grads.astype(jnp.float32) * ctx_ref[...].astype(jnp.float32)
    outs = []
    for h in range(heads):
        delta = jnp.sum(jnp.where(lane_head == h, product, 0.0), axis=1, keepdims=True)
        wide = jnp.zeros((block, LANES), jnp.float32)
        for j, piece in enumerate(split3(-delta)):
            wide = jnp.where(place == IDS + j, piece, wide)
        outs.append(jnp.where(lane_head == h, grads, wide.astype(grads.dtype)))

    def step(kb, carry):
        start = pl.multiple_of(kb * block, block)
        probs, scores, fresh = [], [], []
        for h in range(heads):
            p = jnp.exp2(nt(k_all[h, pl.ds(start, block), :], queries[h]))
            ds = (p * nt(v_all[h, pl.ds(start, block), :], outs[h])).astype(jnp.bfloat16)
            probs.append(p.astype(jnp.bfloat16))
            scores.append(ds)
            fresh.append(carry[h] + nn(kt_all[h * size : (h + 1) * size, pl.ds(start, block)], ds))
        dv_all[pl.ds(start, block), :] += nn(jnp.concatenate(probs, axis=1), plain_do)
        dk_all[pl.ds(start, block), :] += nn(jnp.concatenate(scores, axis=1), plain_q)
        return tuple(fresh)

    dq = lax.fori_loop(
        info[2 + 2 * slot], info[3 + 2 * slot], step,
        tuple(jnp.zeros((size, block), jnp.float32) for _ in range(heads)),
    )
    dq_ref[...] = (jnp.concatenate(dq, axis=0) * (1.0 / math.sqrt(size))).T.astype(dq_ref.dtype)

    @pl.when(slot == pl.num_programs(1) - 1)
    def _():
        for b in range(count):
            spot = pl.multiple_of(((b // 2) ^ info[1]) * block, block)
            for j, (total, factor) in enumerate(((dk_all, LN2), (dv_all, 1.0))):

                @pl.when(info[0] == b % 2)
                def _():
                    own_ref[j, pl.ds(spot, block), :] = (total[pl.ds(b * block, block), :] * factor).astype(own_ref.dtype)

                @pl.when(info[0] != b % 2)
                def _():
                    mate_ref[j, pl.ds(spot, block), :] = (total[pl.ds(b * block, block), :] * factor).astype(mate_ref.dtype)


def attention_backward(info, own, mate, ext, grads, ctx, kx, size, first):
    rows, width = ctx.shape
    length = kx.shape[0]
    slots = (info.shape[0] - 2) // 2
    block = rows // slots
    pairs = width // LANES
    heads = LANES // size
    tile = pl.BlockSpec((block, LANES), lambda p, s, i: (s, p))
    return pl.pallas_call(
        functools.partial(backward_kernel, size=size),
        grid_spec=pltpu.PrefetchScalarGridSpec(
            num_scalar_prefetch=1,
            grid=(pairs, slots),
            in_specs=[
                tile,
                tile,
                pl.BlockSpec((block, LANES), lambda p, s, i: (s, first + p)),
                tile,
                pl.BlockSpec((rows, LANES), lambda p, s, i: (0, pairs + p)),
                pl.BlockSpec((rows, LANES), lambda p, s, i: (0, pairs + p)),
                pl.BlockSpec((rows, LANES), lambda p, s, i: (0, 2 * pairs + p)),
                pl.BlockSpec((rows, LANES), lambda p, s, i: (0, 2 * pairs + p)),
                pl.BlockSpec((length, LANES), lambda p, s, i: (0, 0)),
            ],
            out_specs=[
                tile,
                pl.BlockSpec((2, rows, LANES), lambda p, s, i: (0, 0, p)),
                pl.BlockSpec((2, rows, LANES), lambda p, s, i: (0, 0, p)),
            ],
            scratch_shapes=[
                pltpu.VMEM((heads, length, LANES), jnp.bfloat16),
                pltpu.VMEM((LANES, length), jnp.bfloat16),
                pltpu.VMEM((heads, length, LANES), jnp.bfloat16),
                pltpu.VMEM((length, LANES), jnp.float32),
                pltpu.VMEM((length, LANES), jnp.float32),
            ],
        ),
        out_shape=[
            jax.ShapeDtypeStruct((rows, width), jnp.bfloat16),
            jax.ShapeDtypeStruct((2, rows, width), jnp.float32),
            jax.ShapeDtypeStruct((2, rows, width), jnp.bfloat16),
        ],
        compiler_params=pltpu.CompilerParams(dimension_semantics=("arbitrary", "arbitrary")),
        cost_estimate=pl.CostEstimate(
            flops=5 * rows * length * width, bytes_accessed=24 * rows * width, transcendentals=rows * length * pairs
        ),
        name="attention_backward",
    )(info, own, ext, grads, ctx, own, mate, own, mate, kx)


def key_extension(ids):
    place = jnp.arange(LANES) % (LANES // 2)
    hot = ids[:, None] == place[None, :]
    return (hot | ((place >= IDS) & (place < IDS + 3))[None, :]).astype(jnp.bfloat16)


def query_extension(ids):
    place = jnp.arange(LANES) % (LANES // 2)
    other = (place < IDS)[None, :] & (ids[:, None] != place[None, :])
    return jnp.where(other, FAR, 0.0).astype(jnp.bfloat16)


H = 12
HD = 64
LOG2E = 1.0 / LN2
PARTS = 3
eps_norm = 1e-06
bf16 = jnp.bfloat16
f32 = jnp.float32


def norm_forward(total, gain, shift):
    middle = jnp.mean(total, axis=-1, keepdims=True)
    centred = total - middle
    factor = lax.rsqrt(jnp.mean(centred * centred, axis=-1, keepdims=True) + eps_norm)
    normed = centred * factor
    return (normed * gain + shift, normed, factor)


def norm_backward(grad_out, normed, factor, gain):
    scaled = grad_out * gain
    inner = (
        scaled
        - jnp.mean(scaled, axis=-1, keepdims=True)
        - normed * jnp.mean(scaled * normed, axis=-1, keepdims=True)
    )
    return (factor * inner, jnp.sum(grad_out * normed, axis=0), jnp.sum(grad_out, axis=0))


def gelu_parts(hidden):
    normal_cdf = 0.5 * (1.0 + jax.scipy.special.erf(hidden * (1.0 / math.sqrt(2.0))))
    density = jnp.exp(-0.5 * hidden * hidden) * (1.0 / math.sqrt(2.0 * math.pi))
    return (hidden * normal_cdf, normal_cdf + hidden * density)


def dot(a, b):
    return jnp.dot(a, b, preferred_element_type=f32)


def column_sums(values):
    return jnp.sum(values.astype(f32), axis=0)


def xor_pairs(size, bits):
    return [(i, i ^ bits) for i in range(size)]


def straight(values):
    return with_layout_constraint(values, Layout(tuple(range(values.ndim))))


def pick(values, index, axis=0):
    return lax.dynamic_index_in_dim(values, index, axis, keepdims=False)


def after(values, *marks):
    return lax.optimization_barrier((values, marks))[0]


class Places:
    def __init__(self):
        self.columns = lax.axis_size("seq")
        self.shards = lax.axis_size("fsdp")
        self.column = lax.axis_index("seq")
        self.shard = lax.axis_index("fsdp")
        self.core = self.shard & 1
        self.plane = self.shard >> 1

    def mate(self, values):
        return lax.ppermute(values, "fsdp", xor_pairs(self.shards, 1))

    def across(self, values, bits):
        return lax.ppermute(values, "seq", xor_pairs(self.columns, bits))

    def aside(self, values, bits):
        return lax.ppermute(values, "fsdp", xor_pairs(self.shards, 2 * bits))


def to_sequence_parts(here, values):
    groups, piece, width = values.shape
    halves = values.reshape(groups, 2, piece // 2, width)
    kept = straight(pick(halves, here.core, 1))
    other = straight(here.mate(straight(pick(halves, 1 - here.core, 1))))
    parts = []
    for k in range(here.columns):
        want = here.column ^ k
        same = lax.div(want, groups) == here.core
        spot = lax.rem(want, groups)
        parts.append(straight(jnp.where(same, pick(kept, spot), pick(other, spot))))
    return parts


def from_sequence_send(here, slots):
    return [here.across(slots[k], k) if k else slots[k] for k in range(here.columns)]


def from_sequence_end(here, slots, groups):
    rows = jnp.stack(slots)

    def of(core):
        return jnp.stack([pick(rows, here.column ^ (core * groups + j)) for j in range(groups)])

    kept = of(here.core)
    other = here.mate(of(1 - here.core))
    first = here.core == 0
    return jnp.concatenate([jnp.where(first, kept, other), jnp.where(first, other, kept)], axis=1)


def place_kernel(info, *refs, moves, outs):
    count = len(moves)
    parts, full, buffers = refs[:count], refs[count : count + outs], refs[count + outs : 2 * count + outs]
    in_sem, out_sem = refs[2 * count + outs :]
    reads = [pltpu.make_async_copy(parts[k], buffers[k], in_sem.at[k]) for k in range(count)]
    for read in reads:
        read.start()
    writes = []
    for k in range(count):
        reads[k].wait()
        for j, (row, rows, cut_row, col, cols, out) in enumerate(moves[k]):
            write = pltpu.make_async_copy(
                buffers[k].at[pl.ds(cut_row, rows), pl.ds(col, cols)],
                full[out].at[info[k], pl.ds(row, rows), :],
                out_sem.at[k, j],
            )
            write.start()
            writes.append(write)
    for write in writes:
        write.wait()


def place(parts, spots, firsts, rows, cuts):
    kind = parts[0].dtype
    shards = sum(part.shape[0] for part in parts) // rows
    moves = [
        [(first, part.shape[0], 0, col, cols, out) for out, (col, cols) in enumerate(cuts)] for first, part in zip(firsts, parts)
    ]
    full = pl.pallas_call(
        functools.partial(place_kernel, moves=moves, outs=len(cuts)),
        grid_spec=pltpu.PrefetchScalarGridSpec(
            num_scalar_prefetch=1,
            grid=(),
            in_specs=[pl.BlockSpec(memory_space=pl.ANY)] * len(parts),
            out_specs=[pl.BlockSpec(memory_space=pl.ANY)] * len(cuts),
            scratch_shapes=[pltpu.VMEM(part.shape, kind) for part in parts]
            + [pltpu.SemaphoreType.DMA((len(parts),)), pltpu.SemaphoreType.DMA((len(parts), len(cuts)))],
        ),
        out_shape=[jax.ShapeDtypeStruct((shards, rows, cols), kind) for _, cols in cuts],
        cost_estimate=pl.CostEstimate(flops=0, bytes_accessed=0, transcendentals=0),
        name="place_parts",
    )(jnp.stack(spots).astype(jnp.int32), *parts)
    return [f.reshape(-1, f.shape[2]) for f in full]


def gather_cut(here, local, cuts, mark):
    if here.shards != 8:
        full = lax.all_gather(local, "fsdp", axis=0, tiled=True)
        return [full[:, col : col + cols] for col, cols in cuts]
    rows = local.shape[0]
    middle = rows // 2
    across_x, across_y = here.aside(local, 1), here.aside(local, 2)
    across_x, across_y = after((across_x, across_y), mark)
    low, high = here.aside(across_x[:middle], 2), here.aside(across_y[middle:], 1)
    parts = [local, across_x, across_y, low, high]
    spots = [here.shard ^ (2 * k) for k in (0, 1, 2, 3, 3)]
    parts, spots = parts + [here.mate(part) for part in parts], spots + [spot ^ 1 for spot in spots]
    return place(parts, spots, [0, 0, 0, 0, middle] * 2, rows, cuts)


def pack_kernel(mix_ref, merge_ref, columns_ref, out_ref, *, size, parts):
    rows, width = merge_ref.shape
    per = LANES // size
    lane_low = lane_of(rows) < size
    pairs = width // LANES // parts
    for pair in range(width // LANES):
        part, spot = pair // pairs, pair % pairs
        for j in range(3):
            one, two = [((3 * (per * pair + k) + j) * size) // LANES * LANES for k in range(2)]
            one, two = mix_ref[:, one : one + LANES].astype(jnp.float32), mix_ref[:, two : two + LANES].astype(jnp.float32)
            if j % 2:
                joined = pltpu.roll(jnp.where(lane_low, two, one), size, 1)
            else:
                joined = jnp.where(lane_low, one, two)
            at = (part * 3 + j) * pairs * LANES + spot * LANES
            out_ref[:, at : at + LANES] = joined.astype(out_ref.dtype)
    out_ref[:, 3 * width : 4 * width] = merge_ref[...]
    out_ref[:, 4 * width :] = columns_ref[...]


def pack(mix, merge, columns, size, parts):
    rows, width = merge.shape
    return pl.pallas_call(
        functools.partial(pack_kernel, size=size, parts=parts),
        out_shape=jax.ShapeDtypeStruct((rows, 4 * width + LANES), mix.dtype),
        name="pack_projection",
    )(mix, merge, columns)


def share_pair(here, partial):
    shards, rows, width = partial.shape
    pairs = partial.reshape(shards // 2, 2, rows, width)
    return pick(pairs, here.core, 1), here.mate(pick(pairs, 1 - here.core, 1).astype(bf16))


def share_plane(here, kept, other):
    def total(k):
        spot = here.plane ^ k
        return pick(kept, spot).astype(f32) + pick(other, spot).astype(f32)

    return total(0), [here.aside(total(k).astype(bf16), k) for k in range(1, here.shards // 2)]


def share_sum(share, others):
    for other in others:
        share = share + other.astype(f32)
    return share.astype(bf16)


def column_first(here, share):
    low = share.reshape(2, share.shape[0] // 2, share.shape[1])
    side = here.column & 1
    return pick(low, side), here.across(pick(low, 1 - side), 1)


def column_second(here, half, other):
    low = (half.astype(f32) + other.astype(f32)).astype(bf16)
    step, others = 2, []
    while 2 * step < here.columns:
        low = (low.astype(f32) + here.across(low, step).astype(f32)).astype(bf16)
        step *= 2
    return low, here.across(low, step)


def column_third(here, half, other):
    half = (half.astype(f32) + other.astype(f32)).astype(bf16)
    return half, here.across(half, 1)


def column_last(here, half, other):
    first = (here.column & 1) == 0
    return jnp.concatenate([jnp.where(first, half, other), jnp.where(first, other, half)], axis=0)


def per_device(
    tokens,
    segment_ids,
    mix_weight,
    query_bias,
    value_bias,
    merge_weight,
    merge_bias,
    first_gain,
    first_shift,
    up_weight,
    up_bias,
    down_weight,
    down_bias,
    second_gain,
    second_shift,
    output_grad,
):
    here = Places()
    groups, piece, width = tokens.shape
    shards = here.shards
    own = width // shards
    hidden_size = up_weight.shape[1]
    half = piece // 2
    rows = here.columns * half
    length = here.columns * piece

    def send(parts):
        return [straight(part) for part in from_sequence_send(here, parts)]

    ups = hidden_size // width
    part_width = width // PARTS
    token_parts = to_sequence_parts(here, tokens)
    token_slots = send(token_parts)

    vectors = (query_bias, value_bias, merge_bias, first_gain, first_shift, down_bias, second_gain, second_shift)
    local_weights = after((vectors, up_bias, mix_weight, merge_weight), token_parts)
    lines = jnp.concatenate([jnp.stack(local_weights[0]), local_weights[1].reshape(ups, own)], axis=0)
    columns = jnp.pad(lines, ((0, LANES - lines.shape[0]), (0, 0))).T
    mix_local = pack(local_weights[2], local_weights[3], columns, HD, PARTS)
    *mix_parts, merge_full, columns_full = gather_cut(
        here, mix_local, [(p * width, width) for p in range(PARTS + 1)] + [(4 * width, LANES)], token_slots[2]
    )
    lines_full = columns_full.T.astype(f32)
    query_full, value_full, merge_bias_full, gain_one, shift_one, down_bias_full, gain_two, shift_two = [
        lines_full[j] for j in range(8)
    ]
    up_bias_full = lines_full[8 : 8 + ups].reshape(ups, shards, own).transpose(1, 0, 2).reshape(-1)

    ids_parts = to_sequence_parts(here, after(segment_ids, token_parts).reshape(groups, piece, 1))
    ids_own = jnp.concatenate(send(ids_parts), axis=0).reshape(here.columns, half)
    ids_mate = here.mate(ids_own)
    by_core = jnp.stack([jnp.where(here.core == 0, ids_own, ids_mate), jnp.where(here.core == 0, ids_mate, ids_own)], axis=1)
    ids = jnp.stack([pick(by_core, k ^ here.column) for k in range(here.columns)]).reshape(2 * here.columns, half)
    first_id, last_id = ids[:, 0], ids[:, -1]
    low = jnp.sum(last_id[None, :] < ids_own[:, :1], axis=1)
    high = jnp.sum(first_id[None, :] <= ids_own[:, -1:], axis=1)
    info = jnp.concatenate([jnp.stack([here.core, here.column]), jnp.stack([low, high], axis=1).reshape(-1)]).astype(jnp.int32)
    key_ext = key_extension(ids.reshape(length))
    query_ext = query_extension(ids_own.reshape(rows))

    cotangent_parts = to_sequence_parts(here, after(output_grad, token_parts))
    ready = (cotangent_parts, mix_parts, merge_full, lines_full, info, key_ext, query_ext)
    token_slots, (cotangent_parts, mix_parts, merge_full, lines_full, info, key_ext, query_ext) = lax.optimization_barrier(
        (token_slots, ready)
    )
    flat = straight(jnp.concatenate(token_slots, axis=0))
    cotangent_slots = send(after(cotangent_parts, flat))
    direct = shards == 8
    up_local, down_local = after((up_weight, down_weight), mix_parts[0])
    if direct:
        up_parts = [up_local, here.aside(up_local, 1), here.aside(up_local, 2)]
        down_parts = [down_local, here.aside(down_local, 1), here.aside(down_local, 2)]
    else:
        up_full, down_full = [lax.all_gather(w, "fsdp", axis=0, tiled=True) for w in (up_local, down_local)]

    column_scale = jnp.where(jnp.arange(width) < part_width, LOG2E / math.sqrt(HD), 1.0)
    mixed, mixed_mate = [], []
    for p in range(PARTS):
        of_part = slice(p * part_width, (p + 1) * part_width)
        bias = jnp.concatenate([query_full[of_part], jnp.zeros((part_width,), f32), value_full[of_part]])
        mixed.append(((dot(flat, mix_parts[p]) + bias) * column_scale).astype(bf16))
        mixed_mate.append(here.mate(mixed[p]))

    contexts, exts = [], []
    plan, spots = NOTHING, ()
    for p in range(PARTS):
        if p:
            mixed[p], mixed_mate[p] = after((mixed[p], mixed_mate[p]), contexts[-1])
        if p == 1 and direct:
            up_parts, down_parts = after((up_parts, down_parts), contexts[-1])
            up_parts.append(here.aside(up_parts[1], 2))
            down_parts.append(here.aside(down_parts[2], 1))
            mates = [[here.mate(w) for w in parts] for parts in (up_parts, down_parts)]
        if p == PARTS - 1:
            mixed[p], cotangent_slots = after((mixed[p], cotangent_slots), cotangent_slots)
            if direct:
                pieces = up_parts + mates[0] + down_parts + mates[1]
                outs = [(shards,) + up_weight.shape, (shards,) + down_weight.shape]
                spots = [here.shard ^ (2 * k) for k in range(4)]
                spots = (spots + [spot ^ 1 for spot in spots]) * 2
                plan = (tuple(after(pieces, contexts[-1])), (0,) * 8 + (1,) * 8, tuple(outs))
        context, ext, *placed = attention_forward(info, mixed[p], mixed_mate[p], query_ext, key_ext, HD, plan, spots)
        contexts.append(context)
        exts.append(ext)
    if direct:
        up_full, down_full = [full.reshape(-1, full.shape[2]) for full in placed]
    context = jnp.concatenate(contexts, axis=1)
    cotangent = jnp.concatenate(after(cotangent_slots, contexts[-1]), axis=0).astype(f32)

    attended = dot(context, merge_full) + merge_bias_full
    first_out, normed_one, factor_one = norm_forward(flat.astype(f32) + attended, gain_one, shift_one)
    first_low = first_out.astype(bf16)
    hidden = dot(first_low, up_full) + up_bias_full
    active, slope = gelu_parts(hidden)
    active_low, slope_low = lax.optimization_barrier((active.astype(bf16), slope.astype(bf16)))
    branch = dot(active_low, down_full) + down_bias_full
    result, normed_two, factor_two = norm_forward(first_out + branch, gain_two, shift_two)
    output_slots = from_sequence_send(here, list(result.astype(bf16).reshape(here.columns, half, width)))

    grad_second, second_gain_grad, second_shift_grad = norm_backward(cotangent, normed_two, factor_two, gain_two)
    grad_branch = grad_second.astype(bf16)
    down_grad = dot(active_low.T, grad_branch)
    down_kept, down_other = share_pair(here, down_grad.reshape(shards, -1, width))
    down_bias_grad = column_sums(grad_branch)
    grad_active = dot(grad_branch, down_full.T)
    grad_hidden = (grad_active * slope_low.astype(f32)).astype(bf16)
    down_share, down_others = share_plane(here, down_kept, after(down_other, grad_hidden))
    up_grad = dot(first_low.T, grad_hidden)
    up_bias_grad = column_sums(grad_hidden)
    grad_first = grad_second + dot(grad_hidden, up_full.T)
    grad_sum, first_gain_grad, first_shift_grad = norm_backward(grad_first, normed_one, factor_one, gain_one)
    grad_attended = grad_sum.astype(bf16)
    merge_grad = dot(context.T, grad_attended)
    merge_bias_grad = column_sums(grad_attended)
    up_merge = jnp.concatenate([up_grad.reshape(shards, own, hidden_size), merge_grad.reshape(shards, own, width)], axis=2)
    up_kept, up_other = share_pair(here, up_merge)
    grad_context = dot(grad_attended, merge_full.T).astype(bf16)
    up_share, up_others = share_plane(here, up_kept, after(up_other, grad_context))

    def backward(part, grads):
        dq, kept, other = attention_backward(
            info, mixed[part], mixed_mate[part], exts[part], grads, contexts[part], key_ext, HD, part * part_width // LANES
        )
        return dq, kept, here.mate(other)

    def mixed_part(pieces):
        dq, kept, other = pieces
        kv = (kept + other.astype(f32)).astype(bf16)
        return jnp.concatenate([dq, kv[0], kv[1]], axis=1)

    down_half, down_other = column_first(here, share_sum(down_share, down_others))
    one = backward(0, after(grad_context, down_half, up_share, output_slots))
    down_half, down_other = column_second(here, *after((down_half, down_other), one[0]))
    up_others, up_share = after((up_others, up_share), one[0])
    up_half, up_other = column_first(here, share_sum(up_share, up_others))
    two = backward(1, after(grad_context, down_half, up_half))
    down_half, down_other = column_third(here, *after((down_half, down_other), two[0]))
    up_half, up_other = column_second(here, *after((up_half, up_other), two[0]))
    mixed_one = mixed_part(after(one, two[0]))
    mix_grad_one = dot(flat.T, mixed_one)
    mix_kept_one, mix_other_one = share_pair(here, mix_grad_one.reshape(shards, own, -1))
    input_part = grad_sum + dot(mixed_one, mix_parts[0].T)
    mix_share_one, mix_others_one = share_plane(here, mix_kept_one, after(mix_other_one, input_part))
    three = backward(2, after(grad_context, down_half, up_half, mix_share_one))
    down_half, down_other = after((down_half, down_other), three[0])
    up_half, up_other = column_third(here, *after((up_half, up_other), three[0]))
    mixed_two = mixed_part(after(two, three[0]))
    mix_grad_two = dot(flat.T, mixed_two)
    mix_kept_two, mix_other_two = share_pair(here, mix_grad_two.reshape(shards, own, -1))
    input_part = input_part + dot(mixed_two, mix_parts[1].T)
    mixed_three = mixed_part(after(three, input_part, mix_kept_two))
    input_low = (input_part + dot(mixed_three, mix_parts[2].T)).astype(bf16)
    input_slots = from_sequence_send(here, list(input_low.reshape(here.columns, half, width)))
    mixed_three, mix_other_two, down_other, up_other = after((mixed_three, mix_other_two, down_other, up_other), input_low)
    mix_share_two, mix_others_two = share_plane(here, mix_kept_two, mix_other_two)
    mix_grad_rest = dot(flat.T, mixed_three)

    sums = [column_sums(m) for m in (mixed_one, mixed_two, mixed_three)]
    query_grad = jnp.concatenate([s[:part_width] for s in sums])
    value_grad = jnp.concatenate([s[2 * part_width :] for s in sums])
    vectors = (
        query_grad,
        value_grad,
        merge_bias_grad,
        first_gain_grad,
        first_shift_grad,
        down_bias_grad,
        second_gain_grad,
        second_shift_grad,
    )
    up_lines = up_bias_grad.reshape(shards, ups, own).transpose(1, 0, 2).reshape(ups, width)
    lines_grad = jnp.concatenate([jnp.stack(vectors), up_lines], axis=0)
    columns_grad = jnp.pad(lines_grad, ((0, LANES - lines_grad.shape[0]), (0, 0))).T
    rest = jnp.concatenate([mix_grad_rest, columns_grad], axis=1).reshape(shards, own, -1)
    rest_kept, rest_other = share_pair(here, rest)
    rest_share, rest_others = share_plane(here, rest_kept, after(rest_other, input_slots[1]))
    mix_share = jnp.concatenate(
        [
            share_sum(mix_share_one, mix_others_one),
            share_sum(mix_share_two, mix_others_two),
            share_sum(rest_share, rest_others),
        ],
        axis=1,
    )
    mix_last = column_last(here, *column_third(here, *column_second(here, *column_first(here, mix_share))))

    output = from_sequence_end(here, after(output_slots, input_low), groups)
    final_input = from_sequence_end(here, input_slots, groups).astype(f32)
    final_down = column_last(here, down_half, down_other).astype(f32)
    final_up_merge = column_last(here, up_half, up_other).astype(f32)
    final_mix = mix_last[:, : 3 * width].astype(f32).reshape(own, PARTS, 3, H // PARTS, HD)
    final_mix = final_mix.transpose(0, 1, 3, 2, 4).reshape(own, 3 * width)
    final_columns = mix_last[:, 3 * width :].astype(f32)
    finals = final_columns.T
    (
        final_query,
        final_value,
        final_merge_bias,
        final_gain_one,
        final_shift_one,
        final_down_bias,
        final_gain_two,
        final_shift_two,
    ) = [finals[j] for j in range(8)]
    final_up_bias = finals[8 : 8 + ups].reshape(-1)
    return (
        output,
        final_input,
        final_mix,
        final_query,
        final_value,
        final_up_merge[:, hidden_size:],
        final_merge_bias,
        final_gain_one,
        final_shift_one,
        final_up_merge[:, :hidden_size],
        final_up_bias,
        final_down,
        final_down_bias,
        final_gain_two,
        final_shift_two,
    )


def solution(mesh):
    wide, row, thin = P("fsdp", "seq", None), P("fsdp", None), P("fsdp")
    return jax.shard_map(
        per_device,
        mesh=mesh,
        in_specs=(wide, P("fsdp", "seq"), row, thin, thin, row, thin, thin, thin, row, thin, row, thin, thin, thin, wide),
        out_specs=(wide, wide, row, thin, thin, row, thin, thin, thin, row, thin, row, thin, thin, thin),
        check_vma=False,
    )
```

```python
import functools, math
import jax, jax.numpy as jnp
from jax import lax
from jax.experimental import pallas as pl
from jax.experimental.layout import Layout, with_layout_constraint
from jax.experimental.pallas import tpu as pltpu
from jax.sharding import PartitionSpec as P

LANES = 128
FAR = -1000000000.0
IDS = 4
LN2 = math.log(2.0)


def nt(a, b):
    return lax.dot_general(a, b, (((1,), (1,)), ((), ())), preferred_element_type=jnp.float32)


def nn(a, b):
    return lax.dot_general(a, b, (((1,), (0,)), ((), ())), preferred_element_type=jnp.float32)


def lane_of(rows):
    return lax.broadcasted_iota(jnp.int32, (rows, LANES), 1)


def split3(x):
    high = x.astype(jnp.bfloat16).astype(jnp.float32)
    middle = (x - high).astype(jnp.bfloat16).astype(jnp.float32)
    return high, middle, x - high - middle


def gather_blocks(info, block, count, own_ref, mate_ref, put):
    for b in range(count):
        start = pl.multiple_of(((b // 2) ^ info[1]) * block, block)

        @pl.when(info[0] == b % 2)
        def _():
            put(b, own_ref[pl.ds(start, block), :])

        @pl.when(info[0] != b % 2)
        def _():
            put(b, mate_ref[pl.ds(start, block), :])


def forward_kernel(info, q_ref, k_own, k_mate, v_own, v_mate, qx_ref, kx_ref, *refs, size, plan):
    count, moves, outs = plan
    beside, (out_ref, ext_ref), full = refs[:count], refs[count : count + 2], refs[count + 2 : count + 2 + len(outs)]
    k_all, vt_all, s_all, *buffers = refs[count + 2 + len(outs) :]
    slot = pl.program_id(1)
    if count:
        in_sem, out_sem = buffers[count:]
        reads = [pltpu.make_async_copy(beside[j], buffers[j], in_sem.at[j]) for j in range(count)]
        writes = [
            pltpu.make_async_copy(
                buffers[j].at[pl.ds(row, rows), :],
                full[out].at[info[info.shape[0] - count + j], :, pl.ds(col, buffers[j].shape[1])],
                out_sem.at[j, k],
            )
            for j in range(count)
            for k, (row, rows, out, col) in enumerate(moves)
        ]
        at = pl.program_id(0) * pl.num_programs(1) + slot

        @pl.when(at == 0)
        def _():
            for read in reads:
                read.start()

        @pl.when(at == 2)
        def _():
            for read in reads:
                read.wait()
            for write in writes:
                write.start()

        @pl.when(at == pl.num_programs(0) * pl.num_programs(1) - 1)
        def _():
            for write in writes:
                write.wait()

    block = q_ref.shape[0]
    count = kx_ref.shape[0] // block
    heads = LANES // size
    lane_head = lane_of(block) // size

    @pl.when(slot == 0)
    def _():
        def put_k(b, rows):
            ext = kx_ref[b * block : (b + 1) * block, :]
            for h in range(heads):
                k_all[h, b * block : (b + 1) * block, :] = jnp.where(lane_head == h, rows, ext)

        def put_v(b, rows):
            turned = rows.T
            for h in range(heads):
                vt_all[h, :size, b * block : (b + 1) * block] = turned[h * size : (h + 1) * size]

        gather_blocks(info, block, count, k_own, k_mate, put_k)
        gather_blocks(info, block, count, v_own, v_mate, put_v)
        for h in range(heads):
            vt_all[h, size:, :] = jnp.ones((vt_all.shape[1] - size, vt_all.shape[2]), vt_all.dtype)

    rows = q_ref[...]
    qx = qx_ref[...]
    queries = [jnp.where(lane_head == h, rows, qx) for h in range(heads)]

    part = block
    lo, hi = info[2 + 2 * slot], info[3 + 2 * slot]

    def score(h, kb, i, top):
        at = pl.multiple_of(kb * block + i * part, part)
        st = nt(k_all[h, pl.ds(at, part), :], queries[h])
        s_all[h, i * part : (i + 1) * part, :] = st
        return jnp.maximum(top, jnp.max(st.reshape(part // 8, 8, block), axis=0))

    def weigh(h, kb, i, m, acc):
        at = pl.multiple_of(kb * block + i * part, part)
        p = jnp.exp2(s_all[h, i * part : (i + 1) * part, :] - m).astype(jnp.bfloat16)
        return acc + nn(vt_all[h, :, pl.ds(at, part)], p)

    least = jnp.full((8, block), -jnp.inf, jnp.float32)

    def step(kb, carry):
        tops, state = carry
        tops, state = list(tops), list(state)
        after = jnp.minimum(kb + 1, count - 1)
        for h in range(heads):
            ahead = (h + 1) % heads
            ahead_kb = kb if ahead else after
            m, acc = state[h]
            m_new = jnp.maximum(m, jnp.max(tops[h], axis=0, keepdims=True))
            acc = acc * jnp.exp2(m - m_new)
            top = least
            for i in range(1):
                top = score(ahead, ahead_kb, i, top)
                acc = weigh(h, kb, i, m_new, acc)
            tops[ahead] = top
            state[h] = (m_new, acc)
        return tuple(tops), tuple(state)

    start = tuple(
        (jnp.full((1, block), -jnp.inf, jnp.float32), jnp.zeros((vt_all.shape[1], block), jnp.float32))
        for _ in range(heads)
    )
    first = score(0, lo, 0, least)
    _, done = lax.fori_loop(lo, hi, step, ((first,) + (least,) * (heads - 1), start))
    sums = [acc[size : size + 1] for _, acc in done]
    out_t = jnp.concatenate([acc[:size] * (1.0 / l) for (_, acc), l in zip(done, sums)], axis=0)
    out_ref[...] = out_t.T.astype(out_ref.dtype)
    row = lax.broadcasted_iota(jnp.int32, (size, block), 0)
    parts = []
    for (m, _), l in zip(done, sums):
        pieces = split3(-(m + jnp.log2(l)))
        part = jnp.zeros((size, block), jnp.float32)
        for j, piece in enumerate(pieces):
            part = jnp.where(row == IDS + j, piece, part)
        parts.append(part)
    ext_ref[...] = (jnp.concatenate(parts[::-1], axis=0).T + qx.astype(jnp.float32)).astype(ext_ref.dtype)


NOTHING = ((), (), ())


def attention_forward(info, own, mate, qx, kx, size, plan=NOTHING, spots=()):
    rows, width = own.shape[0], own.shape[1] // 3
    length = kx.shape[0]
    slots = (info.shape[0] - 2) // 2
    block = rows // slots
    pairs = width // LANES
    heads = LANES // size
    pieces, moves, outs = plan
    if pieces:
        info = jnp.concatenate([info, jnp.stack(spots).astype(jnp.int32)])
    anywhere = pl.BlockSpec(memory_space=pl.ANY)
    return pl.pallas_call(
        functools.partial(forward_kernel, size=size, plan=(len(pieces), moves, outs)),
        grid_spec=pltpu.PrefetchScalarGridSpec(
            num_scalar_prefetch=1,
            grid=(pairs, slots),
            in_specs=[
                pl.BlockSpec((block, LANES), lambda p, s, i: (s, p)),
                pl.BlockSpec((rows, LANES), lambda p, s, i: (0, pairs + p)),
                pl.BlockSpec((rows, LANES), lambda p, s, i: (0, pairs + p)),
                pl.BlockSpec((rows, LANES), lambda p, s, i: (0, 2 * pairs + p)),
                pl.BlockSpec((rows, LANES), lambda p, s, i: (0, 2 * pairs + p)),
                pl.BlockSpec((block, LANES), lambda p, s, i: (s, 0)),
                pl.BlockSpec((length, LANES), lambda p, s, i: (0, 0)),
            ]
            + [anywhere] * len(pieces),
            out_specs=[pl.BlockSpec((block, LANES), lambda p, s, i: (s, p))] * 2 + [anywhere] * len(outs),
            scratch_shapes=[
                pltpu.VMEM((heads, length, LANES), jnp.bfloat16),
                pltpu.VMEM((heads, size + 16, length), jnp.bfloat16),
                pltpu.VMEM((heads, block, block), jnp.float32),
            ]
            + [pltpu.VMEM(piece.shape, piece.dtype) for piece in pieces]
            + [pltpu.SemaphoreType.DMA((len(pieces),)), pltpu.SemaphoreType.DMA((len(pieces), len(moves)))] * bool(pieces),
        ),
        out_shape=[jax.ShapeDtypeStruct((rows, width), jnp.bfloat16)] * 2
        + [jax.ShapeDtypeStruct(shape, jnp.bfloat16) for shape in outs],
        compiler_params=pltpu.CompilerParams(dimension_semantics=("arbitrary", "arbitrary")),
        cost_estimate=pl.CostEstimate(
            flops=2 * rows * length * width, bytes_accessed=8 * rows * width * 2, transcendentals=rows * length * pairs
        ),
        name="attention_forward",
    )(info, own, own, mate, own, mate, qx, kx, *pieces)


def backward_kernel(
    info, q_ref, ext_ref, do_ref, ctx_ref, k_own, k_mate, v_own, v_mate, kx_ref,
    dq_ref, own_ref, mate_ref, k_all, kt_all, v_all, dk_all, dv_all, *, size
):
    slot = pl.program_id(1)
    block = q_ref.shape[0]
    count = kx_ref.shape[0] // block
    heads = LANES // size
    lane = lane_of(block)
    lane_head = lane // size
    place = lane % size
    three = (place >= IDS) & (place < IDS + 3)

    @pl.when(slot == 0)
    def _():
        def put_k(b, rows):
            ext = kx_ref[b * block : (b + 1) * block, :]
            for h in range(heads):
                k_all[h, b * block : (b + 1) * block, :] = jnp.where(lane_head == h, rows, ext)
            kt_all[:, b * block : (b + 1) * block] = rows.T

        def put_v(b, rows):
            one = three.astype(rows.dtype)
            for h in range(heads):
                v_all[h, b * block : (b + 1) * block, :] = jnp.where(lane_head == h, rows, one)

        gather_blocks(info, block, count, k_own, k_mate, put_k)
        gather_blocks(info, block, count, v_own, v_mate, put_v)
        dk_all[...] = jnp.zeros_like(dk_all)
        dv_all[...] = jnp.zeros_like(dv_all)

    rows = q_ref[...]
    ext = ext_ref[...]
    grads = do_ref[...]
    zero = jnp.zeros_like(rows)
    queries = [jnp.where(lane_head == h, rows, ext) for h in range(heads)]
    plain_q = jnp.concatenate([jnp.where(lane_head == h, rows, zero) for h in range(heads)], axis=0)
    plain_do = jnp.concatenate([jnp.where(lane_head == h, grads, zero) for h in range(heads)], axis=0)
    product = grads.astype(jnp.float32) * ctx_ref[...].astype(jnp.float32)
    outs = []
    for h in range(heads):
        delta = jnp.sum(jnp.where(lane_head == h, product, 0.0), axis=1, keepdims=True)
        wide = jnp.zeros((block, LANES), jnp.float32)
        for j, piece in enumerate(split3(-delta)):
            wide = jnp.where(place == IDS + j, piece, wide)
        outs.append(jnp.where(lane_head == h, grads, wide.astype(grads.dtype)))

    def step(kb, carry):
        start = pl.multiple_of(kb * block, block)
        probs, scores, fresh = [], [], []
        for h in range(heads):
            p = jnp.exp2(nt(k_all[h, pl.ds(start, block), :], queries[h]))
            ds = (p * nt(v_all[h, pl.ds(start, block), :], outs[h])).astype(jnp.bfloat16)
            probs.append(p.astype(jnp.bfloat16))
            scores.append(ds)
            fresh.append(carry[h] + nn(kt_all[h * size : (h + 1) * size, pl.ds(start, block)], ds))
        dv_all[pl.ds(start, block), :] += nn(jnp.concatenate(probs, axis=1), plain_do)
        dk_all[pl.ds(start, block), :] += nn(jnp.concatenate(scores, axis=1), plain_q)
        return tuple(fresh)

    dq = lax.fori_loop(
        info[2 + 2 * slot], info[3 + 2 * slot], step,
        tuple(jnp.zeros((size, block), jnp.float32) for _ in range(heads)),
    )
    dq_ref[...] = (jnp.concatenate(dq, axis=0) * (1.0 / math.sqrt(size))).T.astype(dq_ref.dtype)

    @pl.when(slot == pl.num_programs(1) - 1)
    def _():
        for b in range(count):
            spot = pl.multiple_of(((b // 2) ^ info[1]) * block, block)
            for j, (total, factor) in enumerate(((dk_all, LN2), (dv_all, 1.0))):

                @pl.when(info[0] == b % 2)
                def _():
                    own_ref[j, pl.ds(spot, block), :] = (total[pl.ds(b * block, block), :] * factor).astype(own_ref.dtype)

                @pl.when(info[0] != b % 2)
                def _():
                    mate_ref[j, pl.ds(spot, block), :] = (total[pl.ds(b * block, block), :] * factor).astype(mate_ref.dtype)


def attention_backward(info, own, mate, ext, grads, ctx, kx, size, first):
    rows, width = ctx.shape
    length = kx.shape[0]
    slots = (info.shape[0] - 2) // 2
    block = rows // slots
    pairs = width // LANES
    heads = LANES // size
    tile = pl.BlockSpec((block, LANES), lambda p, s, i: (s, p))
    return pl.pallas_call(
        functools.partial(backward_kernel, size=size),
        grid_spec=pltpu.PrefetchScalarGridSpec(
            num_scalar_prefetch=1,
            grid=(pairs, slots),
            in_specs=[
                tile,
                tile,
                pl.BlockSpec((block, LANES), lambda p, s, i: (s, first + p)),
                tile,
                pl.BlockSpec((rows, LANES), lambda p, s, i: (0, pairs + p)),
                pl.BlockSpec((rows, LANES), lambda p, s, i: (0, pairs + p)),
                pl.BlockSpec((rows, LANES), lambda p, s, i: (0, 2 * pairs + p)),
                pl.BlockSpec((rows, LANES), lambda p, s, i: (0, 2 * pairs + p)),
                pl.BlockSpec((length, LANES), lambda p, s, i: (0, 0)),
            ],
            out_specs=[
                tile,
                pl.BlockSpec((2, rows, LANES), lambda p, s, i: (0, 0, p)),
                pl.BlockSpec((2, rows, LANES), lambda p, s, i: (0, 0, p)),
            ],
            scratch_shapes=[
                pltpu.VMEM((heads, length, LANES), jnp.bfloat16),
                pltpu.VMEM((LANES, length), jnp.bfloat16),
                pltpu.VMEM((heads, length, LANES), jnp.bfloat16),
                pltpu.VMEM((length, LANES), jnp.float32),
                pltpu.VMEM((length, LANES), jnp.float32),
            ],
        ),
        out_shape=[
            jax.ShapeDtypeStruct((rows, width), jnp.bfloat16),
            jax.ShapeDtypeStruct((2, rows, width), jnp.float32),
            jax.ShapeDtypeStruct((2, rows, width), jnp.bfloat16),
        ],
        compiler_params=pltpu.CompilerParams(dimension_semantics=("arbitrary", "arbitrary")),
        cost_estimate=pl.CostEstimate(
            flops=5 * rows * length * width, bytes_accessed=24 * rows * width, transcendentals=rows * length * pairs
        ),
        name="attention_backward",
    )(info, own, ext, grads, ctx, own, mate, own, mate, kx)


def key_extension(ids):
    place = jnp.arange(LANES) % (LANES // 2)
    hot = ids[:, None] == place[None, :]
    return (hot | ((place >= IDS) & (place < IDS + 3))[None, :]).astype(jnp.bfloat16)


def query_extension(ids):
    place = jnp.arange(LANES) % (LANES // 2)
    other = (place < IDS)[None, :] & (ids[:, None] != place[None, :])
    return jnp.where(other, FAR, 0.0).astype(jnp.bfloat16)


H = 12
HD = 64
LOG2E = 1.0 / LN2
PARTS = 3
eps_norm = 1e-06
bf16 = jnp.bfloat16
f32 = jnp.float32


def norm_forward(total, gain, shift):
    middle = jnp.mean(total, axis=-1, keepdims=True)
    centred = total - middle
    factor = lax.rsqrt(jnp.mean(centred * centred, axis=-1, keepdims=True) + eps_norm)
    normed = centred * factor
    return (normed * gain + shift, normed, factor)


def norm_backward(grad_out, normed, factor, gain):
    scaled = grad_out * gain
    inner = (
        scaled
        - jnp.mean(scaled, axis=-1, keepdims=True)
        - normed * jnp.mean(scaled * normed, axis=-1, keepdims=True)
    )
    return (factor * inner, jnp.sum(grad_out * normed, axis=0), jnp.sum(grad_out, axis=0))


def gelu_parts(hidden):
    normal_cdf = 0.5 * (1.0 + jax.scipy.special.erf(hidden * (1.0 / math.sqrt(2.0))))
    density = jnp.exp(-0.5 * hidden * hidden) * (1.0 / math.sqrt(2.0 * math.pi))
    return (hidden * normal_cdf, normal_cdf + hidden * density)


def dot(a, b):
    return jnp.dot(a, b, preferred_element_type=f32)


def column_sums(values):
    return jnp.sum(values.astype(f32), axis=0)


def xor_pairs(size, bits):
    return [(i, i ^ bits) for i in range(size)]


def straight(values):
    return with_layout_constraint(values, Layout(tuple(range(values.ndim))))


def pick(values, index, axis=0):
    return lax.dynamic_index_in_dim(values, index, axis, keepdims=False)


def after(values, *marks):
    return lax.optimization_barrier((values, marks))[0]


class Places:
    def __init__(self):
        self.columns = lax.axis_size("seq")
        self.shards = lax.axis_size("fsdp")
        self.column = lax.axis_index("seq")
        self.shard = lax.axis_index("fsdp")
        self.core = self.shard & 1
        self.plane = self.shard >> 1

    def mate(self, values):
        return lax.ppermute(values, "fsdp", xor_pairs(self.shards, 1))

    def across(self, values, bits):
        return lax.ppermute(values, "seq", xor_pairs(self.columns, bits))

    def aside(self, values, bits):
        return lax.ppermute(values, "fsdp", xor_pairs(self.shards, 2 * bits))


def to_sequence_parts(here, values):
    groups, piece, width = values.shape
    halves = values.reshape(groups, 2, piece // 2, width)
    kept = straight(pick(halves, here.core, 1))
    other = straight(here.mate(straight(pick(halves, 1 - here.core, 1))))
    parts = []
    for k in range(here.columns):
        want = here.column ^ k
        same = lax.div(want, groups) == here.core
        spot = lax.rem(want, groups)
        parts.append(straight(jnp.where(same, pick(kept, spot), pick(other, spot))))
    return parts


def from_sequence_send(here, slots, first=0):
    return [here.across(part, k) if k else part for k, part in enumerate(slots, first)]


def from_sequence_end(here, slots, groups):
    rows = jnp.stack(slots)

    def of(core):
        return jnp.stack([pick(rows, here.column ^ (core * groups + j)) for j in range(groups)])

    kept = of(here.core)
    other = here.mate(of(1 - here.core))
    first = here.core == 0
    return jnp.concatenate([jnp.where(first, kept, other), jnp.where(first, other, kept)], axis=1)


def place_kernel(info, *refs, moves, outs):
    count = len(moves)
    parts, full, buffers = refs[:count], refs[count : count + outs], refs[count + outs : 2 * count + outs]
    in_sem, out_sem = refs[2 * count + outs :]
    reads = [pltpu.make_async_copy(parts[k], buffers[k], in_sem.at[k]) for k in range(count)]
    for read in reads:
        read.start()
    writes = []
    for k in range(count):
        reads[k].wait()
        for j, (row, rows, cut_row, col, cols, out) in enumerate(moves[k]):
            write = pltpu.make_async_copy(
                buffers[k].at[pl.ds(cut_row, rows), pl.ds(col, cols)],
                full[out].at[info[k], pl.ds(row, rows), :],
                out_sem.at[k, j],
            )
            write.start()
            writes.append(write)
    for write in writes:
        write.wait()


def place(parts, spots, firsts, rows, cuts):
    kind = parts[0].dtype
    shards = sum(part.shape[0] for part in parts) // rows
    moves = [
        [(first, part.shape[0], 0, col, cols, out) for out, (col, cols) in enumerate(cuts)] for first, part in zip(firsts, parts)
    ]
    full = pl.pallas_call(
        functools.partial(place_kernel, moves=moves, outs=len(cuts)),
        grid_spec=pltpu.PrefetchScalarGridSpec(
            num_scalar_prefetch=1,
            grid=(),
            in_specs=[pl.BlockSpec(memory_space=pl.ANY)] * len(parts),
            out_specs=[pl.BlockSpec(memory_space=pl.ANY)] * len(cuts),
            scratch_shapes=[pltpu.VMEM(part.shape, kind) for part in parts]
            + [pltpu.SemaphoreType.DMA((len(parts),)), pltpu.SemaphoreType.DMA((len(parts), len(cuts)))],
        ),
        out_shape=[jax.ShapeDtypeStruct((shards, rows, cols), kind) for _, cols in cuts],
        cost_estimate=pl.CostEstimate(flops=0, bytes_accessed=0, transcendentals=0),
        name="place_parts",
    )(jnp.stack(spots).astype(jnp.int32), *parts)
    return [f.reshape(-1, f.shape[2]) for f in full]


def gather_direct(here, local):
    return [local] + [here.aside(local, k) for k in range(1, 4)]


def with_mates(here, parts):
    spots = [here.shard ^ (2 * k) for k in range(4)]
    return parts + [here.mate(part) for part in parts], spots + [spot ^ 1 for spot in spots]


def gather_cut(here, local, cuts, mark):
    if here.shards != 8:
        full = lax.all_gather(local, "fsdp", axis=0, tiled=True)
        return [full[:, col : col + cols] for col, cols in cuts]
    parts, spots = with_mates(here, after(gather_direct(here, local), mark))
    return place(parts, spots, [0] * 8, local.shape[0], cuts)


def pack_kernel(mix_ref, merge_ref, columns_ref, out_ref, *, size, parts):
    rows, width = merge_ref.shape
    per = LANES // size
    lane_low = lane_of(rows) < size
    pairs = width // LANES // parts
    for pair in range(width // LANES):
        part, spot = pair // pairs, pair % pairs
        for j in range(3):
            one, two = [((3 * (per * pair + k) + j) * size) // LANES * LANES for k in range(2)]
            one, two = mix_ref[:, one : one + LANES].astype(jnp.float32), mix_ref[:, two : two + LANES].astype(jnp.float32)
            if j % 2:
                joined = pltpu.roll(jnp.where(lane_low, two, one), size, 1)
            else:
                joined = jnp.where(lane_low, one, two)
            at = (part * 3 + j) * pairs * LANES + spot * LANES
            out_ref[:, at : at + LANES] = joined.astype(out_ref.dtype)
    out_ref[:, 3 * width : 4 * width] = merge_ref[...]
    out_ref[:, 4 * width :] = columns_ref[...]


def pack(mix, merge, columns, size, parts):
    rows, width = merge.shape
    return pl.pallas_call(
        functools.partial(pack_kernel, size=size, parts=parts),
        out_shape=jax.ShapeDtypeStruct((rows, 4 * width + LANES), mix.dtype),
        name="pack_projection",
    )(mix, merge, columns)


def share_pair(here, partial):
    shards, rows, width = partial.shape
    pairs = partial.reshape(shards // 2, 2, rows, width)
    return pick(pairs, here.core, 1), here.mate(pick(pairs, 1 - here.core, 1).astype(bf16))


def share_plane(here, kept, other):
    def total(k):
        spot = here.plane ^ k
        return pick(kept, spot).astype(f32) + pick(other, spot).astype(f32)

    return total(0), [here.aside(total(k).astype(bf16), k) for k in range(1, here.shards // 2)]


def share_sum(share, others):
    for other in others:
        share = share + other.astype(f32)
    return share.astype(bf16)


def column_first(here, share):
    low = share.reshape(2, share.shape[0] // 2, share.shape[1])
    side = here.column & 1
    return pick(low, side), here.across(pick(low, 1 - side), 1)


def column_second(here, half, other):
    low = (half.astype(f32) + other.astype(f32)).astype(bf16)
    step, others = 2, []
    while 2 * step < here.columns:
        low = (low.astype(f32) + here.across(low, step).astype(f32)).astype(bf16)
        step *= 2
    return low, here.across(low, step)


def column_third(here, half, other):
    half = (half.astype(f32) + other.astype(f32)).astype(bf16)
    return half, here.across(half, 1)


def column_last(here, half, other):
    first = (here.column & 1) == 0
    return jnp.concatenate([jnp.where(first, half, other), jnp.where(first, other, half)], axis=0)


def per_device(
    tokens,
    segment_ids,
    mix_weight,
    query_bias,
    value_bias,
    merge_weight,
    merge_bias,
    first_gain,
    first_shift,
    up_weight,
    up_bias,
    down_weight,
    down_bias,
    second_gain,
    second_shift,
    output_grad,
):
    here = Places()
    groups, piece, width = tokens.shape
    shards = here.shards
    own = width // shards
    hidden_size = up_weight.shape[1]
    half = piece // 2
    rows = here.columns * half
    length = here.columns * piece

    def send(parts, first=0):
        return [straight(part) for part in from_sequence_send(here, parts, first)]

    ups = hidden_size // width
    part_width = width // PARTS
    ids_sent = [segment_ids] + [here.across(segment_ids, k) for k in range(1, here.columns)]
    ids_slots = jnp.stack([pick(i, lax.rem(here.column, groups)) for i in ids_sent])
    ids_other = here.mate(ids_slots)
    ids_slots = jnp.where(lax.div(here.column, groups) == here.core, ids_slots, ids_other)
    ids_own = pick(ids_slots.reshape(here.columns, 2, half), here.core, 1)
    ids = jnp.stack([pick(ids_slots, here.column ^ k) for k in range(here.columns)]).reshape(2 * here.columns, half)
    first_id, last_id = ids[:, 0], ids[:, -1]
    low = jnp.sum(last_id[None, :] < ids_own[:, :1], axis=1)
    high = jnp.sum(first_id[None, :] <= ids_own[:, -1:], axis=1)
    info = jnp.concatenate([jnp.stack([here.core, here.column]), jnp.stack([low, high], axis=1).reshape(-1)]).astype(jnp.int32)
    key_ext = key_extension(ids.reshape(length))
    query_ext = query_extension(ids_own.reshape(rows))

    token_parts, ids_sent = lax.optimization_barrier((to_sequence_parts(here, tokens), ids_sent))
    token_slots = send(token_parts)

    vectors = (query_bias, value_bias, merge_bias, first_gain, first_shift, down_bias, second_gain, second_shift)
    local_weights = after((vectors, up_bias, mix_weight, merge_weight), token_parts)
    lines = jnp.concatenate([jnp.stack(local_weights[0]), local_weights[1].reshape(ups, own)], axis=0)
    columns = jnp.pad(lines, ((0, LANES - lines.shape[0]), (0, 0))).T
    mix_local = pack(local_weights[2], local_weights[3], columns, HD, PARTS)
    *mix_parts, merge_full, columns_full = gather_cut(
        here, mix_local, [(p * width, width) for p in range(PARTS + 1)] + [(4 * width, LANES)], token_slots[2]
    )
    lines_full = columns_full.T.astype(f32)
    query_full, value_full, merge_bias_full, gain_one, shift_one, down_bias_full, gain_two, shift_two = [
        lines_full[j] for j in range(8)
    ]
    up_bias_full = lines_full[8 : 8 + ups].reshape(ups, shards, own).transpose(1, 0, 2).reshape(-1)

    cotangent_parts = to_sequence_parts(here, after(output_grad, token_parts))
    ready = (cotangent_parts, mix_parts, merge_full, lines_full, info, key_ext, query_ext)
    token_slots, (cotangent_parts, mix_parts, merge_full, lines_full, info, key_ext, query_ext) = lax.optimization_barrier(
        (token_slots, ready)
    )
    flat = straight(jnp.concatenate(token_slots, axis=0))
    cotangent_parts = after(cotangent_parts, flat)
    cotangent_two = send(cotangent_parts[2:3], 2)
    direct = shards == 8
    up_local, down_local = after((up_weight, down_weight), mix_parts[0])
    if direct:
        packed = jnp.concatenate([up_local[:, j * width : (j + 1) * width] for j in range(ups)] + [down_local], axis=0)
        packed_parts = gather_direct(here, after(packed, flat))
    else:
        up_full, down_full = [lax.all_gather(w, "fsdp", axis=0, tiled=True) for w in (up_local, down_local)]

    column_scale = jnp.where(jnp.arange(width) < part_width, LOG2E / math.sqrt(HD), 1.0)
    mixed, mixed_mate = [], []
    for p in range(PARTS):
        of_part = slice(p * part_width, (p + 1) * part_width)
        bias = jnp.concatenate([query_full[of_part], jnp.zeros((part_width,), f32), value_full[of_part]])
        mixed.append(((dot(flat, mix_parts[p]) + bias) * column_scale).astype(bf16))
        mixed_mate.append(here.mate(mixed[p]))

    mixed, mixed_mate = lax.optimization_barrier((mixed, mixed_mate))
    contexts, exts = [], []
    plan, spots = NOTHING, ()
    for p in range(PARTS):
        if p:
            mixed[p], mixed_mate[p] = after((mixed[p], mixed_mate[p]), contexts[-1])
        if p == 1:
            mixed[p], cotangent_two = lax.optimization_barrier((mixed[p], cotangent_two))
            later = after(cotangent_parts, contexts[-1])
            cotangent_slots = send(later[:2]) + cotangent_two + send(later[3:], 3)
        if p == PARTS - 1 and direct:
            pieces, spots = with_mates(here, after(packed_parts, contexts[-1]))
            moves = [(j * own, own, 0, j * width) for j in range(ups)] + [(ups * own, ups * own, 1, 0)]
            outs = [(shards,) + up_weight.shape, (shards,) + down_weight.shape]
            plan = (pieces, tuple(moves), tuple(outs))
        context, ext, *placed = attention_forward(info, mixed[p], mixed_mate[p], query_ext, key_ext, HD, plan, spots)
        contexts.append(context)
        exts.append(ext)
    if direct:
        up_full, down_full = [full.reshape(-1, full.shape[2]) for full in placed]
    context = jnp.concatenate(contexts, axis=1)
    cotangent = jnp.concatenate(after(cotangent_slots, contexts[-1]), axis=0).astype(f32)

    attended = dot(context, merge_full) + merge_bias_full
    first_out, normed_one, factor_one = norm_forward(flat.astype(f32) + attended, gain_one, shift_one)
    first_low = first_out.astype(bf16)
    hidden = dot(first_low, up_full) + up_bias_full
    active, slope = gelu_parts(hidden)
    active_low, slope_low = lax.optimization_barrier((active.astype(bf16), slope.astype(bf16)))
    branch = dot(active_low, down_full) + down_bias_full
    result, normed_two, factor_two = norm_forward(first_out + branch, gain_two, shift_two)
    result_low = result.astype(bf16)

    grad_second, second_gain_grad, second_shift_grad = norm_backward(cotangent, normed_two, factor_two, gain_two)
    grad_branch = grad_second.astype(bf16)
    down_grad = dot(active_low.T, grad_branch)
    down_kept, down_other = share_pair(here, down_grad.reshape(shards, -1, width))
    down_bias_grad = column_sums(grad_branch)
    grad_active = dot(grad_branch, down_full.T)
    grad_hidden = (grad_active * slope_low.astype(f32)).astype(bf16)
    down_share, down_others = share_plane(here, down_kept, after(down_other, grad_hidden))
    up_grad = dot(first_low.T, grad_hidden)
    up_bias_grad = column_sums(grad_hidden)
    grad_first = grad_second + dot(grad_hidden, up_full.T)
    grad_sum, first_gain_grad, first_shift_grad = norm_backward(grad_first, normed_one, factor_one, gain_one)
    grad_attended = grad_sum.astype(bf16)
    merge_grad = dot(context.T, grad_attended)
    merge_bias_grad = column_sums(grad_attended)
    up_merge = jnp.concatenate([up_grad.reshape(shards, own, hidden_size), merge_grad.reshape(shards, own, width)], axis=2)
    up_kept, up_other = share_pair(here, up_merge)
    grad_context = dot(grad_attended, merge_full.T).astype(bf16)
    up_share, up_others = share_plane(here, up_kept, after(up_other, grad_context))

    def backward(part, grads):
        dq, kept, other = attention_backward(
            info, mixed[part], mixed_mate[part], exts[part], grads, contexts[part], key_ext, HD, part * part_width // LANES
        )
        return dq, kept, here.mate(other)

    def mixed_part(pieces):
        dq, kept, other = pieces
        kv = (kept + other.astype(f32)).astype(bf16)
        return jnp.concatenate([dq, kv[0], kv[1]], axis=1)

    one = backward(0, after(grad_context, down_share, up_share))
    down_others, down_share = after((down_others, down_share), one[0])
    down_half, down_other = column_first(here, share_sum(down_share, down_others))
    up_others, up_share = after((up_others, up_share), one[0])
    up_half, up_other = column_first(here, share_sum(up_share, up_others))
    output_slots = from_sequence_send(here, list(after(result_low, one[0]).reshape(here.columns, half, width)))
    two = backward(1, after(grad_context, down_half, up_half))
    down_half, down_other = column_second(here, *after((down_half, down_other), two[0]))
    up_half, up_other = column_second(here, *after((up_half, up_other), two[0]))
    mixed_one = mixed_part(after(one, two[0]))
    mix_grad_one = dot(flat.T, mixed_one)
    mix_kept_one, mix_other_one = share_pair(here, mix_grad_one.reshape(shards, own, -1))
    input_part = grad_sum + dot(mixed_one, mix_parts[0].T)
    mix_share_one, mix_others_one = share_plane(here, mix_kept_one, after(mix_other_one, input_part))
    three = backward(2, after(grad_context, down_half, up_half, mix_share_one, output_slots[:3]))
    down_half, down_other, up_half, up_other = after((down_half, down_other, up_half, up_other), three[0])
    mixed_two = mixed_part(after(two, three[0]))
    input_part = input_part + dot(mixed_two, mix_parts[1].T)
    mixed_three = mixed_part(after(three, input_part))
    input_low = (input_part + dot(mixed_three, mix_parts[2].T)).astype(bf16)
    input_slots = from_sequence_send(here, list(input_low.reshape(here.columns, half, width)))
    mixed_rest = after(jnp.concatenate([mixed_two, mixed_three], axis=1), input_low)
    mix_grad_rest = dot(flat.T, mixed_rest)
    down_half, down_other = column_third(here, *after((down_half, down_other), mix_grad_rest))
    up_half, up_other = column_third(here, *after((up_half, up_other), mix_grad_rest))

    sums = [column_sums(m) for m in (mixed_one, mixed_two, mixed_three)]
    query_grad = jnp.concatenate([s[:part_width] for s in sums])
    value_grad = jnp.concatenate([s[2 * part_width :] for s in sums])
    vectors = (
        query_grad,
        value_grad,
        merge_bias_grad,
        first_gain_grad,
        first_shift_grad,
        down_bias_grad,
        second_gain_grad,
        second_shift_grad,
    )
    up_lines = up_bias_grad.reshape(shards, ups, own).transpose(1, 0, 2).reshape(ups, width)
    lines_grad = jnp.concatenate([jnp.stack(vectors), up_lines], axis=0)
    columns_grad = jnp.pad(lines_grad, ((0, LANES - lines_grad.shape[0]), (0, 0))).T
    rest = jnp.concatenate([mix_grad_rest, columns_grad], axis=1).reshape(shards, own, -1)
    rest_kept, rest_other = share_pair(here, rest)
    rest_share, rest_others = share_plane(here, rest_kept, rest_other)
    mix_share = jnp.concatenate(
        [
            share_sum(mix_share_one, mix_others_one),
            share_sum(rest_share, rest_others),
        ],
        axis=1,
    )
    mix_last = column_last(here, *column_third(here, *column_second(here, *column_first(here, mix_share))))

    output = from_sequence_end(here, after(output_slots, input_low), groups)
    final_input = from_sequence_end(here, input_slots, groups).astype(f32)
    final_down = column_last(here, down_half, down_other).astype(f32)
    final_up_merge = column_last(here, up_half, up_other).astype(f32)
    final_mix = mix_last[:, : 3 * width].astype(f32).reshape(own, PARTS, 3, H // PARTS, HD)
    final_mix = final_mix.transpose(0, 1, 3, 2, 4).reshape(own, 3 * width)
    final_columns = mix_last[:, 3 * width :].astype(f32)
    finals = final_columns.T
    (
        final_query,
        final_value,
        final_merge_bias,
        final_gain_one,
        final_shift_one,
        final_down_bias,
        final_gain_two,
        final_shift_two,
    ) = [finals[j] for j in range(8)]
    final_up_bias = finals[8 : 8 + ups].reshape(-1)
    return (
        output,
        final_input,
        final_mix,
        final_query,
        final_value,
        final_up_merge[:, hidden_size:],
        final_merge_bias,
        final_gain_one,
        final_shift_one,
        final_up_merge[:, :hidden_size],
        final_up_bias,
        final_down,
        final_down_bias,
        final_gain_two,
        final_shift_two,
    )


def solution(mesh):
    wide, row, thin = P("fsdp", "seq", None), P("fsdp", None), P("fsdp")
    return jax.shard_map(
        per_device,
        mesh=mesh,
        in_specs=(wide, P("fsdp", "seq"), row, thin, thin, row, thin, thin, thin, row, thin, row, thin, thin, thin, wide),
        out_specs=(wide, wide, row, thin, thin, row, thin, thin, thin, row, thin, row, thin, thin, thin),
        check_vma=False,
    )
```

```python
import functools, math
import jax, jax.numpy as jnp
from jax import lax
from jax.experimental import pallas as pl
from jax.experimental.layout import Layout, with_layout_constraint
from jax.experimental.pallas import tpu as pltpu
from jax.sharding import PartitionSpec as P

LANES = 128
FAR = -1000000000.0
IDS = 4
LN2 = math.log(2.0)


def nt(a, b):
    return lax.dot_general(a, b, (((1,), (1,)), ((), ())), preferred_element_type=jnp.float32)


def nn(a, b):
    return lax.dot_general(a, b, (((1,), (0,)), ((), ())), preferred_element_type=jnp.float32)


def lane_of(rows):
    return lax.broadcasted_iota(jnp.int32, (rows, LANES), 1)


def split3(x):
    high = x.astype(jnp.bfloat16).astype(jnp.float32)
    middle = (x - high).astype(jnp.bfloat16).astype(jnp.float32)
    return high, middle, x - high - middle


def gather_blocks(info, block, count, own_ref, mate_ref, put):
    for b in range(count):
        start = pl.multiple_of(((b // 2) ^ info[1]) * block, block)

        @pl.when(info[0] == b % 2)
        def _():
            put(b, own_ref[pl.ds(start, block), :])

        @pl.when(info[0] != b % 2)
        def _():
            put(b, mate_ref[pl.ds(start, block), :])


def forward_kernel(info, q_ref, k_own, k_mate, v_own, v_mate, qx_ref, kx_ref, *refs, size, plan):
    count, moves, outs = plan
    beside, (out_ref, ext_ref), full = refs[:count], refs[count : count + 2], refs[count + 2 : count + 2 + len(outs)]
    k_all, vt_all, s_all, *buffers = refs[count + 2 + len(outs) :]
    slot = pl.program_id(1)
    if count:
        in_sem, out_sem = buffers[count:]
        reads = [pltpu.make_async_copy(beside[j], buffers[j], in_sem.at[j]) for j in range(count)]
        writes = [
            pltpu.make_async_copy(
                buffers[j].at[pl.ds(row, rows), :],
                full[out].at[info[info.shape[0] - count + j], :, pl.ds(col, buffers[j].shape[1])],
                out_sem.at[j, k],
            )
            for j in range(count)
            for k, (row, rows, out, col) in enumerate(moves)
        ]
        at = pl.program_id(0) * pl.num_programs(1) + slot

        @pl.when(at == 0)
        def _():
            for read in reads:
                read.start()

        @pl.when(at == 2)
        def _():
            for read in reads:
                read.wait()
            for write in writes:
                write.start()

        @pl.when(at == pl.num_programs(0) * pl.num_programs(1) - 1)
        def _():
            for write in writes:
                write.wait()

    block = q_ref.shape[0]
    count = kx_ref.shape[0] // block
    heads = LANES // size
    lane_head = lane_of(block) // size

    @pl.when(slot == 0)
    def _():
        def put_k(b, rows):
            ext = kx_ref[b * block : (b + 1) * block, :]
            for h in range(heads):
                k_all[h, b * block : (b + 1) * block, :] = jnp.where(lane_head == h, rows, ext)

        def put_v(b, rows):
            turned = rows.T
            for h in range(heads):
                vt_all[h, :size, b * block : (b + 1) * block] = turned[h * size : (h + 1) * size]

        gather_blocks(info, block, count, k_own, k_mate, put_k)
        gather_blocks(info, block, count, v_own, v_mate, put_v)
        for h in range(heads):
            vt_all[h, size:, :] = jnp.ones((vt_all.shape[1] - size, vt_all.shape[2]), vt_all.dtype)

    rows = q_ref[...]
    qx = qx_ref[...]
    queries = [jnp.where(lane_head == h, rows, qx) for h in range(heads)]

    part = block
    lo, hi = info[2 + 2 * slot], info[3 + 2 * slot]

    def score(h, kb, i, top):
        at = pl.multiple_of(kb * block + i * part, part)
        st = nt(k_all[h, pl.ds(at, part), :], queries[h])
        s_all[h, i * part : (i + 1) * part, :] = st
        return jnp.maximum(top, jnp.max(st.reshape(part // 8, 8, block), axis=0))

    def weigh(h, kb, i, m, acc):
        at = pl.multiple_of(kb * block + i * part, part)
        p = jnp.exp2(s_all[h, i * part : (i + 1) * part, :] - m).astype(jnp.bfloat16)
        return acc + nn(vt_all[h, :, pl.ds(at, part)], p)

    least = jnp.full((8, block), -jnp.inf, jnp.float32)

    def step(kb, carry):
        tops, state = carry
        tops, state = list(tops), list(state)
        after = jnp.minimum(kb + 1, count - 1)
        for h in range(heads):
            ahead = (h + 1) % heads
            ahead_kb = kb if ahead else after
            m, acc = state[h]
            m_new = jnp.maximum(m, jnp.max(tops[h], axis=0, keepdims=True))
            acc = acc * jnp.exp2(m - m_new)
            top = least
            for i in range(1):
                top = score(ahead, ahead_kb, i, top)
                acc = weigh(h, kb, i, m_new, acc)
            tops[ahead] = top
            state[h] = (m_new, acc)
        return tuple(tops), tuple(state)

    start = tuple(
        (jnp.full((1, block), -jnp.inf, jnp.float32), jnp.zeros((vt_all.shape[1], block), jnp.float32))
        for _ in range(heads)
    )
    first = score(0, lo, 0, least)
    _, done = lax.fori_loop(lo, hi, step, ((first,) + (least,) * (heads - 1), start))
    sums = [acc[size : size + 1] for _, acc in done]
    out_t = jnp.concatenate([acc[:size] * (1.0 / l) for (_, acc), l in zip(done, sums)], axis=0)
    out_ref[...] = out_t.T.astype(out_ref.dtype)
    row = lax.broadcasted_iota(jnp.int32, (size, block), 0)
    parts = []
    for (m, _), l in zip(done, sums):
        pieces = split3(-(m + jnp.log2(l)))
        part = jnp.zeros((size, block), jnp.float32)
        for j, piece in enumerate(pieces):
            part = jnp.where(row == IDS + j, piece, part)
        parts.append(part)
    ext_ref[...] = (jnp.concatenate(parts[::-1], axis=0).T + qx.astype(jnp.float32)).astype(ext_ref.dtype)


NOTHING = ((), (), ())


def attention_forward(info, own, mate, qx, kx, size, plan=NOTHING, spots=()):
    rows, width = own.shape[0], own.shape[1] // 3
    length = kx.shape[0]
    slots = (info.shape[0] - 2) // 2
    block = rows // slots
    pairs = width // LANES
    heads = LANES // size
    pieces, moves, outs = plan
    if pieces:
        info = jnp.concatenate([info, jnp.stack(spots).astype(jnp.int32)])
    anywhere = pl.BlockSpec(memory_space=pl.ANY)
    return pl.pallas_call(
        functools.partial(forward_kernel, size=size, plan=(len(pieces), moves, outs)),
        grid_spec=pltpu.PrefetchScalarGridSpec(
            num_scalar_prefetch=1,
            grid=(pairs, slots),
            in_specs=[
                pl.BlockSpec((block, LANES), lambda p, s, i: (s, p)),
                pl.BlockSpec((rows, LANES), lambda p, s, i: (0, pairs + p)),
                pl.BlockSpec((rows, LANES), lambda p, s, i: (0, pairs + p)),
                pl.BlockSpec((rows, LANES), lambda p, s, i: (0, 2 * pairs + p)),
                pl.BlockSpec((rows, LANES), lambda p, s, i: (0, 2 * pairs + p)),
                pl.BlockSpec((block, LANES), lambda p, s, i: (s, 0)),
                pl.BlockSpec((length, LANES), lambda p, s, i: (0, 0)),
            ]
            + [anywhere] * len(pieces),
            out_specs=[pl.BlockSpec((block, LANES), lambda p, s, i: (s, p))] * 2 + [anywhere] * len(outs),
            scratch_shapes=[
                pltpu.VMEM((heads, length, LANES), jnp.bfloat16),
                pltpu.VMEM((heads, size + 16, length), jnp.bfloat16),
                pltpu.VMEM((heads, block, block), jnp.float32),
            ]
            + [pltpu.VMEM(piece.shape, piece.dtype) for piece in pieces]
            + [pltpu.SemaphoreType.DMA((len(pieces),)), pltpu.SemaphoreType.DMA((len(pieces), len(moves)))] * bool(pieces),
        ),
        out_shape=[jax.ShapeDtypeStruct((rows, width), jnp.bfloat16)] * 2
        + [jax.ShapeDtypeStruct(shape, jnp.bfloat16) for shape in outs],
        compiler_params=pltpu.CompilerParams(dimension_semantics=("arbitrary", "arbitrary")),
        cost_estimate=pl.CostEstimate(
            flops=2 * rows * length * width, bytes_accessed=8 * rows * width * 2, transcendentals=rows * length * pairs
        ),
        name="attention_forward",
    )(info, own, own, mate, own, mate, qx, kx, *pieces)


def backward_kernel(
    info, q_ref, ext_ref, do_ref, ctx_ref, k_own, k_mate, v_own, v_mate, kx_ref,
    dq_ref, own_ref, mate_ref, k_all, kt_all, v_all, dk_all, dv_all, *, size
):
    slot = pl.program_id(1)
    block = q_ref.shape[0]
    count = kx_ref.shape[0] // block
    heads = LANES // size
    lane = lane_of(block)
    lane_head = lane // size
    place = lane % size
    three = (place >= IDS) & (place < IDS + 3)

    @pl.when(slot == 0)
    def _():
        def put_k(b, rows):
            ext = kx_ref[b * block : (b + 1) * block, :]
            for h in range(heads):
                k_all[h, b * block : (b + 1) * block, :] = jnp.where(lane_head == h, rows, ext)
            kt_all[:, b * block : (b + 1) * block] = rows.T

        def put_v(b, rows):
            one = three.astype(rows.dtype)
            for h in range(heads):
                v_all[h, b * block : (b + 1) * block, :] = jnp.where(lane_head == h, rows, one)

        gather_blocks(info, block, count, k_own, k_mate, put_k)
        gather_blocks(info, block, count, v_own, v_mate, put_v)
        dk_all[...] = jnp.zeros_like(dk_all)
        dv_all[...] = jnp.zeros_like(dv_all)

    rows = q_ref[...]
    ext = ext_ref[...]
    grads = do_ref[...]
    zero = jnp.zeros_like(rows)
    queries = [jnp.where(lane_head == h, rows, ext) for h in range(heads)]
    plain_q = jnp.concatenate([jnp.where(lane_head == h, rows, zero) for h in range(heads)], axis=0)
    plain_do = jnp.concatenate([jnp.where(lane_head == h, grads, zero) for h in range(heads)], axis=0)
    product = grads.astype(jnp.float32) * ctx_ref[...].astype(jnp.float32)
    outs = []
    for h in range(heads):
        delta = jnp.sum(jnp.where(lane_head == h, product, 0.0), axis=1, keepdims=True)
        wide = jnp.zeros((block, LANES), jnp.float32)
        for j, piece in enumerate(split3(-delta)):
            wide = jnp.where(place == IDS + j, piece, wide)
        outs.append(jnp.where(lane_head == h, grads, wide.astype(grads.dtype)))

    def step(kb, carry):
        start = pl.multiple_of(kb * block, block)
        probs, scores, fresh = [], [], []
        for h in range(heads):
            p = jnp.exp2(nt(k_all[h, pl.ds(start, block), :], queries[h]))
            ds = (p * nt(v_all[h, pl.ds(start, block), :], outs[h])).astype(jnp.bfloat16)
            probs.append(p.astype(jnp.bfloat16))
            scores.append(ds)
            fresh.append(carry[h] + nn(kt_all[h * size : (h + 1) * size, pl.ds(start, block)], ds))
        dv_all[pl.ds(start, block), :] += nn(jnp.concatenate(probs, axis=1), plain_do)
        dk_all[pl.ds(start, block), :] += nn(jnp.concatenate(scores, axis=1), plain_q)
        return tuple(fresh)

    dq = lax.fori_loop(
        info[2 + 2 * slot], info[3 + 2 * slot], step,
        tuple(jnp.zeros((size, block), jnp.float32) for _ in range(heads)),
    )
    dq_ref[...] = (jnp.concatenate(dq, axis=0) * (1.0 / math.sqrt(size))).T.astype(dq_ref.dtype)

    @pl.when(slot == pl.num_programs(1) - 1)
    def _():
        for b in range(count):
            spot = pl.multiple_of(((b // 2) ^ info[1]) * block, block)
            for j, (total, factor) in enumerate(((dk_all, LN2), (dv_all, 1.0))):

                @pl.when(info[0] == b % 2)
                def _():
                    own_ref[j, pl.ds(spot, block), :] = (total[pl.ds(b * block, block), :] * factor).astype(own_ref.dtype)

                @pl.when(info[0] != b % 2)
                def _():
                    mate_ref[j, pl.ds(spot, block), :] = (total[pl.ds(b * block, block), :] * factor).astype(mate_ref.dtype)


def attention_backward(info, own, mate, ext, grads, ctx, kx, size, first):
    rows, width = ctx.shape
    length = kx.shape[0]
    slots = (info.shape[0] - 2) // 2
    block = rows // slots
    pairs = width // LANES
    heads = LANES // size
    tile = pl.BlockSpec((block, LANES), lambda p, s, i: (s, p))
    return pl.pallas_call(
        functools.partial(backward_kernel, size=size),
        grid_spec=pltpu.PrefetchScalarGridSpec(
            num_scalar_prefetch=1,
            grid=(pairs, slots),
            in_specs=[
                tile,
                tile,
                pl.BlockSpec((block, LANES), lambda p, s, i: (s, first + p)),
                tile,
                pl.BlockSpec((rows, LANES), lambda p, s, i: (0, pairs + p)),
                pl.BlockSpec((rows, LANES), lambda p, s, i: (0, pairs + p)),
                pl.BlockSpec((rows, LANES), lambda p, s, i: (0, 2 * pairs + p)),
                pl.BlockSpec((rows, LANES), lambda p, s, i: (0, 2 * pairs + p)),
                pl.BlockSpec((length, LANES), lambda p, s, i: (0, 0)),
            ],
            out_specs=[
                tile,
                pl.BlockSpec((2, rows, LANES), lambda p, s, i: (0, 0, p)),
                pl.BlockSpec((2, rows, LANES), lambda p, s, i: (0, 0, p)),
            ],
            scratch_shapes=[
                pltpu.VMEM((heads, length, LANES), jnp.bfloat16),
                pltpu.VMEM((LANES, length), jnp.bfloat16),
                pltpu.VMEM((heads, length, LANES), jnp.bfloat16),
                pltpu.VMEM((length, LANES), jnp.float32),
                pltpu.VMEM((length, LANES), jnp.float32),
            ],
        ),
        out_shape=[
            jax.ShapeDtypeStruct((rows, width), jnp.bfloat16),
            jax.ShapeDtypeStruct((2, rows, width), jnp.float32),
            jax.ShapeDtypeStruct((2, rows, width), jnp.bfloat16),
        ],
        compiler_params=pltpu.CompilerParams(dimension_semantics=("arbitrary", "arbitrary")),
        cost_estimate=pl.CostEstimate(
            flops=5 * rows * length * width, bytes_accessed=24 * rows * width, transcendentals=rows * length * pairs
        ),
        name="attention_backward",
    )(info, own, ext, grads, ctx, own, mate, own, mate, kx)


def key_extension(ids):
    place = jnp.arange(LANES) % (LANES // 2)
    hot = ids[:, None] == place[None, :]
    return (hot | ((place >= IDS) & (place < IDS + 3))[None, :]).astype(jnp.bfloat16)


def query_extension(ids):
    place = jnp.arange(LANES) % (LANES // 2)
    other = (place < IDS)[None, :] & (ids[:, None] != place[None, :])
    return jnp.where(other, FAR, 0.0).astype(jnp.bfloat16)


H = 12
HD = 64
LOG2E = 1.0 / LN2
PARTS = 3
eps_norm = 1e-06
bf16 = jnp.bfloat16
f32 = jnp.float32


def norm_forward(total, gain, shift):
    middle = jnp.mean(total, axis=-1, keepdims=True)
    centred = total - middle
    factor = lax.rsqrt(jnp.mean(centred * centred, axis=-1, keepdims=True) + eps_norm)
    normed = centred * factor
    return (normed * gain + shift, normed, factor)


def norm_backward(grad_out, normed, factor, gain):
    scaled = grad_out * gain
    inner = (
        scaled
        - jnp.mean(scaled, axis=-1, keepdims=True)
        - normed * jnp.mean(scaled * normed, axis=-1, keepdims=True)
    )
    return (factor * inner, jnp.sum(grad_out * normed, axis=0), jnp.sum(grad_out, axis=0))


def gelu_parts(hidden):
    normal_cdf = 0.5 * (1.0 + jax.scipy.special.erf(hidden * (1.0 / math.sqrt(2.0))))
    density = jnp.exp(-0.5 * hidden * hidden) * (1.0 / math.sqrt(2.0 * math.pi))
    return (hidden * normal_cdf, normal_cdf + hidden * density)


def dot(a, b):
    return jnp.dot(a, b, preferred_element_type=f32)


def column_sums(values):
    return jnp.sum(values.astype(f32), axis=0)


def xor_pairs(size, bits):
    return [(i, i ^ bits) for i in range(size)]


def straight(values):
    return with_layout_constraint(values, Layout(tuple(range(values.ndim))))


def pick(values, index, axis=0):
    return lax.dynamic_index_in_dim(values, index, axis, keepdims=False)


def after(values, *marks):
    return lax.optimization_barrier((values, marks))[0]


class Places:
    def __init__(self):
        self.columns = lax.axis_size("seq")
        self.shards = lax.axis_size("fsdp")
        self.column = lax.axis_index("seq")
        self.shard = lax.axis_index("fsdp")
        self.core = self.shard & 1
        self.plane = self.shard >> 1

    def mate(self, values):
        return lax.ppermute(values, "fsdp", xor_pairs(self.shards, 1))

    def across(self, values, bits):
        return lax.ppermute(values, "seq", xor_pairs(self.columns, bits))

    def aside(self, values, bits):
        return lax.ppermute(values, "fsdp", xor_pairs(self.shards, 2 * bits))


def to_sequence_parts(here, values):
    groups, piece, width = values.shape
    halves = values.reshape(groups, 2, piece // 2, width)
    kept = straight(pick(halves, here.core, 1))
    other = straight(here.mate(straight(pick(halves, 1 - here.core, 1))))
    parts = []
    for k in range(here.columns):
        want = here.column ^ k
        same = lax.div(want, groups) == here.core
        spot = lax.rem(want, groups)
        parts.append(straight(jnp.where(same, pick(kept, spot), pick(other, spot))))
    return parts


def from_sequence_send(here, slots, first=0):
    return [here.across(part, k) if k else part for k, part in enumerate(slots, first)]


def from_sequence_end(here, slots, groups):
    rows = jnp.stack(slots)

    def of(core):
        return jnp.stack([pick(rows, here.column ^ (core * groups + j)) for j in range(groups)])

    kept = of(here.core)
    other = here.mate(of(1 - here.core))
    first = here.core == 0
    return jnp.concatenate([jnp.where(first, kept, other), jnp.where(first, other, kept)], axis=1)


def place_kernel(info, *refs, moves, outs):
    count = len(moves)
    parts, full, buffers = refs[:count], refs[count : count + outs], refs[count + outs : 2 * count + outs]
    in_sem, out_sem = refs[2 * count + outs :]
    reads = [pltpu.make_async_copy(parts[k], buffers[k], in_sem.at[k]) for k in range(count)]
    for read in reads:
        read.start()
    writes = []
    for k in range(count):
        reads[k].wait()
        for j, (row, rows, cut_row, col, cols, out) in enumerate(moves[k]):
            write = pltpu.make_async_copy(
                buffers[k].at[pl.ds(cut_row, rows), pl.ds(col, cols)],
                full[out].at[info[k], pl.ds(row, rows), :],
                out_sem.at[k, j],
            )
            write.start()
            writes.append(write)
    for write in writes:
        write.wait()


def place(parts, spots, firsts, rows, cuts):
    kind = parts[0].dtype
    shards = sum(part.shape[0] for part in parts) // rows
    moves = [
        [(first, part.shape[0], 0, col, cols, out) for out, (col, cols) in enumerate(cuts)] for first, part in zip(firsts, parts)
    ]
    full = pl.pallas_call(
        functools.partial(place_kernel, moves=moves, outs=len(cuts)),
        grid_spec=pltpu.PrefetchScalarGridSpec(
            num_scalar_prefetch=1,
            grid=(),
            in_specs=[pl.BlockSpec(memory_space=pl.ANY)] * len(parts),
            out_specs=[pl.BlockSpec(memory_space=pl.ANY)] * len(cuts),
            scratch_shapes=[pltpu.VMEM(part.shape, kind) for part in parts]
            + [pltpu.SemaphoreType.DMA((len(parts),)), pltpu.SemaphoreType.DMA((len(parts), len(cuts)))],
        ),
        out_shape=[jax.ShapeDtypeStruct((shards, rows, cols), kind) for _, cols in cuts],
        cost_estimate=pl.CostEstimate(flops=0, bytes_accessed=0, transcendentals=0),
        name="place_parts",
    )(jnp.stack(spots).astype(jnp.int32), *parts)
    return [f.reshape(-1, f.shape[2]) for f in full]


def gather_direct(here, local):
    return [local] + [here.aside(local, k) for k in range(1, 4)]


def with_mates(here, parts):
    spots = [here.shard ^ (2 * k) for k in range(4)]
    return parts + [here.mate(part) for part in parts], spots + [spot ^ 1 for spot in spots]


def gather_cut(here, local, cuts, mark):
    if here.shards != 8:
        full = lax.all_gather(local, "fsdp", axis=0, tiled=True)
        return [full[:, col : col + cols] for col, cols in cuts]
    parts, spots = with_mates(here, after(gather_direct(here, local), mark))
    return place(parts, spots, [0] * 8, local.shape[0], cuts)


def pack_kernel(mix_ref, merge_ref, columns_ref, out_ref, *, size, parts):
    rows, width = merge_ref.shape
    per = LANES // size
    lane_low = lane_of(rows) < size
    pairs = width // LANES // parts
    for pair in range(width // LANES):
        part, spot = pair // pairs, pair % pairs
        for j in range(3):
            one, two = [((3 * (per * pair + k) + j) * size) // LANES * LANES for k in range(2)]
            one, two = mix_ref[:, one : one + LANES].astype(jnp.float32), mix_ref[:, two : two + LANES].astype(jnp.float32)
            if j % 2:
                joined = pltpu.roll(jnp.where(lane_low, two, one), size, 1)
            else:
                joined = jnp.where(lane_low, one, two)
            at = (part * 3 + j) * pairs * LANES + spot * LANES
            out_ref[:, at : at + LANES] = joined.astype(out_ref.dtype)
    out_ref[:, 3 * width : 4 * width] = merge_ref[...]
    out_ref[:, 4 * width :] = columns_ref[...]


def pack(mix, merge, columns, size, parts):
    rows, width = merge.shape
    return pl.pallas_call(
        functools.partial(pack_kernel, size=size, parts=parts),
        out_shape=jax.ShapeDtypeStruct((rows, 4 * width + LANES), mix.dtype),
        name="pack_projection",
    )(mix, merge, columns)


def share_pair(here, partial):
    shards, rows, width = partial.shape
    pairs = partial.reshape(shards // 2, 2, rows, width)
    return pick(pairs, here.core, 1), here.mate(pick(pairs, 1 - here.core, 1).astype(bf16))


def share_plane(here, kept, other):
    def total(k):
        spot = here.plane ^ k
        return pick(kept, spot).astype(f32) + pick(other, spot).astype(f32)

    return total(0), [total(k).astype(bf16) for k in range(1, here.shards // 2)]


def share_send(here, lows):
    others = []
    for k, low in enumerate(lows, 1):
        others.append(here.aside(after(low, others[k - 3]) if k > 2 else low, k))
    return others


def share_sum(share, others):
    for other in others:
        share = share + other.astype(f32)
    return share.astype(bf16)


def column_first(here, share):
    low = share.reshape(2, share.shape[0] // 2, share.shape[1])
    side = here.column & 1
    return pick(low, side), here.across(pick(low, 1 - side), 1)


def column_second(here, half, other):
    low = (half.astype(f32) + other.astype(f32)).astype(bf16)
    step, others = 2, []
    while 2 * step < here.columns:
        low = (low.astype(f32) + here.across(low, step).astype(f32)).astype(bf16)
        step *= 2
    return low, here.across(low, step)


def column_third(here, half, other):
    half = (half.astype(f32) + other.astype(f32)).astype(bf16)
    return half, here.across(half, 1)


def column_last(here, half, other):
    first = (here.column & 1) == 0
    return jnp.concatenate([jnp.where(first, half, other), jnp.where(first, other, half)], axis=0)


def per_device(
    tokens,
    segment_ids,
    mix_weight,
    query_bias,
    value_bias,
    merge_weight,
    merge_bias,
    first_gain,
    first_shift,
    up_weight,
    up_bias,
    down_weight,
    down_bias,
    second_gain,
    second_shift,
    output_grad,
):
    here = Places()
    groups, piece, width = tokens.shape
    shards = here.shards
    own = width // shards
    hidden_size = up_weight.shape[1]
    half = piece // 2
    rows = here.columns * half
    length = here.columns * piece

    def send(parts, first=0):
        return [straight(part) for part in from_sequence_send(here, parts, first)]

    ups = hidden_size // width
    part_width = width // PARTS
    ids_sent = [segment_ids] + [here.across(segment_ids, k) for k in range(1, here.columns)]
    ids_slots = jnp.stack([pick(i, lax.rem(here.column, groups)) for i in ids_sent])
    ids_other = here.mate(ids_slots)
    ids_slots = jnp.where(lax.div(here.column, groups) == here.core, ids_slots, ids_other)
    ids_own = pick(ids_slots.reshape(here.columns, 2, half), here.core, 1)
    ids = jnp.stack([pick(ids_slots, here.column ^ k) for k in range(here.columns)]).reshape(2 * here.columns, half)
    first_id, last_id = ids[:, 0], ids[:, -1]
    low = jnp.sum(last_id[None, :] < ids_own[:, :1], axis=1)
    high = jnp.sum(first_id[None, :] <= ids_own[:, -1:], axis=1)
    info = jnp.concatenate([jnp.stack([here.core, here.column]), jnp.stack([low, high], axis=1).reshape(-1)]).astype(jnp.int32)
    key_ext = key_extension(ids.reshape(length))
    query_ext = query_extension(ids_own.reshape(rows))

    token_parts, ids_sent = lax.optimization_barrier((to_sequence_parts(here, tokens), ids_sent))
    token_slots = send(token_parts)

    vectors = (query_bias, value_bias, merge_bias, first_gain, first_shift, down_bias, second_gain, second_shift)
    local_weights = after((vectors, up_bias, mix_weight, merge_weight), ids_sent)
    lines = jnp.concatenate([jnp.stack(local_weights[0]), local_weights[1].reshape(ups, own)], axis=0)
    columns = jnp.pad(lines, ((0, LANES - lines.shape[0]), (0, 0))).T
    mix_local = pack(local_weights[2], local_weights[3], columns, HD, PARTS)
    *mix_parts, merge_full, columns_full = gather_cut(
        here, mix_local, [(p * width, width) for p in range(PARTS + 1)] + [(4 * width, LANES)], token_slots[2:]
    )
    lines_full = columns_full.T.astype(f32)
    query_full, value_full, merge_bias_full, gain_one, shift_one, down_bias_full, gain_two, shift_two = [
        lines_full[j] for j in range(8)
    ]
    up_bias_full = lines_full[8 : 8 + ups].reshape(ups, shards, own).transpose(1, 0, 2).reshape(-1)

    cotangent_parts = to_sequence_parts(here, after(output_grad, token_parts))
    ready = (cotangent_parts, mix_parts, merge_full, lines_full, info, key_ext, query_ext)
    token_slots, (cotangent_parts, mix_parts, merge_full, lines_full, info, key_ext, query_ext) = lax.optimization_barrier(
        (token_slots, ready)
    )
    flat = straight(jnp.concatenate(token_slots, axis=0))
    cotangent_parts = after(cotangent_parts, flat)
    cotangent_two = send(cotangent_parts[2:3], 2)
    direct = shards == 8
    up_local, down_local = after((up_weight, down_weight), mix_parts[0])
    if direct:
        packed = jnp.concatenate([up_local[:, j * width : (j + 1) * width] for j in range(ups)] + [down_local], axis=0)
        packed_parts = gather_direct(here, after(packed, flat))
    else:
        up_full, down_full = [lax.all_gather(w, "fsdp", axis=0, tiled=True) for w in (up_local, down_local)]

    column_scale = jnp.where(jnp.arange(width) < part_width, LOG2E / math.sqrt(HD), 1.0)
    mixed, mixed_mate = [], []
    for p in range(PARTS):
        of_part = slice(p * part_width, (p + 1) * part_width)
        bias = jnp.concatenate([query_full[of_part], jnp.zeros((part_width,), f32), value_full[of_part]])
        mixed.append(((dot(flat, mix_parts[p]) + bias) * column_scale).astype(bf16))
        mixed_mate.append(here.mate(mixed[p]))

    mixed, mixed_mate = lax.optimization_barrier((mixed, mixed_mate))
    contexts, exts = [], []
    plan, spots = NOTHING, ()
    for p in range(PARTS):
        if p:
            mixed[p], mixed_mate[p] = after((mixed[p], mixed_mate[p]), contexts[-1])
        if p == 1:
            mixed[p], cotangent_two = lax.optimization_barrier((mixed[p], cotangent_two))
            later = after(cotangent_parts, contexts[-1])
            cotangent_slots = send(later[:2]) + cotangent_two + send(later[3:], 3)
        if p == PARTS - 1 and direct:
            pieces, spots = with_mates(here, after(packed_parts, contexts[-1]))
            moves = [(j * own, own, 0, j * width) for j in range(ups)] + [(ups * own, ups * own, 1, 0)]
            outs = [(shards,) + up_weight.shape, (shards,) + down_weight.shape]
            plan = (pieces, tuple(moves), tuple(outs))
        context, ext, *placed = attention_forward(info, mixed[p], mixed_mate[p], query_ext, key_ext, HD, plan, spots)
        contexts.append(context)
        exts.append(ext)
    if direct:
        up_full, down_full = [full.reshape(-1, full.shape[2]) for full in placed]
    context = jnp.concatenate(contexts, axis=1)
    cotangent = jnp.concatenate(after(cotangent_slots, contexts[-1]), axis=0).astype(f32)

    attended = dot(context, merge_full) + merge_bias_full
    first_out, normed_one, factor_one = norm_forward(flat.astype(f32) + attended, gain_one, shift_one)
    first_low = first_out.astype(bf16)
    hidden = dot(first_low, up_full) + up_bias_full
    active, slope = gelu_parts(hidden)
    active_low, slope_low = lax.optimization_barrier((active.astype(bf16), slope.astype(bf16)))
    branch = dot(active_low, down_full) + down_bias_full
    result, normed_two, factor_two = norm_forward(first_out + branch, gain_two, shift_two)
    result_low = list(result.astype(bf16).reshape(here.columns, half, width))
    output_far = from_sequence_send(here, result_low[3:], 3)

    grad_second, second_gain_grad, second_shift_grad = norm_backward(cotangent, normed_two, factor_two, gain_two)
    grad_branch = grad_second.astype(bf16)
    down_grad = dot(active_low.T, grad_branch).astype(bf16)
    down_kept, down_other = share_pair(here, down_grad.reshape(shards, -1, width))
    down_bias_grad = column_sums(grad_branch)
    grad_active = dot(grad_branch, down_full.T)
    grad_hidden = (grad_active * slope_low.astype(f32)).astype(bf16)
    down_share, down_lows = share_plane(here, down_kept, after(down_other, grad_hidden))
    grad_hidden, down_lows = lax.optimization_barrier((grad_hidden, down_lows))
    down_others = share_send(here, down_lows)
    up_grad = dot(first_low.T, grad_hidden).astype(bf16)
    up_bias_grad = column_sums(grad_hidden)
    grad_first = grad_second + dot(grad_hidden, up_full.T)
    grad_sum, first_gain_grad, first_shift_grad = norm_backward(grad_first, normed_one, factor_one, gain_one)
    grad_attended, down_others[0] = lax.optimization_barrier((grad_sum.astype(bf16), down_others[0]))
    merge_grad = dot(context.T, grad_attended).astype(bf16)
    merge_bias_grad = column_sums(grad_attended)
    up_merge = jnp.concatenate([up_grad.reshape(shards, own, hidden_size), merge_grad.reshape(shards, own, width)], axis=2)
    up_kept, up_other = share_pair(here, up_merge)
    grad_context = dot(grad_attended, merge_full.T).astype(bf16)
    up_share, up_lows = share_plane(here, up_kept, after(up_other, grad_context))
    up_others = share_send(here, up_lows)

    def backward(part, grads):
        dq, kept, other = attention_backward(
            info, mixed[part], mixed_mate[part], exts[part], grads, contexts[part], key_ext, HD, part * part_width // LANES
        )
        return dq, kept, here.mate(other)

    def mixed_part(pieces):
        dq, kept, other = pieces
        kv = (kept + other.astype(f32)).astype(bf16)
        return jnp.concatenate([dq, kv[0], kv[1]], axis=1)

    one = backward(0, after(grad_context, down_share, up_share))
    down_others, down_share = after((down_others, down_share), one[0])
    down_half, down_other = column_first(here, share_sum(down_share, down_others))
    up_others, up_share = after((up_others, up_share), one[0])
    up_half, up_other = column_first(here, share_sum(up_share, up_others))
    grad_context, output_far = lax.optimization_barrier((after(grad_context, one[0]), output_far))
    output_slots = from_sequence_send(here, after(result_low[:3], one[0])) + output_far
    two = backward(1, after(grad_context, down_half, up_half))
    one, up_half, up_other = after((one, up_half, up_other), two[0])
    mixed_one = mixed_part(one)
    down_half, down_other = column_second(here, *after((down_half, down_other), two[0]))
    up_half, up_other = column_second(here, up_half, up_other)
    input_part = grad_sum + dot(mixed_one, mix_parts[0].T)
    three = backward(2, after(grad_context, down_half, up_half, input_part, output_slots[:3]))
    two, down_half, down_other, up_half, up_other = after((two, down_half, down_other, up_half, up_other), three[0])
    mixed_two = mixed_part(two)
    input_part = input_part + dot(mixed_two, mix_parts[1].T)
    mixed_three = mixed_part(after(three, input_part))
    input_low = (input_part + dot(mixed_three, mix_parts[2].T)).astype(bf16)
    input_slots = from_sequence_send(here, list(input_low.reshape(here.columns, half, width)))
    mixed_all = after(jnp.concatenate([mixed_one, mixed_two, mixed_three], axis=1), input_low)
    mix_grad = dot(flat.T, mixed_all).astype(bf16)

    sums = [column_sums(m) for m in (mixed_one, mixed_two, mixed_three)]
    query_grad = jnp.concatenate([s[:part_width] for s in sums])
    value_grad = jnp.concatenate([s[2 * part_width :] for s in sums])
    vectors = (
        query_grad,
        value_grad,
        merge_bias_grad,
        first_gain_grad,
        first_shift_grad,
        down_bias_grad,
        second_gain_grad,
        second_shift_grad,
    )
    up_lines = up_bias_grad.reshape(shards, ups, own).transpose(1, 0, 2).reshape(ups, width)
    lines_grad = jnp.concatenate([jnp.stack(vectors), up_lines], axis=0)
    columns_grad = jnp.pad(lines_grad, ((0, LANES - lines_grad.shape[0]), (0, 0))).T
    whole = jnp.concatenate([mix_grad, columns_grad.astype(bf16)], axis=1).reshape(shards, own, -1)
    mix_share, mix_lows = share_plane(here, *share_pair(here, whole))
    mix_others = share_send(here, mix_lows)
    input_mark = mix_others[0]
    mix_share = share_sum(mix_share, mix_others)
    mix_half, mix_other = column_first(here, mix_share)
    down_half, down_other = column_third(here, *after((down_half, down_other), mix_share))
    up_half, up_other = column_third(here, *after((up_half, up_other), mix_share))
    mix_half, mix_other = column_second(here, mix_half, mix_other)
    down_half, down_other, up_half, up_other = after((down_half, down_other, up_half, up_other), mix_half)
    mix_last = column_last(here, *column_third(here, mix_half, mix_other))

    output = from_sequence_end(here, after(output_slots, input_low), groups)
    final_input = from_sequence_end(here, after(input_slots, input_mark), groups).astype(f32)
    final_down = column_last(here, down_half, down_other).astype(f32)
    final_up_merge = column_last(here, up_half, up_other).astype(f32)
    final_mix = mix_last[:, : 3 * width].astype(f32).reshape(own, PARTS, 3, H // PARTS, HD)
    final_mix = final_mix.transpose(0, 1, 3, 2, 4).reshape(own, 3 * width)
    final_columns = mix_last[:, 3 * width :].astype(f32)
    finals = final_columns.T
    (
        final_query,
        final_value,
        final_merge_bias,
        final_gain_one,
        final_shift_one,
        final_down_bias,
        final_gain_two,
        final_shift_two,
    ) = [finals[j] for j in range(8)]
    final_up_bias = finals[8 : 8 + ups].reshape(-1)
    return (
        output,
        final_input,
        final_mix,
        final_query,
        final_value,
        final_up_merge[:, hidden_size:],
        final_merge_bias,
        final_gain_one,
        final_shift_one,
        final_up_merge[:, :hidden_size],
        final_up_bias,
        final_down,
        final_down_bias,
        final_gain_two,
        final_shift_two,
    )


def solution(mesh):
    wide, row, thin = P("fsdp", "seq", None), P("fsdp", None), P("fsdp")
    return jax.shard_map(
        per_device,
        mesh=mesh,
        in_specs=(wide, P("fsdp", "seq"), row, thin, thin, row, thin, thin, thin, row, thin, row, thin, thin, thin, wide),
        out_specs=(wide, wide, row, thin, thin, row, thin, thin, thin, row, thin, row, thin, thin, thin),
        check_vma=False,
    )
```

```python
import functools, math
import jax, jax.numpy as jnp
from jax import lax
from jax.experimental import pallas as pl
from jax.experimental.layout import Layout, with_layout_constraint
from jax.experimental.pallas import tpu as pltpu
from jax.sharding import PartitionSpec as P

LANES = 128
FAR = -1000000000.0
IDS = 4
LN2 = math.log(2.0)


def nt(a, b):
    return lax.dot_general(a, b, (((1,), (1,)), ((), ())), preferred_element_type=jnp.float32)


def nn(a, b):
    return lax.dot_general(a, b, (((1,), (0,)), ((), ())), preferred_element_type=jnp.float32)


def lane_of(rows):
    return lax.broadcasted_iota(jnp.int32, (rows, LANES), 1)


def split3(x):
    high = x.astype(jnp.bfloat16).astype(jnp.float32)
    middle = (x - high).astype(jnp.bfloat16).astype(jnp.float32)
    return high, middle, x - high - middle


def gather_blocks(info, block, count, own_ref, mate_ref, put):
    for b in range(count):
        start = pl.multiple_of(((b // 2) ^ info[1]) * block, block)

        @pl.when(info[0] == b % 2)
        def _():
            put(b, own_ref[pl.ds(start, block), :])

        @pl.when(info[0] != b % 2)
        def _():
            put(b, mate_ref[pl.ds(start, block), :])


def forward_kernel(info, q_ref, k_own, k_mate, v_own, v_mate, qx_ref, kx_ref, *refs, size, plan):
    count, moves, outs = plan
    beside, (out_ref, ext_ref), full = refs[:count], refs[count : count + 2], refs[count + 2 : count + 2 + len(outs)]
    k_all, vt_all, s_all, *buffers = refs[count + 2 + len(outs) :]
    slot = pl.program_id(1)
    if count:
        in_sem, out_sem = buffers[count:]
        reads = [pltpu.make_async_copy(beside[j], buffers[j], in_sem.at[j]) for j in range(count)]
        writes = [
            pltpu.make_async_copy(
                buffers[j].at[pl.ds(row, rows), :],
                full[out].at[info[info.shape[0] - count + j], :, pl.ds(col, buffers[j].shape[1])],
                out_sem.at[j, k],
            )
            for j in range(count)
            for k, (row, rows, out, col) in enumerate(moves)
        ]
        at = pl.program_id(0) * pl.num_programs(1) + slot

        @pl.when(at == 0)
        def _():
            for read in reads:
                read.start()

        @pl.when(at == 2)
        def _():
            for read in reads:
                read.wait()
            for write in writes:
                write.start()

        @pl.when(at == pl.num_programs(0) * pl.num_programs(1) - 1)
        def _():
            for write in writes:
                write.wait()

    block = q_ref.shape[0]
    count = kx_ref.shape[0] // block
    heads = LANES // size
    lane_head = lane_of(block) // size

    @pl.when(slot == 0)
    def _():
        def put_k(b, rows):
            ext = kx_ref[b * block : (b + 1) * block, :]
            for h in range(heads):
                k_all[h, b * block : (b + 1) * block, :] = jnp.where(lane_head == h, rows, ext)

        def put_v(b, rows):
            turned = rows.T
            for h in range(heads):
                vt_all[h, :size, b * block : (b + 1) * block] = turned[h * size : (h + 1) * size]

        gather_blocks(info, block, count, k_own, k_mate, put_k)
        gather_blocks(info, block, count, v_own, v_mate, put_v)
        for h in range(heads):
            vt_all[h, size:, :] = jnp.ones((vt_all.shape[1] - size, vt_all.shape[2]), vt_all.dtype)

    rows = q_ref[...]
    qx = qx_ref[...]
    queries = [jnp.where(lane_head == h, rows, qx) for h in range(heads)]

    part = block
    lo, hi = info[2 + 2 * slot], info[3 + 2 * slot]

    def score(h, kb, i, top):
        at = pl.multiple_of(kb * block + i * part, part)
        st = nt(k_all[h, pl.ds(at, part), :], queries[h])
        s_all[h, i * part : (i + 1) * part, :] = st
        return jnp.maximum(top, jnp.max(st.reshape(part // 8, 8, block), axis=0))

    def weigh(h, kb, i, m, acc):
        at = pl.multiple_of(kb * block + i * part, part)
        p = jnp.exp2(s_all[h, i * part : (i + 1) * part, :] - m).astype(jnp.bfloat16)
        return acc + nn(vt_all[h, :, pl.ds(at, part)], p)

    least = jnp.full((8, block), -jnp.inf, jnp.float32)

    def step(kb, carry):
        tops, state = carry
        tops, state = list(tops), list(state)
        after = jnp.minimum(kb + 1, count - 1)
        for h in range(heads):
            ahead = (h + 1) % heads
            ahead_kb = kb if ahead else after
            m, acc = state[h]
            m_new = jnp.maximum(m, jnp.max(tops[h], axis=0, keepdims=True))
            acc = acc * jnp.exp2(m - m_new)
            top = least
            for i in range(1):
                top = score(ahead, ahead_kb, i, top)
                acc = weigh(h, kb, i, m_new, acc)
            tops[ahead] = top
            state[h] = (m_new, acc)
        return tuple(tops), tuple(state)

    start = tuple(
        (jnp.full((1, block), -jnp.inf, jnp.float32), jnp.zeros((vt_all.shape[1], block), jnp.float32))
        for _ in range(heads)
    )
    first = score(0, lo, 0, least)
    _, done = lax.fori_loop(lo, hi, step, ((first,) + (least,) * (heads - 1), start))
    sums = [acc[size : size + 1] for _, acc in done]
    out_t = jnp.concatenate([acc[:size] * (1.0 / l) for (_, acc), l in zip(done, sums)], axis=0)
    out_ref[...] = out_t.T.astype(out_ref.dtype)
    row = lax.broadcasted_iota(jnp.int32, (size, block), 0)
    parts = []
    for (m, _), l in zip(done, sums):
        pieces = split3(-(m + jnp.log2(l)))
        part = jnp.zeros((size, block), jnp.float32)
        for j, piece in enumerate(pieces):
            part = jnp.where(row == IDS + j, piece, part)
        parts.append(part)
    ext_ref[...] = (jnp.concatenate(parts[::-1], axis=0).T + qx.astype(jnp.float32)).astype(ext_ref.dtype)


NOTHING = ((), (), ())


def attention_forward(info, own, mate, qx, kx, size, plan=NOTHING, spots=()):
    rows, width = own.shape[0], own.shape[1] // 3
    length = kx.shape[0]
    slots = (info.shape[0] - 2) // 2
    block = rows // slots
    pairs = width // LANES
    heads = LANES // size
    pieces, moves, outs = plan
    if pieces:
        info = jnp.concatenate([info, jnp.stack(spots).astype(jnp.int32)])
    anywhere = pl.BlockSpec(memory_space=pl.ANY)
    return pl.pallas_call(
        functools.partial(forward_kernel, size=size, plan=(len(pieces), moves, outs)),
        grid_spec=pltpu.PrefetchScalarGridSpec(
            num_scalar_prefetch=1,
            grid=(pairs, slots),
            in_specs=[
                pl.BlockSpec((block, LANES), lambda p, s, i: (s, p)),
                pl.BlockSpec((rows, LANES), lambda p, s, i: (0, pairs + p)),
                pl.BlockSpec((rows, LANES), lambda p, s, i: (0, pairs + p)),
                pl.BlockSpec((rows, LANES), lambda p, s, i: (0, 2 * pairs + p)),
                pl.BlockSpec((rows, LANES), lambda p, s, i: (0, 2 * pairs + p)),
                pl.BlockSpec((block, LANES), lambda p, s, i: (s, 0)),
                pl.BlockSpec((length, LANES), lambda p, s, i: (0, 0)),
            ]
            + [anywhere] * len(pieces),
            out_specs=[pl.BlockSpec((block, LANES), lambda p, s, i: (s, p))] * 2 + [anywhere] * len(outs),
            scratch_shapes=[
                pltpu.VMEM((heads, length, LANES), jnp.bfloat16),
                pltpu.VMEM((heads, size + 16, length), jnp.bfloat16),
                pltpu.VMEM((heads, block, block), jnp.float32),
            ]
            + [pltpu.VMEM(piece.shape, piece.dtype) for piece in pieces]
            + [pltpu.SemaphoreType.DMA((len(pieces),)), pltpu.SemaphoreType.DMA((len(pieces), len(moves)))] * bool(pieces),
        ),
        out_shape=[jax.ShapeDtypeStruct((rows, width), jnp.bfloat16)] * 2
        + [jax.ShapeDtypeStruct(shape, jnp.bfloat16) for shape in outs],
        compiler_params=pltpu.CompilerParams(dimension_semantics=("arbitrary", "arbitrary")),
        cost_estimate=pl.CostEstimate(
            flops=2 * rows * length * width, bytes_accessed=8 * rows * width * 2, transcendentals=rows * length * pairs
        ),
        name="attention_forward",
    )(info, own, own, mate, own, mate, qx, kx, *pieces)


def backward_kernel(
    info, q_ref, ext_ref, do_ref, ctx_ref, k_own, k_mate, v_own, v_mate, kx_ref,
    dq_ref, own_ref, mate_ref, k_all, kt_all, v_all, dk_all, dv_all, *, size
):
    slot = pl.program_id(1)
    block = q_ref.shape[0]
    count = kx_ref.shape[0] // block
    heads = LANES // size
    lane = lane_of(block)
    lane_head = lane // size
    place = lane % size
    three = (place >= IDS) & (place < IDS + 3)

    @pl.when(slot == 0)
    def _():
        def put_k(b, rows):
            ext = kx_ref[b * block : (b + 1) * block, :]
            for h in range(heads):
                k_all[h, b * block : (b + 1) * block, :] = jnp.where(lane_head == h, rows, ext)
            kt_all[:, b * block : (b + 1) * block] = rows.T

        def put_v(b, rows):
            one = three.astype(rows.dtype)
            for h in range(heads):
                v_all[h, b * block : (b + 1) * block, :] = jnp.where(lane_head == h, rows, one)

        gather_blocks(info, block, count, k_own, k_mate, put_k)
        gather_blocks(info, block, count, v_own, v_mate, put_v)
        dk_all[...] = jnp.zeros_like(dk_all)
        dv_all[...] = jnp.zeros_like(dv_all)

    rows = q_ref[...]
    ext = ext_ref[...]
    grads = do_ref[...]
    zero = jnp.zeros_like(rows)
    queries = [jnp.where(lane_head == h, rows, ext) for h in range(heads)]
    plain_q = jnp.concatenate([jnp.where(lane_head == h, rows, zero) for h in range(heads)], axis=0)
    plain_do = jnp.concatenate([jnp.where(lane_head == h, grads, zero) for h in range(heads)], axis=0)
    product = grads.astype(jnp.float32) * ctx_ref[...].astype(jnp.float32)
    outs = []
    for h in range(heads):
        delta = jnp.sum(jnp.where(lane_head == h, product, 0.0), axis=1, keepdims=True)
        wide = jnp.zeros((block, LANES), jnp.float32)
        for j, piece in enumerate(split3(-delta)):
            wide = jnp.where(place == IDS + j, piece, wide)
        outs.append(jnp.where(lane_head == h, grads, wide.astype(grads.dtype)))

    def step(kb, carry):
        start = pl.multiple_of(kb * block, block)
        probs, scores, fresh = [], [], []
        for h in range(heads):
            p = jnp.exp2(nt(k_all[h, pl.ds(start, block), :], queries[h]))
            ds = (p * nt(v_all[h, pl.ds(start, block), :], outs[h])).astype(jnp.bfloat16)
            probs.append(p.astype(jnp.bfloat16))
            scores.append(ds)
            fresh.append(carry[h] + nn(kt_all[h * size : (h + 1) * size, pl.ds(start, block)], ds))
        dv_all[pl.ds(start, block), :] += nn(jnp.concatenate(probs, axis=1), plain_do)
        dk_all[pl.ds(start, block), :] += nn(jnp.concatenate(scores, axis=1), plain_q)
        return tuple(fresh)

    dq = lax.fori_loop(
        info[2 + 2 * slot], info[3 + 2 * slot], step,
        tuple(jnp.zeros((size, block), jnp.float32) for _ in range(heads)),
    )
    dq_ref[...] = (jnp.concatenate(dq, axis=0) * (1.0 / math.sqrt(size))).T.astype(dq_ref.dtype)

    @pl.when(slot == pl.num_programs(1) - 1)
    def _():
        for b in range(count):
            spot = pl.multiple_of(((b // 2) ^ info[1]) * block, block)
            for j, (total, factor) in enumerate(((dk_all, LN2), (dv_all, 1.0))):

                @pl.when(info[0] == b % 2)
                def _():
                    own_ref[j, pl.ds(spot, block), :] = (total[pl.ds(b * block, block), :] * factor).astype(own_ref.dtype)

                @pl.when(info[0] != b % 2)
                def _():
                    mate_ref[j, pl.ds(spot, block), :] = (total[pl.ds(b * block, block), :] * factor).astype(mate_ref.dtype)


def attention_backward(info, own, mate, ext, grads, ctx, kx, size, first):
    rows, width = ctx.shape
    length = kx.shape[0]
    slots = (info.shape[0] - 2) // 2
    block = rows // slots
    pairs = width // LANES
    heads = LANES // size
    tile = pl.BlockSpec((block, LANES), lambda p, s, i: (s, p))
    return pl.pallas_call(
        functools.partial(backward_kernel, size=size),
        grid_spec=pltpu.PrefetchScalarGridSpec(
            num_scalar_prefetch=1,
            grid=(pairs, slots),
            in_specs=[
                tile,
                tile,
                pl.BlockSpec((block, LANES), lambda p, s, i: (s, first + p)),
                tile,
                pl.BlockSpec((rows, LANES), lambda p, s, i: (0, pairs + p)),
                pl.BlockSpec((rows, LANES), lambda p, s, i: (0, pairs + p)),
                pl.BlockSpec((rows, LANES), lambda p, s, i: (0, 2 * pairs + p)),
                pl.BlockSpec((rows, LANES), lambda p, s, i: (0, 2 * pairs + p)),
                pl.BlockSpec((length, LANES), lambda p, s, i: (0, 0)),
            ],
            out_specs=[
                tile,
                pl.BlockSpec((2, rows, LANES), lambda p, s, i: (0, 0, p)),
                pl.BlockSpec((2, rows, LANES), lambda p, s, i: (0, 0, p)),
            ],
            scratch_shapes=[
                pltpu.VMEM((heads, length, LANES), jnp.bfloat16),
                pltpu.VMEM((LANES, length), jnp.bfloat16),
                pltpu.VMEM((heads, length, LANES), jnp.bfloat16),
                pltpu.VMEM((length, LANES), jnp.float32),
                pltpu.VMEM((length, LANES), jnp.float32),
            ],
        ),
        out_shape=[
            jax.ShapeDtypeStruct((rows, width), jnp.bfloat16),
            jax.ShapeDtypeStruct((2, rows, width), jnp.float32),
            jax.ShapeDtypeStruct((2, rows, width), jnp.bfloat16),
        ],
        compiler_params=pltpu.CompilerParams(dimension_semantics=("arbitrary", "arbitrary")),
        cost_estimate=pl.CostEstimate(
            flops=5 * rows * length * width, bytes_accessed=24 * rows * width, transcendentals=rows * length * pairs
        ),
        name="attention_backward",
    )(info, own, ext, grads, ctx, own, mate, own, mate, kx)


def key_extension(ids):
    place = jnp.arange(LANES) % (LANES // 2)
    hot = ids[:, None] == place[None, :]
    return (hot | ((place >= IDS) & (place < IDS + 3))[None, :]).astype(jnp.bfloat16)


def query_extension(ids):
    place = jnp.arange(LANES) % (LANES // 2)
    other = (place < IDS)[None, :] & (ids[:, None] != place[None, :])
    return jnp.where(other, FAR, 0.0).astype(jnp.bfloat16)


H = 12
HD = 64
LOG2E = 1.0 / LN2
PARTS = 3
eps_norm = 1e-06
bf16 = jnp.bfloat16
f32 = jnp.float32


def norm_forward(total, gain, shift):
    middle = jnp.mean(total, axis=-1, keepdims=True)
    centred = total - middle
    factor = lax.rsqrt(jnp.mean(centred * centred, axis=-1, keepdims=True) + eps_norm)
    normed = centred * factor
    return (normed * gain + shift, normed, factor)


def norm_backward(grad_out, normed, factor, gain):
    scaled = grad_out * gain
    inner = (
        scaled
        - jnp.mean(scaled, axis=-1, keepdims=True)
        - normed * jnp.mean(scaled * normed, axis=-1, keepdims=True)
    )
    return (factor * inner, jnp.sum(grad_out * normed, axis=0), jnp.sum(grad_out, axis=0))


def gelu_parts(hidden):
    normal_cdf = 0.5 * (1.0 + jax.scipy.special.erf(hidden * (1.0 / math.sqrt(2.0))))
    density = jnp.exp(-0.5 * hidden * hidden) * (1.0 / math.sqrt(2.0 * math.pi))
    return (hidden * normal_cdf, normal_cdf + hidden * density)


def dot(a, b):
    return jnp.dot(a, b, preferred_element_type=f32)


def column_sums(values):
    return jnp.sum(values.astype(f32), axis=0)


def xor_pairs(size, bits):
    return [(i, i ^ bits) for i in range(size)]


def straight(values):
    return with_layout_constraint(values, Layout(tuple(range(values.ndim))))


def pick(values, index, axis=0):
    return lax.dynamic_index_in_dim(values, index, axis, keepdims=False)


def after(values, *marks):
    return lax.optimization_barrier((values, marks))[0]


class Places:
    def __init__(self):
        self.columns = lax.axis_size("seq")
        self.shards = lax.axis_size("fsdp")
        self.column = lax.axis_index("seq")
        self.shard = lax.axis_index("fsdp")
        self.core = self.shard & 1
        self.plane = self.shard >> 1

    def mate(self, values):
        return lax.ppermute(values, "fsdp", xor_pairs(self.shards, 1))

    def across(self, values, bits):
        return lax.ppermute(values, "seq", xor_pairs(self.columns, bits))

    def aside(self, values, bits):
        return lax.ppermute(values, "fsdp", xor_pairs(self.shards, 2 * bits))


def to_sequence_parts(here, values):
    groups, piece, width = values.shape
    halves = values.reshape(groups, 2, piece // 2, width)
    kept = straight(pick(halves, here.core, 1))
    other = straight(here.mate(straight(pick(halves, 1 - here.core, 1))))
    parts = []
    for k in range(here.columns):
        want = here.column ^ k
        same = lax.div(want, groups) == here.core
        spot = lax.rem(want, groups)
        parts.append(straight(jnp.where(same, pick(kept, spot), pick(other, spot))))
    return parts


def from_sequence_send(here, slots, first=0):
    return [here.across(part, k) if k else part for k, part in enumerate(slots, first)]


def from_sequence_end(here, slots, groups):
    rows = jnp.stack(slots)

    def of(core):
        return jnp.stack([pick(rows, here.column ^ (core * groups + j)) for j in range(groups)])

    kept = of(here.core)
    other = here.mate(of(1 - here.core))
    first = here.core == 0
    return jnp.concatenate([jnp.where(first, kept, other), jnp.where(first, other, kept)], axis=1)


def place_kernel(info, *refs, moves, outs):
    count = len(moves)
    parts, full, buffers = refs[:count], refs[count : count + outs], refs[count + outs : 2 * count + outs]
    in_sem, out_sem = refs[2 * count + outs :]
    reads = [pltpu.make_async_copy(parts[k], buffers[k], in_sem.at[k]) for k in range(count)]
    for read in reads:
        read.start()
    writes = []
    for k in range(count):
        reads[k].wait()
        for j, (row, rows, cut_row, col, cols, out) in enumerate(moves[k]):
            write = pltpu.make_async_copy(
                buffers[k].at[pl.ds(cut_row, rows), pl.ds(col, cols)],
                full[out].at[info[k], pl.ds(row, rows), :],
                out_sem.at[k, j],
            )
            write.start()
            writes.append(write)
    for write in writes:
        write.wait()


def place(parts, spots, firsts, rows, cuts):
    kind = parts[0].dtype
    shards = sum(part.shape[0] for part in parts) // rows
    moves = [
        [(first, part.shape[0], 0, col, cols, out) for out, (col, cols) in enumerate(cuts)] for first, part in zip(firsts, parts)
    ]
    full = pl.pallas_call(
        functools.partial(place_kernel, moves=moves, outs=len(cuts)),
        grid_spec=pltpu.PrefetchScalarGridSpec(
            num_scalar_prefetch=1,
            grid=(),
            in_specs=[pl.BlockSpec(memory_space=pl.ANY)] * len(parts),
            out_specs=[pl.BlockSpec(memory_space=pl.ANY)] * len(cuts),
            scratch_shapes=[pltpu.VMEM(part.shape, kind) for part in parts]
            + [pltpu.SemaphoreType.DMA((len(parts),)), pltpu.SemaphoreType.DMA((len(parts), len(cuts)))],
        ),
        out_shape=[jax.ShapeDtypeStruct((shards, rows, cols), kind) for _, cols in cuts],
        cost_estimate=pl.CostEstimate(flops=0, bytes_accessed=0, transcendentals=0),
        name="place_parts",
    )(jnp.stack(spots).astype(jnp.int32), *parts)
    return [f.reshape(-1, f.shape[2]) for f in full]


def gather_direct(here, local):
    return [local] + [here.aside(local, k) for k in range(1, 4)]


def with_mates(here, parts):
    spots = [here.shard ^ (2 * k) for k in range(4)]
    return parts + [here.mate(part) for part in parts], spots + [spot ^ 1 for spot in spots]


def gather_cut(here, local, cuts, mark):
    if here.shards != 8:
        full = lax.all_gather(local, "fsdp", axis=0, tiled=True)
        return [full[:, col : col + cols] for col, cols in cuts]
    parts, spots = with_mates(here, after(gather_direct(here, local), mark))
    return place(parts, spots, [0] * 8, local.shape[0], cuts)


def pack_kernel(mix_ref, merge_ref, columns_ref, out_ref, *, size, parts):
    rows, width = merge_ref.shape
    per = LANES // size
    lane_low = lane_of(rows) < size
    pairs = width // LANES // parts
    for pair in range(width // LANES):
        part, spot = pair // pairs, pair % pairs
        for j in range(3):
            one, two = [((3 * (per * pair + k) + j) * size) // LANES * LANES for k in range(2)]
            one, two = mix_ref[:, one : one + LANES].astype(jnp.float32), mix_ref[:, two : two + LANES].astype(jnp.float32)
            if j % 2:
                joined = pltpu.roll(jnp.where(lane_low, two, one), size, 1)
            else:
                joined = jnp.where(lane_low, one, two)
            at = (part * 3 + j) * pairs * LANES + spot * LANES
            out_ref[:, at : at + LANES] = joined.astype(out_ref.dtype)
    out_ref[:, 3 * width : 4 * width] = merge_ref[...]
    out_ref[:, 4 * width :] = columns_ref[...]


def pack(mix, merge, columns, size, parts):
    rows, width = merge.shape
    return pl.pallas_call(
        functools.partial(pack_kernel, size=size, parts=parts),
        out_shape=jax.ShapeDtypeStruct((rows, 4 * width + LANES), mix.dtype),
        name="pack_projection",
    )(mix, merge, columns)


def share_pair(here, partial):
    shards, rows, width = partial.shape
    pairs = partial.reshape(shards // 2, 2, rows, width)
    return pick(pairs, here.core, 1), here.mate(pick(pairs, 1 - here.core, 1).astype(bf16))


def share_plane(here, kept, other):
    def total(k):
        spot = here.plane ^ k
        return pick(kept, spot).astype(f32) + pick(other, spot).astype(f32)

    return total(0), [total(k).astype(bf16) for k in range(1, here.shards // 2)]


def share_send(here, lows, apart=False):
    others = []
    for k, low in enumerate(lows, 1):
        others.append(here.aside(after(low, others[k - 3]) if apart and k > 2 else low, k))
    return others


def share_sum(share, others):
    for other in others:
        share = share + other.astype(f32)
    return share.astype(bf16)


def column_first(here, share):
    low = share.reshape(2, share.shape[0] // 2, share.shape[1])
    side = here.column & 1
    return pick(low, side), here.across(pick(low, 1 - side), 1)


def column_second(here, half, other):
    low = (half.astype(f32) + other.astype(f32)).astype(bf16)
    step, others = 2, []
    while 2 * step < here.columns:
        low = (low.astype(f32) + here.across(low, step).astype(f32)).astype(bf16)
        step *= 2
    return low, here.across(low, step)


def column_third(here, half, other):
    half = (half.astype(f32) + other.astype(f32)).astype(bf16)
    return half, here.across(half, 1)


def column_last(here, half, other):
    first = (here.column & 1) == 0
    return jnp.concatenate([jnp.where(first, half, other), jnp.where(first, other, half)], axis=0)


def per_device(
    tokens,
    segment_ids,
    mix_weight,
    query_bias,
    value_bias,
    merge_weight,
    merge_bias,
    first_gain,
    first_shift,
    up_weight,
    up_bias,
    down_weight,
    down_bias,
    second_gain,
    second_shift,
    output_grad,
):
    here = Places()
    groups, piece, width = tokens.shape
    shards = here.shards
    own = width // shards
    hidden_size = up_weight.shape[1]
    half = piece // 2
    rows = here.columns * half
    length = here.columns * piece

    def send(parts, first=0):
        return [straight(part) for part in from_sequence_send(here, parts, first)]

    ups = hidden_size // width
    part_width = width // PARTS
    ids_sent = [segment_ids] + [here.across(segment_ids, k) for k in range(1, here.columns)]
    ids_slots = jnp.stack([pick(i, lax.rem(here.column, groups)) for i in ids_sent])
    ids_other = here.mate(ids_slots)
    ids_slots = jnp.where(lax.div(here.column, groups) == here.core, ids_slots, ids_other)
    ids_own = pick(ids_slots.reshape(here.columns, 2, half), here.core, 1)
    ids = jnp.stack([pick(ids_slots, here.column ^ k) for k in range(here.columns)]).reshape(2 * here.columns, half)
    first_id, last_id = ids[:, 0], ids[:, -1]
    low = jnp.sum(last_id[None, :] < ids_own[:, :1], axis=1)
    high = jnp.sum(first_id[None, :] <= ids_own[:, -1:], axis=1)
    info = jnp.concatenate([jnp.stack([here.core, here.column]), jnp.stack([low, high], axis=1).reshape(-1)]).astype(jnp.int32)
    key_ext = key_extension(ids.reshape(length))
    query_ext = query_extension(ids_own.reshape(rows))

    token_parts, ids_sent = lax.optimization_barrier((to_sequence_parts(here, tokens), ids_sent))
    token_slots = send(token_parts)

    vectors = (query_bias, value_bias, merge_bias, first_gain, first_shift, down_bias, second_gain, second_shift)
    local_weights = after((vectors, up_bias, mix_weight, merge_weight), ids_sent)
    lines = jnp.concatenate([jnp.stack(local_weights[0]), local_weights[1].reshape(ups, own)], axis=0)
    columns = jnp.pad(lines, ((0, LANES - lines.shape[0]), (0, 0))).T
    mix_local = pack(local_weights[2], local_weights[3], columns, HD, PARTS)
    *mix_parts, merge_full, columns_full = gather_cut(
        here, mix_local, [(p * width, width) for p in range(PARTS + 1)] + [(4 * width, LANES)], token_slots[2:]
    )
    lines_full = columns_full.T.astype(f32)
    query_full, value_full, merge_bias_full, gain_one, shift_one, down_bias_full, gain_two, shift_two = [
        lines_full[j] for j in range(8)
    ]
    up_bias_full = lines_full[8 : 8 + ups].reshape(ups, shards, own).transpose(1, 0, 2).reshape(-1)

    cotangent_parts = to_sequence_parts(here, after(output_grad, token_parts))
    ready = (cotangent_parts, mix_parts, merge_full, lines_full, info, key_ext, query_ext)
    token_slots, (cotangent_parts, mix_parts, merge_full, lines_full, info, key_ext, query_ext) = lax.optimization_barrier(
        (token_slots, ready)
    )
    flat = straight(jnp.concatenate(token_slots, axis=0))
    cotangent_parts = after(cotangent_parts, flat)
    cotangent_two = send(cotangent_parts[2:3], 2)
    direct = shards == 8
    up_local, down_local = after((up_weight, down_weight), mix_parts[0])
    if direct:
        packed = jnp.concatenate([up_local[:, j * width : (j + 1) * width] for j in range(ups)] + [down_local], axis=0)
        packed_parts = gather_direct(here, after(packed, flat))
    else:
        up_full, down_full = [lax.all_gather(w, "fsdp", axis=0, tiled=True) for w in (up_local, down_local)]

    column_scale = jnp.where(jnp.arange(width) < part_width, LOG2E / math.sqrt(HD), 1.0)
    mixed, mixed_mate = [], []
    for p in range(PARTS):
        of_part = slice(p * part_width, (p + 1) * part_width)
        bias = jnp.concatenate([query_full[of_part], jnp.zeros((part_width,), f32), value_full[of_part]])
        mixed.append(((dot(flat, mix_parts[p]) + bias) * column_scale).astype(bf16))
        mixed_mate.append(here.mate(mixed[p]))

    mixed, mixed_mate = lax.optimization_barrier((mixed, mixed_mate))
    contexts, exts = [], []
    plan, spots = NOTHING, ()
    for p in range(PARTS):
        if p:
            mixed[p], mixed_mate[p] = after((mixed[p], mixed_mate[p]), contexts[-1])
        if p == 1:
            mixed[p], cotangent_two = lax.optimization_barrier((mixed[p], cotangent_two))
            later = after(cotangent_parts, contexts[-1])
            cotangent_slots = send(later[:2]) + cotangent_two + send(later[3:], 3)
        if p == PARTS - 1 and direct:
            pieces, spots = with_mates(here, after(packed_parts, contexts[-1]))
            moves = [(j * own, own, 0, j * width) for j in range(ups)] + [(ups * own, ups * own, 1, 0)]
            outs = [(shards,) + up_weight.shape, (shards,) + down_weight.shape]
            plan = (pieces, tuple(moves), tuple(outs))
        context, ext, *placed = attention_forward(info, mixed[p], mixed_mate[p], query_ext, key_ext, HD, plan, spots)
        contexts.append(context)
        exts.append(ext)
    if direct:
        up_full, down_full = [full.reshape(-1, full.shape[2]) for full in placed]
    context = jnp.concatenate(contexts, axis=1)
    cotangent = jnp.concatenate(after(cotangent_slots, contexts[-1]), axis=0).astype(f32)

    attended = dot(context, merge_full) + merge_bias_full
    first_out, normed_one, factor_one = norm_forward(flat.astype(f32) + attended, gain_one, shift_one)
    first_low = first_out.astype(bf16)
    hidden = dot(first_low, up_full) + up_bias_full
    active, slope = gelu_parts(hidden)
    active_low, slope_low = lax.optimization_barrier((active.astype(bf16), slope.astype(bf16)))
    branch = dot(active_low, down_full) + down_bias_full
    result, normed_two, factor_two = norm_forward(first_out + branch, gain_two, shift_two)
    result_low = list(result.astype(bf16).reshape(here.columns, half, width))

    grad_second, second_gain_grad, second_shift_grad = norm_backward(cotangent, normed_two, factor_two, gain_two)
    grad_branch = grad_second.astype(bf16)
    down_grad = dot(active_low.T, grad_branch).astype(bf16)
    down_kept, down_other = share_pair(here, down_grad.reshape(shards, -1, width))
    down_bias_grad = column_sums(grad_branch)
    grad_active = dot(grad_branch, down_full.T)
    grad_hidden = (grad_active * slope_low.astype(f32)).astype(bf16)
    down_share, down_lows = share_plane(here, down_kept, after(down_other, grad_hidden))
    down_others = share_send(here, down_lows)
    up_grad = dot(first_low.T, grad_hidden).astype(bf16)
    up_bias_grad = column_sums(grad_hidden)
    grad_first = grad_second + dot(grad_hidden, up_full.T)
    grad_sum, first_gain_grad, first_shift_grad = norm_backward(grad_first, normed_one, factor_one, gain_one)
    grad_attended = grad_sum.astype(bf16)
    merge_grad = dot(context.T, grad_attended).astype(bf16)
    merge_bias_grad = column_sums(grad_attended)
    up_merge = jnp.concatenate([up_grad.reshape(shards, own, hidden_size), merge_grad.reshape(shards, own, width)], axis=2)
    up_kept, up_other = share_pair(here, up_merge)
    grad_context = dot(grad_attended, merge_full.T).astype(bf16)
    up_share, up_lows = share_plane(here, up_kept, after(up_other, grad_context))
    up_others = share_send(here, up_lows)

    def backward(part, grads):
        dq, kept, other = attention_backward(
            info, mixed[part], mixed_mate[part], exts[part], grads, contexts[part], key_ext, HD, part * part_width // LANES
        )
        return dq, kept, here.mate(other)

    def mixed_part(pieces):
        dq, kept, other = pieces
        kv = (kept + other.astype(f32)).astype(bf16)
        return jnp.concatenate([dq, kv[0], kv[1]], axis=1)

    one = backward(0, after(grad_context, down_share, up_share))
    down_others, down_share = after((down_others, down_share), one[0])
    down_half, down_other = column_first(here, share_sum(down_share, down_others))
    up_others, up_share = after((up_others, up_share), one[0])
    up_half, up_other = column_first(here, share_sum(up_share, up_others))
    output_slots = from_sequence_send(here, after(result_low, one[0]))
    two = backward(1, after(grad_context, down_half, up_half))
    one, up_half, up_other = after((one, up_half, up_other), two[0])
    mixed_one = mixed_part(one)
    down_half, down_other = column_second(here, *after((down_half, down_other), two[0]))
    up_half, up_other = column_second(here, up_half, up_other)
    input_part = grad_sum + dot(mixed_one, mix_parts[0].T)
    three = backward(2, after(grad_context, down_half, up_half, input_part, output_slots[:3]))
    two, down_half, down_other, up_half, up_other, output_slots[3:] = after(
        (two, down_half, down_other, up_half, up_other, output_slots[3:]), three[0]
    )
    mixed_two = mixed_part(two)
    input_part = input_part + dot(mixed_two, mix_parts[1].T)
    mixed_three = mixed_part(after(three, input_part))
    input_low = (input_part + dot(mixed_three, mix_parts[2].T)).astype(bf16)
    input_slots = from_sequence_send(here, list(input_low.reshape(here.columns, half, width)))
    mixed_all = after(jnp.concatenate([mixed_one, mixed_two, mixed_three], axis=1), input_low)
    mix_grad = dot(flat.T, mixed_all).astype(bf16)

    sums = [column_sums(m) for m in (mixed_one, mixed_two, mixed_three)]
    query_grad = jnp.concatenate([s[:part_width] for s in sums])
    value_grad = jnp.concatenate([s[2 * part_width :] for s in sums])
    vectors = (
        query_grad,
        value_grad,
        merge_bias_grad,
        first_gain_grad,
        first_shift_grad,
        down_bias_grad,
        second_gain_grad,
        second_shift_grad,
    )
    up_lines = up_bias_grad.reshape(shards, ups, own).transpose(1, 0, 2).reshape(ups, width)
    lines_grad = jnp.concatenate([jnp.stack(vectors), up_lines], axis=0)
    columns_grad = jnp.pad(lines_grad, ((0, LANES - lines_grad.shape[0]), (0, 0))).T
    whole = jnp.concatenate([mix_grad, lax.optimization_barrier(columns_grad).astype(bf16)], axis=1).reshape(shards, own, -1)
    mix_share, mix_lows = share_plane(here, *share_pair(here, whole))
    mix_others = share_send(here, mix_lows, True)
    input_mark = mix_others[0]
    mix_share = share_sum(mix_share, mix_others)
    mix_half, mix_other = column_first(here, mix_share)
    down_half, down_other = column_third(here, *after((down_half, down_other), mix_share))
    up_half, up_other = column_third(here, *after((up_half, up_other), mix_share))
    mix_half, mix_other = column_second(here, mix_half, mix_other)
    down_half, down_other, up_half, up_other = after((down_half, down_other, up_half, up_other), mix_half)
    mix_last = column_last(here, *column_third(here, mix_half, mix_other))

    output = from_sequence_end(here, after(output_slots, input_low), groups)
    final_input = from_sequence_end(here, after(input_slots, input_mark), groups).astype(f32)
    final_down = column_last(here, down_half, down_other).astype(f32)
    final_up_merge = column_last(here, up_half, up_other).astype(f32)
    final_mix = mix_last[:, : 3 * width].astype(f32).reshape(own, PARTS, 3, H // PARTS, HD)
    final_mix = final_mix.transpose(0, 1, 3, 2, 4).reshape(own, 3 * width)
    final_columns = mix_last[:, 3 * width :].astype(f32)
    finals = final_columns.T
    (
        final_query,
        final_value,
        final_merge_bias,
        final_gain_one,
        final_shift_one,
        final_down_bias,
        final_gain_two,
        final_shift_two,
    ) = [finals[j] for j in range(8)]
    final_up_bias = finals[8 : 8 + ups].reshape(-1)
    return (
        output,
        final_input,
        final_mix,
        final_query,
        final_value,
        final_up_merge[:, hidden_size:],
        final_merge_bias,
        final_gain_one,
        final_shift_one,
        final_up_merge[:, :hidden_size],
        final_up_bias,
        final_down,
        final_down_bias,
        final_gain_two,
        final_shift_two,
    )


def solution(mesh):
    wide, row, thin = P("fsdp", "seq", None), P("fsdp", None), P("fsdp")
    return jax.shard_map(
        per_device,
        mesh=mesh,
        in_specs=(wide, P("fsdp", "seq"), row, thin, thin, row, thin, thin, thin, row, thin, row, thin, thin, thin, wide),
        out_specs=(wide, wide, row, thin, thin, row, thin, thin, thin, row, thin, row, thin, thin, thin),
        check_vma=False,
    )
```

```python
import functools, math
import jax, jax.numpy as jnp
from jax import lax
from jax.experimental import pallas as pl
from jax.experimental.layout import Layout, with_layout_constraint
from jax.experimental.pallas import tpu as pltpu
from jax.sharding import PartitionSpec as P

LANES = 128
FAR = -1000000000.0
IDS = 4
LN2 = math.log(2.0)


def nt(a, b):
    return lax.dot_general(a, b, (((1,), (1,)), ((), ())), preferred_element_type=jnp.float32)


def nn(a, b):
    return lax.dot_general(a, b, (((1,), (0,)), ((), ())), preferred_element_type=jnp.float32)


def lane_of(rows):
    return lax.broadcasted_iota(jnp.int32, (rows, LANES), 1)


def split3(x):
    high = x.astype(jnp.bfloat16).astype(jnp.float32)
    middle = (x - high).astype(jnp.bfloat16).astype(jnp.float32)
    return high, middle, x - high - middle


def gather_blocks(info, block, count, own_ref, mate_ref, put):
    for b in range(count):
        start = pl.multiple_of(((b // 2) ^ info[1]) * block, block)

        @pl.when(info[0] == b % 2)
        def _():
            put(b, own_ref[pl.ds(start, block), :])

        @pl.when(info[0] != b % 2)
        def _():
            put(b, mate_ref[pl.ds(start, block), :])


def forward_kernel(info, q_ref, k_own, k_mate, v_own, v_mate, qx_ref, kx_ref, *refs, size, plan):
    count, moves, outs = plan
    beside, (out_ref, ext_ref), full = refs[:count], refs[count : count + 2], refs[count + 2 : count + 2 + len(outs)]
    k_all, vt_all, s_all, *buffers = refs[count + 2 + len(outs) :]
    slot = pl.program_id(1)
    if count:
        in_sem, out_sem = buffers[count:]
        reads = [pltpu.make_async_copy(beside[j], buffers[j], in_sem.at[j]) for j in range(count)]
        writes = [
            pltpu.make_async_copy(
                buffers[j].at[pl.ds(row, rows), :],
                full[out].at[info[info.shape[0] - count + j], :, pl.ds(col, buffers[j].shape[1])],
                out_sem.at[j, k],
            )
            for j in range(count)
            for k, (row, rows, out, col) in enumerate(moves)
        ]
        at = pl.program_id(0) * pl.num_programs(1) + slot

        @pl.when(at == 0)
        def _():
            for read in reads:
                read.start()

        @pl.when(at == 2)
        def _():
            for read in reads:
                read.wait()
            for write in writes:
                write.start()

        @pl.when(at == pl.num_programs(0) * pl.num_programs(1) - 1)
        def _():
            for write in writes:
                write.wait()

    block = q_ref.shape[0]
    count = kx_ref.shape[0] // block
    heads = LANES // size
    lane_head = lane_of(block) // size

    @pl.when(slot == 0)
    def _():
        def put_k(b, rows):
            ext = kx_ref[b * block : (b + 1) * block, :]
            for h in range(heads):
                k_all[h, b * block : (b + 1) * block, :] = jnp.where(lane_head == h, rows, ext)

        def put_v(b, rows):
            turned = rows.T
            for h in range(heads):
                vt_all[h, :size, b * block : (b + 1) * block] = turned[h * size : (h + 1) * size]

        gather_blocks(info, block, count, k_own, k_mate, put_k)
        gather_blocks(info, block, count, v_own, v_mate, put_v)
        for h in range(heads):
            vt_all[h, size:, :] = jnp.ones((vt_all.shape[1] - size, vt_all.shape[2]), vt_all.dtype)

    rows = q_ref[...]
    qx = qx_ref[...]
    queries = [jnp.where(lane_head == h, rows, qx) for h in range(heads)]

    part = block
    lo, hi = info[2 + 2 * slot], info[3 + 2 * slot]

    def score(h, kb, i, top):
        at = pl.multiple_of(kb * block + i * part, part)
        st = nt(k_all[h, pl.ds(at, part), :], queries[h])
        s_all[h, i * part : (i + 1) * part, :] = st
        return jnp.maximum(top, jnp.max(st.reshape(part // 8, 8, block), axis=0))

    def weigh(h, kb, i, m, acc):
        at = pl.multiple_of(kb * block + i * part, part)
        p = jnp.exp2(s_all[h, i * part : (i + 1) * part, :] - m).astype(jnp.bfloat16)
        return acc + nn(vt_all[h, :, pl.ds(at, part)], p)

    least = jnp.full((8, block), -jnp.inf, jnp.float32)

    def step(kb, carry):
        tops, state = carry
        tops, state = list(tops), list(state)
        after = jnp.minimum(kb + 1, count - 1)
        for h in range(heads):
            ahead = (h + 1) % heads
            ahead_kb = kb if ahead else after
            m, acc = state[h]
            m_new = jnp.maximum(m, jnp.max(tops[h], axis=0, keepdims=True))
            acc = acc * jnp.exp2(m - m_new)
            top = least
            for i in range(1):
                top = score(ahead, ahead_kb, i, top)
                acc = weigh(h, kb, i, m_new, acc)
            tops[ahead] = top
            state[h] = (m_new, acc)
        return tuple(tops), tuple(state)

    start = tuple(
        (jnp.full((1, block), -jnp.inf, jnp.float32), jnp.zeros((vt_all.shape[1], block), jnp.float32))
        for _ in range(heads)
    )
    first = score(0, lo, 0, least)
    _, done = lax.fori_loop(lo, hi, step, ((first,) + (least,) * (heads - 1), start))
    sums = [acc[size : size + 1] for _, acc in done]
    out_t = jnp.concatenate([acc[:size] * (1.0 / l) for (_, acc), l in zip(done, sums)], axis=0)
    out_ref[...] = out_t.T.astype(out_ref.dtype)
    row = lax.broadcasted_iota(jnp.int32, (size, block), 0)
    parts = []
    for (m, _), l in zip(done, sums):
        pieces = split3(-(m + jnp.log2(l)))
        part = jnp.zeros((size, block), jnp.float32)
        for j, piece in enumerate(pieces):
            part = jnp.where(row == IDS + j, piece, part)
        parts.append(part)
    ext_ref[...] = (jnp.concatenate(parts[::-1], axis=0).T + qx.astype(jnp.float32)).astype(ext_ref.dtype)


NOTHING = ((), (), ())


def attention_forward(info, own, mate, qx, kx, size, plan=NOTHING, spots=()):
    rows, width = own.shape[0], own.shape[1] // 3
    length = kx.shape[0]
    slots = (info.shape[0] - 2) // 2
    block = rows // slots
    pairs = width // LANES
    heads = LANES // size
    pieces, moves, outs = plan
    if pieces:
        info = jnp.concatenate([info, jnp.stack(spots).astype(jnp.int32)])
    anywhere = pl.BlockSpec(memory_space=pl.ANY)
    return pl.pallas_call(
        functools.partial(forward_kernel, size=size, plan=(len(pieces), moves, outs)),
        grid_spec=pltpu.PrefetchScalarGridSpec(
            num_scalar_prefetch=1,
            grid=(pairs, slots),
            in_specs=[
                pl.BlockSpec((block, LANES), lambda p, s, i: (s, p)),
                pl.BlockSpec((rows, LANES), lambda p, s, i: (0, pairs + p)),
                pl.BlockSpec((rows, LANES), lambda p, s, i: (0, pairs + p)),
                pl.BlockSpec((rows, LANES), lambda p, s, i: (0, 2 * pairs + p)),
                pl.BlockSpec((rows, LANES), lambda p, s, i: (0, 2 * pairs + p)),
                pl.BlockSpec((block, LANES), lambda p, s, i: (s, 0)),
                pl.BlockSpec((length, LANES), lambda p, s, i: (0, 0)),
            ]
            + [anywhere] * len(pieces),
            out_specs=[pl.BlockSpec((block, LANES), lambda p, s, i: (s, p))] * 2 + [anywhere] * len(outs),
            scratch_shapes=[
                pltpu.VMEM((heads, length, LANES), jnp.bfloat16),
                pltpu.VMEM((heads, size + 16, length), jnp.bfloat16),
                pltpu.VMEM((heads, block, block), jnp.float32),
            ]
            + [pltpu.VMEM(piece.shape, piece.dtype) for piece in pieces]
            + [pltpu.SemaphoreType.DMA((len(pieces),)), pltpu.SemaphoreType.DMA((len(pieces), len(moves)))] * bool(pieces),
        ),
        out_shape=[jax.ShapeDtypeStruct((rows, width), jnp.bfloat16)] * 2
        + [jax.ShapeDtypeStruct(shape, jnp.bfloat16) for shape in outs],
        compiler_params=pltpu.CompilerParams(dimension_semantics=("arbitrary", "arbitrary")),
        cost_estimate=pl.CostEstimate(
            flops=2 * rows * length * width, bytes_accessed=8 * rows * width * 2, transcendentals=rows * length * pairs
        ),
        name="attention_forward",
    )(info, own, own, mate, own, mate, qx, kx, *pieces)


def backward_kernel(
    info, q_ref, ext_ref, do_ref, ctx_ref, k_own, k_mate, v_own, v_mate, kx_ref,
    dq_ref, own_ref, mate_ref, k_all, kt_all, v_all, dk_all, dv_all, *, size
):
    slot = pl.program_id(1)
    block = q_ref.shape[0]
    count = kx_ref.shape[0] // block
    heads = LANES // size
    lane = lane_of(block)
    lane_head = lane // size
    place = lane % size
    three = (place >= IDS) & (place < IDS + 3)

    @pl.when(slot == 0)
    def _():
        def put_k(b, rows):
            ext = kx_ref[b * block : (b + 1) * block, :]
            for h in range(heads):
                k_all[h, b * block : (b + 1) * block, :] = jnp.where(lane_head == h, rows, ext)
            kt_all[:, b * block : (b + 1) * block] = rows.T

        def put_v(b, rows):
            one = three.astype(rows.dtype)
            for h in range(heads):
                v_all[h, b * block : (b + 1) * block, :] = jnp.where(lane_head == h, rows, one)

        gather_blocks(info, block, count, k_own, k_mate, put_k)
        gather_blocks(info, block, count, v_own, v_mate, put_v)
        dk_all[...] = jnp.zeros_like(dk_all)
        dv_all[...] = jnp.zeros_like(dv_all)

    rows = q_ref[...]
    ext = ext_ref[...]
    grads = do_ref[...]
    zero = jnp.zeros_like(rows)
    queries = [jnp.where(lane_head == h, rows, ext) for h in range(heads)]
    plain_q = jnp.concatenate([jnp.where(lane_head == h, rows, zero) for h in range(heads)], axis=0)
    plain_do = jnp.concatenate([jnp.where(lane_head == h, grads, zero) for h in range(heads)], axis=0)
    product = grads.astype(jnp.float32) * ctx_ref[...].astype(jnp.float32)
    outs = []
    for h in range(heads):
        delta = jnp.sum(jnp.where(lane_head == h, product, 0.0), axis=1, keepdims=True)
        wide = jnp.zeros((block, LANES), jnp.float32)
        for j, piece in enumerate(split3(-delta)):
            wide = jnp.where(place == IDS + j, piece, wide)
        outs.append(jnp.where(lane_head == h, grads, wide.astype(grads.dtype)))

    def step(kb, carry):
        start = pl.multiple_of(kb * block, block)
        probs, scores, fresh = [], [], []
        for h in range(heads):
            p = jnp.exp2(nt(k_all[h, pl.ds(start, block), :], queries[h]))
            ds = (p * nt(v_all[h, pl.ds(start, block), :], outs[h])).astype(jnp.bfloat16)
            probs.append(p.astype(jnp.bfloat16))
            scores.append(ds)
            fresh.append(carry[h] + nn(kt_all[h * size : (h + 1) * size, pl.ds(start, block)], ds))
        dv_all[pl.ds(start, block), :] += nn(jnp.concatenate(probs, axis=1), plain_do)
        dk_all[pl.ds(start, block), :] += nn(jnp.concatenate(scores, axis=1), plain_q)
        return tuple(fresh)

    dq = lax.fori_loop(
        info[2 + 2 * slot], info[3 + 2 * slot], step,
        tuple(jnp.zeros((size, block), jnp.float32) for _ in range(heads)),
    )
    dq_ref[...] = (jnp.concatenate(dq, axis=0) * (1.0 / math.sqrt(size))).T.astype(dq_ref.dtype)

    @pl.when(slot == pl.num_programs(1) - 1)
    def _():
        for b in range(count):
            spot = pl.multiple_of(((b // 2) ^ info[1]) * block, block)
            for j, (total, factor) in enumerate(((dk_all, LN2), (dv_all, 1.0))):

                @pl.when(info[0] == b % 2)
                def _():
                    own_ref[j, pl.ds(spot, block), :] = (total[pl.ds(b * block, block), :] * factor).astype(own_ref.dtype)

                @pl.when(info[0] != b % 2)
                def _():
                    mate_ref[j, pl.ds(spot, block), :] = (total[pl.ds(b * block, block), :] * factor).astype(mate_ref.dtype)


def attention_backward(info, own, mate, ext, grads, ctx, kx, size, first):
    rows, width = ctx.shape
    length = kx.shape[0]
    slots = (info.shape[0] - 2) // 2
    block = rows // slots
    pairs = width // LANES
    heads = LANES // size
    tile = pl.BlockSpec((block, LANES), lambda p, s, i: (s, p))
    return pl.pallas_call(
        functools.partial(backward_kernel, size=size),
        grid_spec=pltpu.PrefetchScalarGridSpec(
            num_scalar_prefetch=1,
            grid=(pairs, slots),
            in_specs=[
                tile,
                tile,
                pl.BlockSpec((block, LANES), lambda p, s, i: (s, first + p)),
                tile,
                pl.BlockSpec((rows, LANES), lambda p, s, i: (0, pairs + p)),
                pl.BlockSpec((rows, LANES), lambda p, s, i: (0, pairs + p)),
                pl.BlockSpec((rows, LANES), lambda p, s, i: (0, 2 * pairs + p)),
                pl.BlockSpec((rows, LANES), lambda p, s, i: (0, 2 * pairs + p)),
                pl.BlockSpec((length, LANES), lambda p, s, i: (0, 0)),
            ],
            out_specs=[
                tile,
                pl.BlockSpec((2, rows, LANES), lambda p, s, i: (0, 0, p)),
                pl.BlockSpec((2, rows, LANES), lambda p, s, i: (0, 0, p)),
            ],
            scratch_shapes=[
                pltpu.VMEM((heads, length, LANES), jnp.bfloat16),
                pltpu.VMEM((LANES, length), jnp.bfloat16),
                pltpu.VMEM((heads, length, LANES), jnp.bfloat16),
                pltpu.VMEM((length, LANES), jnp.float32),
                pltpu.VMEM((length, LANES), jnp.float32),
            ],
        ),
        out_shape=[
            jax.ShapeDtypeStruct((rows, width), jnp.bfloat16),
            jax.ShapeDtypeStruct((2, rows, width), jnp.float32),
            jax.ShapeDtypeStruct((2, rows, width), jnp.bfloat16),
        ],
        compiler_params=pltpu.CompilerParams(dimension_semantics=("arbitrary", "arbitrary")),
        cost_estimate=pl.CostEstimate(
            flops=5 * rows * length * width, bytes_accessed=24 * rows * width, transcendentals=rows * length * pairs
        ),
        name="attention_backward",
    )(info, own, ext, grads, ctx, own, mate, own, mate, kx)


def key_extension(ids):
    place = jnp.arange(LANES) % (LANES // 2)
    hot = ids[:, None] == place[None, :]
    return (hot | ((place >= IDS) & (place < IDS + 3))[None, :]).astype(jnp.bfloat16)


def query_extension(ids):
    place = jnp.arange(LANES) % (LANES // 2)
    other = (place < IDS)[None, :] & (ids[:, None] != place[None, :])
    return jnp.where(other, FAR, 0.0).astype(jnp.bfloat16)


H = 12
HD = 64
LOG2E = 1.0 / LN2
PARTS = 3
eps_norm = 1e-06
bf16 = jnp.bfloat16
f32 = jnp.float32


def norm_forward(total, gain, shift):
    middle = jnp.mean(total, axis=-1, keepdims=True)
    centred = total - middle
    factor = lax.rsqrt(jnp.mean(centred * centred, axis=-1, keepdims=True) + eps_norm)
    normed = centred * factor
    return (normed * gain + shift, normed, factor)


def norm_backward(grad_out, normed, factor, gain):
    scaled = grad_out * gain
    inner = (
        scaled
        - jnp.mean(scaled, axis=-1, keepdims=True)
        - normed * jnp.mean(scaled * normed, axis=-1, keepdims=True)
    )
    return (factor * inner, jnp.sum(grad_out * normed, axis=0), jnp.sum(grad_out, axis=0))


def gelu_parts(hidden):
    normal_cdf = 0.5 * (1.0 + jax.scipy.special.erf(hidden * (1.0 / math.sqrt(2.0))))
    density = jnp.exp(-0.5 * hidden * hidden) * (1.0 / math.sqrt(2.0 * math.pi))
    return (hidden * normal_cdf, normal_cdf + hidden * density)


def dot(a, b):
    return jnp.dot(a, b, preferred_element_type=f32)


def column_sums(values):
    return jnp.sum(values.astype(f32), axis=0)


def xor_pairs(size, bits):
    return [(i, i ^ bits) for i in range(size)]


def straight(values):
    return with_layout_constraint(values, Layout(tuple(range(values.ndim))))


def pick(values, index, axis=0):
    return lax.dynamic_index_in_dim(values, index, axis, keepdims=False)


def after(values, *marks):
    return lax.optimization_barrier((values, marks))[0]


class Places:
    def __init__(self):
        self.columns = lax.axis_size("seq")
        self.shards = lax.axis_size("fsdp")
        self.column = lax.axis_index("seq")
        self.shard = lax.axis_index("fsdp")
        self.core = self.shard & 1
        self.plane = self.shard >> 1

    def mate(self, values):
        return lax.ppermute(values, "fsdp", xor_pairs(self.shards, 1))

    def across(self, values, bits):
        return lax.ppermute(values, "seq", xor_pairs(self.columns, bits))

    def aside(self, values, bits):
        return lax.ppermute(values, "fsdp", xor_pairs(self.shards, 2 * bits))


def to_sequence_parts(here, values):
    groups, piece, width = values.shape
    halves = values.reshape(groups, 2, piece // 2, width)
    kept = straight(pick(halves, here.core, 1))
    other = straight(here.mate(straight(pick(halves, 1 - here.core, 1))))
    parts = []
    for k in range(here.columns):
        want = here.column ^ k
        same = lax.div(want, groups) == here.core
        spot = lax.rem(want, groups)
        parts.append(straight(jnp.where(same, pick(kept, spot), pick(other, spot))))
    return parts


def from_sequence_send(here, slots, first=0):
    return [here.across(part, k) if k else part for k, part in enumerate(slots, first)]


def from_sequence_end(here, slots, groups):
    rows = jnp.stack(slots)

    def of(core):
        return jnp.stack([pick(rows, here.column ^ (core * groups + j)) for j in range(groups)])

    kept = of(here.core)
    other = here.mate(of(1 - here.core))
    first = here.core == 0
    return jnp.concatenate([jnp.where(first, kept, other), jnp.where(first, other, kept)], axis=1)


def place_kernel(info, *refs, moves, outs):
    count = len(moves)
    parts, full, buffers = refs[:count], refs[count : count + outs], refs[count + outs : 2 * count + outs]
    in_sem, out_sem = refs[2 * count + outs :]
    reads = [pltpu.make_async_copy(parts[k], buffers[k], in_sem.at[k]) for k in range(count)]
    for read in reads:
        read.start()
    writes = []
    for k in range(count):
        reads[k].wait()
        for j, (row, rows, cut_row, col, cols, out) in enumerate(moves[k]):
            write = pltpu.make_async_copy(
                buffers[k].at[pl.ds(cut_row, rows), pl.ds(col, cols)],
                full[out].at[info[k], pl.ds(row, rows), :],
                out_sem.at[k, j],
            )
            write.start()
            writes.append(write)
    for write in writes:
        write.wait()


def place(parts, spots, firsts, rows, cuts):
    kind = parts[0].dtype
    shards = sum(part.shape[0] for part in parts) // rows
    moves = [
        [(first, part.shape[0], 0, col, cols, out) for out, (col, cols) in enumerate(cuts)] for first, part in zip(firsts, parts)
    ]
    full = pl.pallas_call(
        functools.partial(place_kernel, moves=moves, outs=len(cuts)),
        grid_spec=pltpu.PrefetchScalarGridSpec(
            num_scalar_prefetch=1,
            grid=(),
            in_specs=[pl.BlockSpec(memory_space=pl.ANY)] * len(parts),
            out_specs=[pl.BlockSpec(memory_space=pl.ANY)] * len(cuts),
            scratch_shapes=[pltpu.VMEM(part.shape, kind) for part in parts]
            + [pltpu.SemaphoreType.DMA((len(parts),)), pltpu.SemaphoreType.DMA((len(parts), len(cuts)))],
        ),
        out_shape=[jax.ShapeDtypeStruct((shards, rows, cols), kind) for _, cols in cuts],
        cost_estimate=pl.CostEstimate(flops=0, bytes_accessed=0, transcendentals=0),
        name="place_parts",
    )(jnp.stack(spots).astype(jnp.int32), *parts)
    return [f.reshape(-1, f.shape[2]) for f in full]


def gather_direct(here, local):
    return [local] + [here.aside(local, k) for k in range(1, 4)]


def with_mates(here, parts):
    spots = [here.shard ^ (2 * k) for k in range(4)]
    return parts + [here.mate(part) for part in parts], spots + [spot ^ 1 for spot in spots]


def gather_cut(here, local, cuts, mark):
    if here.shards != 8:
        full = lax.all_gather(local, "fsdp", axis=0, tiled=True)
        return [full[:, col : col + cols] for col, cols in cuts]
    parts, spots = with_mates(here, after(gather_direct(here, local), mark))
    return place(parts, spots, [0] * 8, local.shape[0], cuts)


def pack_kernel(mix_ref, merge_ref, columns_ref, out_ref, *, size, parts):
    rows, width = merge_ref.shape
    per = LANES // size
    lane_low = lane_of(rows) < size
    pairs = width // LANES // parts
    for pair in range(width // LANES):
        part, spot = pair // pairs, pair % pairs
        for j in range(3):
            one, two = [((3 * (per * pair + k) + j) * size) // LANES * LANES for k in range(2)]
            one, two = mix_ref[:, one : one + LANES].astype(jnp.float32), mix_ref[:, two : two + LANES].astype(jnp.float32)
            if j % 2:
                joined = pltpu.roll(jnp.where(lane_low, two, one), size, 1)
            else:
                joined = jnp.where(lane_low, one, two)
            at = (part * 3 + j) * pairs * LANES + spot * LANES
            out_ref[:, at : at + LANES] = joined.astype(out_ref.dtype)
    out_ref[:, 3 * width : 4 * width] = merge_ref[...]
    out_ref[:, 4 * width :] = columns_ref[...]


def pack(mix, merge, columns, size, parts):
    rows, width = merge.shape
    return pl.pallas_call(
        functools.partial(pack_kernel, size=size, parts=parts),
        out_shape=jax.ShapeDtypeStruct((rows, 4 * width + LANES), mix.dtype),
        name="pack_projection",
    )(mix, merge, columns)


def share_pair(here, partial):
    shards, rows, width = partial.shape
    pairs = partial.reshape(shards // 2, 2, rows, width)
    return pick(pairs, here.core, 1), here.mate(pick(pairs, 1 - here.core, 1).astype(bf16))


def share_plane(here, kept, other):
    def total(k):
        spot = here.plane ^ k
        return pick(kept, spot).astype(f32) + pick(other, spot).astype(f32)

    return total(0), [total(k).astype(bf16) for k in range(1, here.shards // 2)]


def share_send(here, lows, apart=False):
    others = []
    for k, low in enumerate(lows, 1):
        others.append(here.aside(after(low, others[k - 3]) if apart and k > 2 else low, k))
    return others


def share_sum(share, others):
    for other in others:
        share = share + other.astype(f32)
    return share.astype(bf16)


def column_first(here, share):
    low = share.reshape(2, share.shape[0] // 2, share.shape[1])
    side = here.column & 1
    return pick(low, side), here.across(pick(low, 1 - side), 1)


def column_second(here, half, other):
    low = (half.astype(f32) + other.astype(f32)).astype(bf16)
    step, others = 2, []
    while 2 * step < here.columns:
        low = (low.astype(f32) + here.across(low, step).astype(f32)).astype(bf16)
        step *= 2
    return low, here.across(low, step)


def column_third(here, half, other):
    half = (half.astype(f32) + other.astype(f32)).astype(bf16)
    return half, here.across(half, 1)


def column_last(here, half, other):
    first = (here.column & 1) == 0
    return jnp.concatenate([jnp.where(first, half, other), jnp.where(first, other, half)], axis=0)


def per_device(
    tokens,
    segment_ids,
    mix_weight,
    query_bias,
    value_bias,
    merge_weight,
    merge_bias,
    first_gain,
    first_shift,
    up_weight,
    up_bias,
    down_weight,
    down_bias,
    second_gain,
    second_shift,
    output_grad,
):
    here = Places()
    groups, piece, width = tokens.shape
    shards = here.shards
    own = width // shards
    hidden_size = up_weight.shape[1]
    half = piece // 2
    rows = here.columns * half
    length = here.columns * piece

    def send(parts, first=0):
        return [straight(part) for part in from_sequence_send(here, parts, first)]

    ups = hidden_size // width
    part_width = width // PARTS
    ids_sent = [segment_ids] + [here.across(segment_ids, k) for k in range(1, here.columns)]
    ids_slots = jnp.stack([pick(i, lax.rem(here.column, groups)) for i in ids_sent])
    ids_other = here.mate(ids_slots)
    ids_slots = jnp.where(lax.div(here.column, groups) == here.core, ids_slots, ids_other)
    ids_own = pick(ids_slots.reshape(here.columns, 2, half), here.core, 1)
    ids = jnp.stack([pick(ids_slots, here.column ^ k) for k in range(here.columns)]).reshape(2 * here.columns, half)
    first_id, last_id = ids[:, 0], ids[:, -1]
    low = jnp.sum(last_id[None, :] < ids_own[:, :1], axis=1)
    high = jnp.sum(first_id[None, :] <= ids_own[:, -1:], axis=1)
    info = jnp.concatenate([jnp.stack([here.core, here.column]), jnp.stack([low, high], axis=1).reshape(-1)]).astype(jnp.int32)
    key_ext = key_extension(ids.reshape(length))
    query_ext = query_extension(ids_own.reshape(rows))

    token_parts, ids_sent = lax.optimization_barrier((to_sequence_parts(here, tokens), ids_sent))
    token_slots = send(token_parts)

    vectors = (query_bias, value_bias, merge_bias, first_gain, first_shift, down_bias, second_gain, second_shift)
    local_weights = after((vectors, up_bias, mix_weight, merge_weight), ids_sent)
    lines = jnp.concatenate([jnp.stack(local_weights[0]), local_weights[1].reshape(ups, own)], axis=0)
    columns = jnp.pad(lines, ((0, LANES - lines.shape[0]), (0, 0))).T
    mix_local = pack(local_weights[2], local_weights[3], columns, HD, PARTS)
    *mix_parts, merge_full, columns_full = gather_cut(
        here, mix_local, [(p * width, width) for p in range(PARTS + 1)] + [(4 * width, LANES)], token_slots[2:]
    )
    lines_full = columns_full.T.astype(f32)
    query_full, value_full, merge_bias_full, gain_one, shift_one, down_bias_full, gain_two, shift_two = [
        lines_full[j] for j in range(8)
    ]
    up_bias_full = lines_full[8 : 8 + ups].reshape(ups, shards, own).transpose(1, 0, 2).reshape(-1)

    cotangent_parts = to_sequence_parts(here, after(output_grad, token_parts))
    ready = (cotangent_parts, mix_parts, merge_full, lines_full, info, key_ext, query_ext)
    token_slots, (cotangent_parts, mix_parts, merge_full, lines_full, info, key_ext, query_ext) = lax.optimization_barrier(
        (token_slots, ready)
    )
    flat = straight(jnp.concatenate(token_slots, axis=0))
    cotangent_parts = after(cotangent_parts, flat)
    cotangent_two = send(cotangent_parts[2:3], 2)
    direct = shards == 8
    up_local, down_local = after((up_weight, down_weight), mix_parts[0])
    if direct:
        packed = jnp.concatenate([up_local[:, j * width : (j + 1) * width] for j in range(ups)] + [down_local], axis=0)
        packed_parts = gather_direct(here, after(packed, flat))
    else:
        up_full, down_full = [lax.all_gather(w, "fsdp", axis=0, tiled=True) for w in (up_local, down_local)]

    column_scale = jnp.where(jnp.arange(width) < part_width, LOG2E / math.sqrt(HD), 1.0)
    mixed, mixed_mate = [], []
    for p in range(PARTS):
        of_part = slice(p * part_width, (p + 1) * part_width)
        bias = jnp.concatenate([query_full[of_part], jnp.zeros((part_width,), f32), value_full[of_part]])
        mixed.append(((dot(flat, mix_parts[p]) + bias) * column_scale).astype(bf16))
        mixed_mate.append(here.mate(mixed[p]))

    mixed, mixed_mate = lax.optimization_barrier((mixed, mixed_mate))
    contexts, exts = [], []
    plan, spots = NOTHING, ()
    for p in range(PARTS):
        if p:
            mixed[p], mixed_mate[p] = after((mixed[p], mixed_mate[p]), contexts[-1])
        if p == 1:
            mixed[p], cotangent_two = lax.optimization_barrier((mixed[p], cotangent_two))
            later = after(cotangent_parts, contexts[-1])
            cotangent_slots = send(later[:2]) + cotangent_two + send(later[3:], 3)
        if p == PARTS - 1 and direct:
            pieces, spots = with_mates(here, after(packed_parts, contexts[-1]))
            moves = [(j * own, own, 0, j * width) for j in range(ups)] + [(ups * own, ups * own, 1, 0)]
            outs = [(shards,) + up_weight.shape, (shards,) + down_weight.shape]
            plan = (pieces, tuple(moves), tuple(outs))
        context, ext, *placed = attention_forward(info, mixed[p], mixed_mate[p], query_ext, key_ext, HD, plan, spots)
        contexts.append(context)
        exts.append(ext)
    if direct:
        up_full, down_full = [full.reshape(-1, full.shape[2]) for full in placed]
    context = jnp.concatenate(contexts, axis=1)
    cotangent = jnp.concatenate(after(cotangent_slots, contexts[-1]), axis=0).astype(f32)

    attended = dot(context, merge_full) + merge_bias_full
    first_out, normed_one, factor_one = norm_forward(flat.astype(f32) + attended, gain_one, shift_one)
    first_low = first_out.astype(bf16)
    hidden = dot(first_low, up_full) + up_bias_full
    active, slope = gelu_parts(hidden)
    active_low, slope_low = lax.optimization_barrier((active.astype(bf16), slope.astype(bf16)))
    branch = dot(active_low, down_full) + down_bias_full
    result, normed_two, factor_two = norm_forward(first_out + branch, gain_two, shift_two)
    result_low = list(result.astype(bf16).reshape(here.columns, half, width))

    grad_second, second_gain_grad, second_shift_grad = norm_backward(cotangent, normed_two, factor_two, gain_two)
    grad_branch = grad_second.astype(bf16)
    down_grad = dot(active_low.T, grad_branch).astype(bf16)
    down_kept, down_other = share_pair(here, down_grad.reshape(shards, -1, width))
    down_bias_grad = column_sums(grad_branch)
    grad_active = dot(grad_branch, down_full.T)
    grad_hidden = (grad_active * slope_low.astype(f32)).astype(bf16)
    down_share, down_lows = share_plane(here, down_kept, after(down_other, grad_hidden))
    down_others = share_send(here, down_lows)
    up_grad = dot(first_low.T, grad_hidden).astype(bf16)
    up_bias_grad = column_sums(grad_hidden)
    grad_first = grad_second + dot(grad_hidden, up_full.T)
    grad_sum, first_gain_grad, first_shift_grad = norm_backward(grad_first, normed_one, factor_one, gain_one)
    grad_attended = grad_sum.astype(bf16)
    merge_grad = dot(context.T, grad_attended).astype(bf16)
    merge_bias_grad = column_sums(grad_attended)
    up_merge = jnp.concatenate([up_grad.reshape(shards, own, hidden_size), merge_grad.reshape(shards, own, width)], axis=2)
    up_kept, up_other = share_pair(here, up_merge)
    grad_context = dot(grad_attended, merge_full.T).astype(bf16)
    up_share, up_lows = share_plane(here, up_kept, after(up_other, grad_context))
    up_others = share_send(here, up_lows)

    def backward(part, grads):
        dq, kept, other = attention_backward(
            info, mixed[part], mixed_mate[part], exts[part], grads, contexts[part], key_ext, HD, part * part_width // LANES
        )
        return dq, kept, here.mate(other)

    def mixed_part(pieces):
        dq, kept, other = pieces
        kv = (kept + other.astype(f32)).astype(bf16)
        return jnp.concatenate([dq, kv[0], kv[1]], axis=1)

    one = backward(0, after(grad_context, down_share, up_share))
    down_others, down_share = after((down_others, down_share), one[0])
    down_half, down_other = column_first(here, share_sum(down_share, down_others))
    up_others, up_share = after((up_others, up_share), one[0])
    up_half, up_other = column_first(here, share_sum(up_share, up_others))
    output_slots = from_sequence_send(here, after(result_low, one[0]))
    two = backward(1, after(grad_context, down_half, up_half))
    one, up_half, up_other = after((one, up_half, up_other), two[0])
    mixed_one = mixed_part(one)
    down_half, down_other = column_second(here, *after((down_half, down_other), two[0]))
    up_half, up_other = column_second(here, up_half, up_other)
    input_part = grad_sum + dot(mixed_one, mix_parts[0].T)
    three = backward(2, after(grad_context, down_half, up_half, input_part, output_slots[:3]))
    two, down_half, down_other, up_half, up_other, output_slots[3:] = after(
        (two, down_half, down_other, up_half, up_other, output_slots[3:]), three[0]
    )
    mixed_two = mixed_part(two)
    input_part = input_part + dot(mixed_two, mix_parts[1].T)
    mixed_three = mixed_part(after(three, input_part))
    input_low = (input_part + dot(mixed_three, mix_parts[2].T)).astype(bf16)
    input_slots = from_sequence_send(here, list(input_low.reshape(here.columns, half, width)))
    down_half, down_other = column_third(here, down_half, down_other)
    mixed_all, down_half, down_other = after(
        (jnp.concatenate([mixed_one, mixed_two, mixed_three], axis=1), down_half, down_other), input_low
    )
    up_half, up_other = column_third(here, *after((up_half, up_other), down_other))
    mix_grad = dot(flat.T, mixed_all).astype(bf16)

    sums = [column_sums(m) for m in (mixed_one, mixed_two, mixed_three)]
    query_grad = jnp.concatenate([s[:part_width] for s in sums])
    value_grad = jnp.concatenate([s[2 * part_width :] for s in sums])
    vectors = (
        query_grad,
        value_grad,
        merge_bias_grad,
        first_gain_grad,
        first_shift_grad,
        down_bias_grad,
        second_gain_grad,
        second_shift_grad,
    )
    up_lines = up_bias_grad.reshape(shards, ups, own).transpose(1, 0, 2).reshape(ups, width)
    lines_grad = jnp.concatenate([jnp.stack(vectors), up_lines], axis=0)
    columns_grad = jnp.pad(lines_grad, ((0, LANES - lines_grad.shape[0]), (0, 0))).T
    whole = jnp.concatenate([mix_grad, lax.optimization_barrier(columns_grad).astype(bf16)], axis=1).reshape(shards, own, -1)
    mix_share, mix_lows = share_plane(here, *share_pair(here, whole))
    mix_lows, up_half, up_other = lax.optimization_barrier((mix_lows, up_half, up_other))
    mix_others = share_send(here, mix_lows, True)
    input_mark = mix_others[0]
    mix_share = share_sum(mix_share, mix_others)
    mix_half, mix_other = column_first(here, mix_share)
    mix_half, mix_other = column_second(here, mix_half, mix_other)
    down_half, down_other, up_half, up_other = after((down_half, down_other, up_half, up_other), mix_half)
    mix_last = column_last(here, *column_third(here, mix_half, mix_other))

    output = from_sequence_end(here, after(output_slots, mix_half), groups)
    final_input = from_sequence_end(here, after(input_slots, input_mark), groups).astype(f32)
    final_down = column_last(here, down_half, down_other).astype(f32)
    final_up_merge = column_last(here, up_half, up_other).astype(f32)
    final_mix = mix_last[:, : 3 * width].astype(f32).reshape(own, PARTS, 3, H // PARTS, HD)
    final_mix = final_mix.transpose(0, 1, 3, 2, 4).reshape(own, 3 * width)
    final_columns = mix_last[:, 3 * width :].astype(f32)
    finals = final_columns.T
    (
        final_query,
        final_value,
        final_merge_bias,
        final_gain_one,
        final_shift_one,
        final_down_bias,
        final_gain_two,
        final_shift_two,
    ) = [finals[j] for j in range(8)]
    final_up_bias = finals[8 : 8 + ups].reshape(-1)
    return (
        output,
        final_input,
        final_mix,
        final_query,
        final_value,
        final_up_merge[:, hidden_size:],
        final_merge_bias,
        final_gain_one,
        final_shift_one,
        final_up_merge[:, :hidden_size],
        final_up_bias,
        final_down,
        final_down_bias,
        final_gain_two,
        final_shift_two,
    )


def solution(mesh):
    wide, row, thin = P("fsdp", "seq", None), P("fsdp", None), P("fsdp")
    return jax.shard_map(
        per_device,
        mesh=mesh,
        in_specs=(wide, P("fsdp", "seq"), row, thin, thin, row, thin, thin, thin, row, thin, row, thin, thin, thin, wide),
        out_specs=(wide, wide, row, thin, thin, row, thin, thin, thin, row, thin, row, thin, thin, thin),
        check_vma=False,
    )
```
